256 devices in a mesh: gz: 16 (over y, x), dom: 16 (over z, core).
Axes of the slice: x: 4, y: 4, z: 8, core: 2. Of those that a mesh axis runs over, the one named last changes fastest.
Arguments:
- volume: float32 [768, 4, 384], P('gz'), may hold values from -6 to 6
- observed: bfloat16 [4096, 4, 384], P(('gz', 'dom')), may hold values from -6 to 6
- ctf_table: float32 [32, 2, 384], replicated, may hold values from -1 to 1
- ctf_class: int32 [4096], P(('gz', 'dom')), may hold values from 0 to 31
- bin_ids: int32 [4096], P(('gz', 'dom')), may hold values from 0 to 127
Outputs:
- pose_score: float32 [4096], P(('gz', 'dom'))
- backprojection: float32 [768, 4, 384], P(('gz', 'dom'))
The draws below stay inside these ranges and needn't reach their ends.
All inputs are finite; a program needn't handle non-finite values.
Results may differ from the reference program's by a relative error of at most 0.0034.
Values may be sent and summed in bfloat16 or wider, within the bound.
A program may use at most 64 MiB of HBM per device.

```python
import math
import jax
import jax.numpy as jnp
import numpy as np
from jax import lax

NZ = 768
X = 384
U = 384
Y = 2
NB_DEV = 8
NCTF = 32
ITERS = 3
NB = 128
NPART = 4096
N_DOM = 16


def with_ends(result, key, least, high):
    longest = result.shape.index(max(result.shape))
    spots = []
    for shift in (0, 1):
        where = [jax.random.randint(jax.random.fold_in(key, axis), (), 0, length) for axis, length in enumerate(result.shape)]
        where[longest] = (where[longest] + shift) % result.shape[longest]
        spots.append(tuple(where))
    return result.at[spots[0]].set(least).at[spots[1]].set(high)


def level_of(stream_key, extent, cuts, low, high):
    factor_of, own = 1.0, jax.random.fold_in(stream_key, 6)
    for dim, blocks in cuts:
        heights = jnp.exp(jax.random.uniform(jax.random.fold_in(own, dim), (blocks,), jnp.float32, low / len(cuts), high / len(cuts)))
        factor_of = factor_of * jnp.repeat(heights, extent[dim] // blocks).reshape([-1 if axis == dim else 1 for axis in range(len(extent))])
    return factor_of


def rank_bounds(number_of, slope):
    portions = [(1 << 20) // math.isqrt(standing ** slope) + 1 for standing in range(1, number_of + 1)]
    deviation = 1 + sum(portions) // (1 << 30)
    return np.cumsum(np.array([max(1, weight // deviation) for weight in portions]))


def ranked_ids(rng, dims, amount, slope):
    grid = rank_bounds(amount, slope)
    lot = jax.random.randint(jax.random.fold_in(rng, 1), dims, 0, int(grid[amount - 1]))
    grade = jnp.searchsorted(jnp.asarray(grid, jnp.int32), lot, side="right")
    return jax.random.permutation(jax.random.fold_in(rng, 2), amount)[grade].astype(jnp.int32)


def normal_values(key, extent, deviation, limit, split=(), held_as=jnp.bfloat16):
    factor_of = level_of(key, extent, split, -0.22, 0.18) if split else 1.0
    array = jax.random.normal(key, extent, jnp.float32) * deviation * factor_of
    return jnp.minimum(jnp.maximum(array, -limit), limit).astype(held_as)


def setup_inputs(seed: int = 0) -> dict:
    key_of = jax.random.split(jax.random.key(seed), 6)
    volume = normal_values(key_of[0], (NZ, 2 * Y, X), 1.0, 6.0, ((0, 16),), jnp.float32)
    observed = normal_values(key_of[1], (NPART, 2 * Y, U), 1.0, 6.0, ((0, 256),))
    ctf_table = jnp.clip(jax.random.uniform(key_of[2], (NCTF, Y, U), jnp.float32, -1.0, 1.0), -1.0, 1.0)
    ctf_class = with_ends(jax.random.randint(key_of[3], (NPART,), 0, NCTF), jax.random.fold_in(key_of[3], 1), 0, NCTF - 1).astype(jnp.int32)
    bin_ids = with_ends(ranked_ids(key_of[4], (NPART,), NB, 2), jax.random.fold_in(key_of[4], 3), 0, NB - 1).astype(jnp.int32)
    return dict(volume=volume, observed=observed, ctf_table=ctf_table, ctf_class=ctf_class, bin_ids=bin_ids)


def kernel(offset):
    inside = jnp.abs(offset) < 1.0
    falloff = 1.0 - offset * offset
    return (jnp.where(inside, falloff * falloff, 0.0), jnp.where(inside, -4.0 * offset * falloff, 0.0))

def project(field, bin_index):
    total_bins = NB_DEV * N_DOM
    tilt_angle = -0.5 * math.pi + math.pi * (bin_index.astype(jnp.float32) + 0.5) / total_bins
    sine_value = jnp.sin(tilt_angle)
    cosine = jnp.cos(tilt_angle)
    radius = jnp.arange(U).astype(jnp.float32)
    centre = 0.5 * NZ + radius * sine_value
    lower_plane = jnp.clip(jnp.floor(centre).astype(jnp.int32), 0, NZ - 2)
    planes = lower_plane[:, None] + jnp.arange(2, dtype=jnp.int32)[None, :]
    z_value, z_slope = kernel(planes.astype(jnp.float32) - centre[:, None])
    z_slope = z_slope * (-radius * cosine / U)[:, None]
    x_value, x_slope = kernel(jnp.arange(X).astype(jnp.float32)[None, :] - (radius * cosine)[:, None])
    x_slope = x_slope * (radius * sine_value / U)[:, None]
    picked = field[planes]
    x_sums = jnp.einsum('upcx,ux->upc', picked, x_value, precision=lax.Precision.HIGHEST)
    x_slopes = jnp.einsum('upcx,ux->upc', picked, x_slope, precision=lax.Precision.HIGHEST)
    leading = jnp.einsum('upc,up->cu', x_sums, z_value, precision=lax.Precision.HIGHEST)
    second = jnp.einsum('upc,up->cu', x_sums, z_slope, precision=lax.Precision.HIGHEST) + jnp.einsum('upc,up->cu', x_slopes, z_value, precision=lax.Precision.HIGHEST)
    return (leading, second)

def reference(volume, observed, ctf_table, ctf_class, bin_ids):
    total_bins = NB_DEV * N_DOM
    stacked_rows = 2 * Y
    bin_range = jnp.arange(total_bins, dtype=jnp.int32)
    slices = lax.map(lambda bin_index: jnp.concatenate(project(volume, bin_index), 0), bin_range)
    slices = slices.astype(jnp.bfloat16).astype(jnp.float32)
    chosen = slices[bin_ids]
    contrast = ctf_table[ctf_class]
    contrast = jnp.concatenate([contrast, contrast], 1)
    measured = observed.astype(jnp.float32)
    predicted = contrast * chosen[:, :stacked_rows]
    tangent = contrast * chosen[:, stacked_rows:]
    curvature = lax.optimization_barrier(jnp.sum(tangent * tangent, axis=(1, 2))) + 1e-05
    shift = jnp.zeros((measured.shape[0],), jnp.float32)
    for iteration in range(ITERS):
        residual_map = measured - predicted - shift[:, None, None] * tangent
        shift = shift + 0.5 * lax.optimization_barrier(jnp.sum(residual_map * tangent, axis=(1, 2))) / curvature
    pose_score = shift * jnp.sqrt(curvature)
    weighted = contrast * measured
    contributions = jnp.concatenate([weighted, shift[:, None, None] * weighted], 1)
    bin_sums = jax.ops.segment_sum(contributions, bin_ids, num_segments=total_bins)

    def accumulate(running, bin_index):
        summed = bin_sums[bin_index]
        pullback = jax.vjp(lambda field: project(field, bin_index), volume)[1]
        gradient = pullback((summed[:stacked_rows], summed[stacked_rows:]))[0]
        return (running + gradient, None)
    backprojection, unused = lax.scan(accumulate, jnp.zeros(volume.shape, jnp.float32), bin_range)
    return (pose_score, backprojection)
```

```python
import math

import jax
import jax.numpy as jnp
from jax import lax
from jax.experimental import pallas as pl
from jax.experimental.pallas import tpu as pltpu
from jax.sharding import PartitionSpec as P

NZ = 768
NB = 128
NB_DEV = 8
NCTF = 32
ITERS = 3
EPS = 1e-05
G = 16
D = 16
SLAB = 48
R = 4
X = 384
U = 384
PART = 16
ALLP = PART * D
WC = R * U
EXT = 128
NCH = 12
F32 = jnp.float32
BF16 = jnp.bfloat16
NT = (((1,), (1,)), ((), ()))


def iota(shape, dim):
    return lax.broadcasted_iota(jnp.int32, shape, dim)


def gz_copy(src, dst, send, recv, to):
    return pltpu.make_async_remote_copy(
        src_ref=src, dst_ref=dst, send_sem=send, recv_sem=recv,
        device_id={"gz": to}, device_id_type=pl.DeviceIdType.MESH)


def dom_copy(src, dst, send, recv, to):
    return pltpu.make_async_remote_copy(
        src_ref=src, dst_ref=dst, send_sem=send, recv_sem=recv,
        device_id={"dom": to}, device_id_type=pl.DeviceIdType.MESH)


def body(vol, obs, ctf, cls, bins, pose_out, back_out,
         vb, kt, kl, kz, kzd, sc, sp, sp_in, s_all, ss, ss_in, t_all, t32,
         w_all, c2h, c2l, ls, acc, bk, bk_in, pose_s, pose_in,
         w_send, w_recv, f_send, f_recv,
         rs_send, rs_recv, ag_send, ag_recv,
         rs2_send, rs2_recv, ag2_send, ag2_recv,
         b_send, b_recv, p_send, p_recv):
    g = lax.axis_index("gz")
    d = lax.axis_index("dom")
    core = lax.rem(d, 2)
    zpos = lax.div(d, 2)
    sib = d + 1 - 2 * core
    first_bin = d * NB_DEV

    barrier = pltpu.get_barrier_semaphore()
    for i in range(1, G):
        pl.semaphore_signal(barrier, inc=1, device_id={"gz": lax.rem(g + i, G)},
                            device_id_type=pl.DeviceIdType.MESH)
    for i in range(1, D):
        pl.semaphore_signal(barrier, inc=1, device_id={"dom": lax.rem(d + i, D)},
                            device_id_type=pl.DeviceIdType.MESH)

    rows = iota((PART, EXT), 0)
    lanes = iota((PART, EXT), 1)
    cls_col = jnp.zeros((PART, EXT), jnp.int32)
    bin_col = jnp.zeros((PART, EXT), jnp.int32)
    for i in range(PART):
        cls_col = jnp.where(rows == i, cls[i], cls_col)
        bin_col = jnp.where(rows == i, bins[i], bin_col)
    cls_hot = (cls_col == lanes).astype(F32)
    table = jnp.concatenate([ctf[:, 0, :], ctf[:, 1, :]], 1)
    contrast = jnp.dot(cls_hot[:, :NCTF], table, precision=lax.Precision.HIGHEST,
                       preferred_element_type=F32)
    for r in range(R):
        y = r % 2
        image = obs[:, r, :].astype(F32)
        w_all[d, :, r * U:(r + 1) * U] = (image * contrast[:, y * U:(y + 1) * U]).astype(BF16)
    extra = jnp.where(lanes == NCTF, bin_col.astype(F32), cls_hot)
    w_all[d, :, WC:] = extra.astype(BF16)

    pl.semaphore_wait(barrier, (G - 1) + (D - 1))

    for i in range(1, D // 2):
        to = lax.rem(zpos + i, D // 2) * 2 + core
        dom_copy(w_all.at[d], w_all.at[d], w_send.at[i], w_recv.at[d], to).start()
    dom_copy(w_all.at[d], w_all.at[d], f_send.at[0], f_recv.at[d], sib).start()

    square = table * table
    high = square.astype(BF16)
    c2h[...] = jnp.zeros_like(c2h)
    c2l[...] = jnp.zeros_like(c2l)
    c2h[:NCTF, :] = high
    c2l[:NCTF, :] = (square - high.astype(F32)).astype(BF16)

    for r in range(R):
        plane_rows = vol[:, r, :]
        coarse = plane_rows.astype(BF16)
        vb[r * SLAB:(r + 1) * SLAB, :] = coarse
        vb[(R + r) * SLAB:(R + r + 1) * SLAB, :] = (plane_rows - coarse.astype(F32)).astype(BF16)
    bin_index = (first_bin + iota((NB_DEV, 128), 0)).astype(F32)
    theta = -0.5 * math.pi + math.pi * (bin_index + 0.5) / NB
    sc[:NB_DEV, :] = jnp.sin(theta)
    sc[NB_DEV:, :] = jnp.cos(theta)
    radius = iota((1, U), 1).astype(F32)
    plane = (g * SLAB + iota((SLAB, U), 0)).astype(F32)
    column = iota((X, U), 0).astype(F32)

    def extract(b, carry):
        sine = jnp.concatenate([sc[pl.ds(b, 1), :]] * 3, 1)
        cosine = jnp.concatenate([sc[pl.ds(NB_DEV + b, 1), :]] * 3, 1)
        tx = column - radius * cosine
        fx = jnp.maximum(1.0 - tx * tx, 0.0)
        kx = fx * fx
        kxd = (tx * fx) * (radius * sine * (-4.0 / U))
        kx_high = kx.astype(BF16)
        kxd_high = kxd.astype(BF16)
        kt[b, :, :U] = kx_high
        kt[b, :, U:] = kxd_high
        kl[:, :U] = (kx - kx_high.astype(F32)).astype(BF16)
        kl[:, U:] = (kxd - kxd_high.astype(F32)).astype(BF16)
        tz = plane - (0.5 * NZ + radius * sine)
        fz = jnp.maximum(1.0 - tz * tz, 0.0)
        wz = fz * fz
        wd = (tz * fz) * (radius * cosine * (4.0 / U))
        kz[b] = wz
        kzd[b] = wd
        stacked = jnp.dot(vb[...], kt[b], preferred_element_type=F32)
        both = stacked[:R * SLAB] + stacked[R * SLAB:] + jnp.dot(
            vb[:R * SLAB, :], kl[...], preferred_element_type=F32)
        for r in range(R):
            direct = both[r * SLAB:(r + 1) * SLAB, :U]
            tilted = both[r * SLAB:(r + 1) * SLAB, U:]
            lead = jnp.sum(direct * wz, axis=0, keepdims=True)
            second = jnp.sum(direct * wd + tilted * wz, axis=0, keepdims=True)
            for j in range(3):
                at = pl.ds((r % 2) * 8 + b, 1)
                sp[3 * (r // 2) + j, at, :] = lead[:, 128 * j:128 * (j + 1)]
                sp[3 * (2 + r // 2) + j, at, :] = second[:, 128 * j:128 * (j + 1)]
        return carry

    lax.fori_loop(0, NB_DEV, extract, 0)

    offset = 4 * core
    mine = lax.rem(g - offset + G, G)
    reduces = mine < NCH

    def sum_start(src, src_in, send, recv):
        for i in range(1, G):
            to = lax.rem(g + i, G)
            q = lax.rem(to - offset + G, G)

            @pl.when(q < NCH)
            def _():
                gz_copy(src.at[q], src_in.at[g], send.at[i], recv.at[g], to).start()

    def sum_reduce(src, src_in, out, recv, send2, recv2):
        @pl.when(reduces)
        def _():
            src_in[g] = src[mine]
            for i in range(1, G):
                frm = lax.rem(g + i, G)
                gz_copy(src.at[0], src_in.at[frm], recv.at[frm], recv.at[frm], frm).wait_recv()
            total = src_in[0]
            for i in range(1, G):
                total = total + src_in[i]
            out[mine] = total.astype(out.dtype)
            for i in range(1, G):
                to = lax.rem(g + i, G)
                gz_copy(out.at[mine], out.at[mine], send2.at[i], recv2.at[mine], to).start()

    def sum_wait(out, recv2):
        for q in range(NCH):
            @pl.when(mine != q)
            def _():
                gz_copy(out.at[q], out.at[q], recv2.at[q], recv2.at[q], lax.rem(g + 1, G)).wait_recv()

    def sum_finish(src, src_in, out, send, recv, send2):
        for i in range(1, G):
            to = lax.rem(g + i, G)
            q = lax.rem(to - offset + G, G)

            @pl.when(q < NCH)
            def _():
                gz_copy(src.at[q], src_in.at[g], send.at[i], recv.at[g], to).wait_send()

            @pl.when(reduces)
            def _():
                gz_copy(out.at[0], out.at[0], send2.at[i], send2.at[i], to).wait_send()

    sum_start(sp, sp_in, rs_send, rs_recv)
    sum_reduce(sp, sp_in, s_all, rs_recv, ag_send, ag_recv)

    for i in range(1, D // 2):
        frm = lax.rem(zpos + i, D // 2) * 2 + core
        dom_copy(w_all.at[frm], w_all.at[frm], w_recv.at[frm], w_recv.at[frm], sib).wait_recv()
        dom_copy(w_all.at[frm], w_all.at[frm], f_send.at[i], f_recv.at[frm], sib).start()

    sum_wait(s_all, ag_recv)

    def rows_of(kind, r):
        k = 2 * kind + r // 2
        half = (r % 2) * 8
        return jnp.concatenate(
            [s_all[3 * k + j].astype(F32)[half:half + 8, :] for j in range(3)], 1)

    lead = [rows_of(0, r) for r in range(R)]
    slope = [rows_of(1, r) for r in range(R)]
    curve = jnp.concatenate([slope[y] * slope[y] + slope[y + 2] * slope[y + 2] for y in range(2)], 1)
    cross = jnp.concatenate([lead[y] * slope[y] + lead[y + 2] * slope[y + 2] for y in range(2)], 1)
    quad = jnp.concatenate([curve, cross], 0)
    quad_high = quad.astype(BF16)
    quad_low = (quad - quad_high.astype(F32)).astype(BF16)
    first = lax.dot_general(jnp.concatenate([quad_high, quad_low], 0), c2h[...], NT,
                            preferred_element_type=F32)
    tables = first[:16] + first[16:] + lax.dot_general(quad_high, c2l[...], NT,
                                                       preferred_element_type=F32)
    tables_high = tables.astype(BF16)
    tables_low = (tables - tables_high.astype(F32)).astype(BF16)
    pick = (iota((8, EXT), 1) == NCTF).astype(F32).astype(BF16)
    zero = jnp.zeros((8, EXT), BF16)
    lookup = jnp.concatenate([tables_high, tables_low, pick, zero], 0)
    slope_rows = jnp.concatenate(slope, 1).astype(BF16)

    for i in range(0, D // 2):
        frm = lax.rem(zpos + i, D // 2) * 2 + 1 - core
        dom_copy(w_all.at[frm], w_all.at[frm], f_recv.at[frm], f_recv.at[frm], sib).wait_recv()

    images = w_all[:, :, :WC].reshape(ALLP, WC)
    marks = w_all[:, :, WC:].reshape(ALLP, EXT)
    looked = lax.dot_general(lookup, marks, NT, preferred_element_type=F32)
    along = lax.dot_general(slope_rows, images, NT, preferred_element_type=F32)
    held = looked[0:8] + looked[16:24]
    crossed = looked[8:16] + looked[24:32]
    own = (first_bin + iota((8, ALLP), 0)).astype(F32) == looked[32:40]
    mask = own.astype(F32)
    power = jnp.sum(mask * held, axis=0, keepdims=True)
    match = jnp.sum(mask * (along - crossed), axis=0, keepdims=True)
    curvature = power + EPS
    shift = jnp.zeros_like(power)
    for _ in range(ITERS):
        shift = shift + 0.5 * (match - shift * power) / curvature
    pose_s[...] = shift * jnp.sqrt(curvature)
    moved = mask * shift
    moved_high = moved.astype(BF16)
    moved_low = (moved - moved_high.astype(F32)).astype(BF16)
    spread = jnp.concatenate([mask.astype(BF16), moved_high, moved_low, jnp.zeros((8, ALLP), BF16)], 0)
    sums = jnp.dot(spread, images, preferred_element_type=F32)
    for q in range(NCH):
        part = sums[:, 128 * q:128 * (q + 1)]
        ss[q] = jnp.concatenate([part[:8], part[8:16] + part[16:24]], 0)

    sum_start(ss, ss_in, rs2_send, rs2_recv)
    for i in range(1, D):
        to = lax.rem(d + i, D)
        dom_copy(pose_s, pose_in.at[d], p_send.at[i], p_recv.at[d], to).start()
    sum_reduce(ss, ss_in, t_all, rs2_recv, ag2_send, ag2_recv)
    sum_wait(t_all, ag2_recv)

    for q in range(NCH):
        t32[:, 128 * q:128 * (q + 1)] = t_all[q]
    acc[...] = jnp.zeros_like(acc)

    def spread_back(b, carry):
        wz = kz[b]
        wd = kzd[b]
        for r in range(R):
            plain = t32[pl.ds(b, 1), r * U:(r + 1) * U]
            sloped = t32[pl.ds(8 + b, 1), r * U:(r + 1) * U]
            ls[r * SLAB:(r + 1) * SLAB, :U] = (wz * plain + wd * sloped).astype(BF16)
            ls[r * SLAB:(r + 1) * SLAB, U:] = (wz * sloped).astype(BF16)
        acc[...] += lax.dot_general(ls[...], kt[b], NT, preferred_element_type=F32)
        return carry

    lax.fori_loop(0, NB_DEV, spread_back, 0)

    row = iota((256, R * SLAB), 0)
    within = lax.rem(row, 16)
    source = lax.rem(row, 4) * SLAB + 3 * lax.div(row, 16) + lax.div(within, 4)
    order = ((iota((256, R * SLAB), 1) == source) & (within < 12)).astype(F32).astype(BF16)
    ordered = jnp.dot(order, acc[...].astype(BF16), preferred_element_type=F32)
    bk[...] = ordered.astype(BF16).reshape(D, 16, X)
    for i in range(1, D):
        to = lax.rem(d + i, D)
        dom_copy(bk.at[to], bk_in.at[d], b_send.at[i], b_recv.at[d], to).start()

    pose_in[d] = pose_s[...]
    for i in range(1, D):
        frm = lax.rem(d + i, D)
        dom_copy(pose_s, pose_in.at[frm], p_recv.at[frm], p_recv.at[frm], frm).wait_recv()
    pose = pose_in[0]
    for i in range(1, D):
        pose = pose + pose_in[i]
    lane = iota((8, ALLP), 1)
    kept = jnp.where(lax.div(lane, PART) == d, pose, 0.0)
    choose = (lax.rem(iota((ALLP, 128), 0), PART) == iota((ALLP, 128), 1)).astype(F32)
    picked = jnp.dot(kept, choose, precision=lax.Precision.HIGHEST, preferred_element_type=F32)
    pose_out[...] = picked[0:1, :PART]

    bk_in[d] = bk[d]
    for i in range(1, D):
        frm = lax.rem(d + i, D)
        dom_copy(bk.at[0], bk_in.at[frm], b_recv.at[frm], b_recv.at[frm], frm).wait_recv()
    total = bk_in[0].astype(F32)
    for i in range(1, D):
        total = total + bk_in[i].astype(F32)
    for k in range(3):
        back_out[k] = total[4 * k:4 * k + 4]

    sum_finish(sp, sp_in, s_all, rs_send, rs_recv, ag_send)
    sum_finish(ss, ss_in, t_all, rs2_send, rs2_recv, ag2_send)
    for i in range(1, D // 2):
        dom_copy(w_all.at[d], w_all.at[d], w_send.at[i], w_send.at[i], sib).wait_send()
    for i in range(0, D // 2):
        dom_copy(w_all.at[d], w_all.at[d], f_send.at[i], f_send.at[i], sib).wait_send()
    for i in range(1, D):
        dom_copy(bk.at[0], bk_in.at[d], b_send.at[i], b_send.at[i], sib).wait_send()
        dom_copy(pose_s, pose_in.at[d], p_send.at[i], p_send.at[i], sib).wait_send()


def local(volume, observed, ctf_table, ctf_class, bin_ids):
    vmem = pl.BlockSpec(memory_space=pltpu.VMEM)
    smem = pl.BlockSpec(memory_space=pltpu.SMEM)
    dma = pltpu.SemaphoreType.DMA
    pose, back = pl.pallas_call(
        body,
        out_shape=(jax.ShapeDtypeStruct((1, PART), F32), jax.ShapeDtypeStruct((3, R, X), F32)),
        in_specs=[vmem, vmem, vmem, smem, smem],
        out_specs=(vmem, vmem),
        scratch_shapes=[
            pltpu.VMEM((2 * R * SLAB, X), BF16),
            pltpu.VMEM((NB_DEV, X, 2 * U), BF16),
            pltpu.VMEM((X, 2 * U), BF16),
            pltpu.VMEM((NB_DEV, SLAB, U), F32),
            pltpu.VMEM((NB_DEV, SLAB, U), F32),
            pltpu.VMEM((2 * NB_DEV, 128), F32),
            pltpu.VMEM((NCH, 16, 128), F32),
            pltpu.VMEM((G, 16, 128), F32),
            pltpu.VMEM((NCH, 16, 128), BF16),
            pltpu.VMEM((NCH, 16, 128), F32),
            pltpu.VMEM((G, 16, 128), F32),
            pltpu.VMEM((NCH, 16, 128), F32),
            pltpu.VMEM((16, WC), F32),
            pltpu.VMEM((D, PART, WC + EXT), BF16),
            pltpu.VMEM((EXT, 2 * U), BF16),
            pltpu.VMEM((EXT, 2 * U), BF16),
            pltpu.VMEM((R * SLAB, 2 * U), BF16),
            pltpu.VMEM((R * SLAB, X), F32),
            pltpu.VMEM((D, 16, X), BF16),
            pltpu.VMEM((D, 16, X), BF16),
            pltpu.VMEM((1, ALLP), F32),
            pltpu.VMEM((D, 1, ALLP), F32),
        ] + [dma((16,))] * 16,
        compiler_params=pltpu.CompilerParams(
            collective_id=0, has_side_effects=True, vmem_limit_bytes=32 << 20),
        name="tilt_refine",
    )(volume, observed, ctf_table, ctf_class, bin_ids)
    return (pose.reshape(PART), back)


def solution(mesh):
    return jax.shard_map(
        local,
        mesh=mesh,
        in_specs=(
            P("gz", None, None),
            P(("gz", "dom"), None, None),
            P(),
            P(("gz", "dom")),
            P(("gz", "dom")),
        ),
        out_specs=(P(("gz", "dom")), P(("gz", "dom"), None, None)),
        check_vma=False,
    )
```

```python
import math

import jax
import jax.numpy as jnp
from jax import lax
from jax.experimental import pallas as pl
from jax.experimental.pallas import tpu as pltpu
from jax.sharding import PartitionSpec as P

NZ = 768
NB = 128
NB_DEV = 8
NCTF = 32
ITERS = 3
EPS = 1e-05
G = 16
D = 16
SLAB = 48
R = 4
X = 384
U = 384
PART = 16
ALLP = PART * D
WC = R * U
EXT = 128
NCH = 12
F32 = jnp.float32
BF16 = jnp.bfloat16
NT = (((1,), (1,)), ((), ()))


def iota(shape, dim):
    return lax.broadcasted_iota(jnp.int32, shape, dim)


def gz_copy(src, dst, send, recv, to):
    return pltpu.make_async_remote_copy(
        src_ref=src, dst_ref=dst, send_sem=send, recv_sem=recv,
        device_id={"gz": to}, device_id_type=pl.DeviceIdType.MESH)


def dom_copy(src, dst, send, recv, to):
    return pltpu.make_async_remote_copy(
        src_ref=src, dst_ref=dst, send_sem=send, recv_sem=recv,
        device_id={"dom": to}, device_id_type=pl.DeviceIdType.MESH)


def body(vol_hbm, obs_hbm, ctf_hbm, cls_hbm, bins_hbm, pose_out, back_out,
         vol, obs, ctf, cls, bins, in_sem, vb, kt, kl, kz, kzd, sc, sp, sp_in, s_all, ss, ss_in, t_all, t32,
         w_all, c2h, c2l, ls, acc, bk, bk_in, pose_s, pose_in,
         w_send, w_recv, f_send, f_recv,
         rs_send, rs_recv, ag_send, ag_recv,
         rs2_send, rs2_recv, ag2_send, ag2_recv,
         b_send, b_recv, p_send, p_recv):
    g = lax.axis_index("gz")
    d = lax.axis_index("dom")
    core = lax.rem(d, 2)
    zpos = lax.div(d, 2)
    sib = d + 1 - 2 * core
    first_bin = d * NB_DEV

    barrier = pltpu.get_barrier_semaphore()
    for i in range(1, G):
        pl.semaphore_signal(barrier, inc=1, device_id={"gz": lax.rem(g + i, G)},
                            device_id_type=pl.DeviceIdType.MESH)
    for i in range(1, D):
        pl.semaphore_signal(barrier, inc=1, device_id={"dom": lax.rem(d + i, D)},
                            device_id_type=pl.DeviceIdType.MESH)

    fetches = [pltpu.make_async_copy(src, dst, in_sem.at[k]) for k, (src, dst) in enumerate(
        ((bins_hbm, bins), (cls_hbm, cls), (obs_hbm, obs), (ctf_hbm, ctf), (vol_hbm, vol)))]
    for fetch in fetches:
        fetch.start()
    for fetch in fetches[:4]:
        fetch.wait()

    rows = iota((PART, EXT), 0)
    lanes = iota((PART, EXT), 1)
    cls_col = jnp.zeros((PART, EXT), jnp.int32)
    bin_col = jnp.zeros((PART, EXT), jnp.int32)
    for i in range(PART):
        cls_col = jnp.where(rows == i, cls[i], cls_col)
        bin_col = jnp.where(rows == i, bins[i], bin_col)
    cls_hot = (cls_col == lanes).astype(F32)
    table = jnp.concatenate([ctf[:, 0, :], ctf[:, 1, :]], 1)
    contrast = jnp.dot(cls_hot[:, :NCTF], table, precision=lax.Precision.HIGHEST,
                       preferred_element_type=F32)
    for r in range(R):
        y = r % 2
        image = obs[:, r, :].astype(F32)
        w_all[d, :, r * U:(r + 1) * U] = (image * contrast[:, y * U:(y + 1) * U]).astype(BF16)
    extra = jnp.where(lanes == NCTF, bin_col.astype(F32), cls_hot)
    w_all[d, :, WC:] = extra.astype(BF16)

    square = table * table
    high = square.astype(BF16)
    c2h[...] = jnp.zeros_like(c2h)
    c2l[...] = jnp.zeros_like(c2l)
    c2h[:NCTF, :] = high
    c2l[:NCTF, :] = (square - high.astype(F32)).astype(BF16)

    fetches[4].wait()
    for r in range(R):
        plane_rows = vol[:, r, :]
        coarse = plane_rows.astype(BF16)
        vb[r * SLAB:(r + 1) * SLAB, :] = coarse
        vb[(R + r) * SLAB:(R + r + 1) * SLAB, :] = (plane_rows - coarse.astype(F32)).astype(BF16)
    bin_index = (first_bin + iota((NB_DEV, 128), 0)).astype(F32)
    theta = -0.5 * math.pi + math.pi * (bin_index + 0.5) / NB
    sc[:NB_DEV, :] = jnp.sin(theta)
    sc[NB_DEV:, :] = jnp.cos(theta)
    radius = iota((1, U), 1).astype(F32)
    plane = (g * SLAB + iota((SLAB, U), 0)).astype(F32)
    column = iota((X, U), 0).astype(F32)

    def extract(b, carry):
        sine = jnp.concatenate([sc[pl.ds(b, 1), :]] * 3, 1)
        cosine = jnp.concatenate([sc[pl.ds(NB_DEV + b, 1), :]] * 3, 1)
        tx = column - radius * cosine
        fx = jnp.maximum(1.0 - tx * tx, 0.0)
        kx = fx * fx
        kxd = (tx * fx) * (radius * sine * (-4.0 / U))
        kx_high = kx.astype(BF16)
        kxd_high = kxd.astype(BF16)
        kt[b, :, :U] = kx_high
        kt[b, :, U:] = kxd_high
        kl[:, :U] = (kx - kx_high.astype(F32)).astype(BF16)
        kl[:, U:] = (kxd - kxd_high.astype(F32)).astype(BF16)
        tz = plane - (0.5 * NZ + radius * sine)
        fz = jnp.maximum(1.0 - tz * tz, 0.0)
        wz = fz * fz
        wd = (tz * fz) * (radius * cosine * (4.0 / U))
        kz[b] = wz
        kzd[b] = wd
        stacked = jnp.dot(vb[...], kt[b], preferred_element_type=F32)
        both = stacked[:R * SLAB] + stacked[R * SLAB:] + jnp.dot(
            vb[:R * SLAB, :], kl[...], preferred_element_type=F32)
        for r in range(R):
            direct = both[r * SLAB:(r + 1) * SLAB, :U]
            tilted = both[r * SLAB:(r + 1) * SLAB, U:]
            lead = jnp.sum(direct * wz, axis=0, keepdims=True)
            second = jnp.sum(direct * wd + tilted * wz, axis=0, keepdims=True)
            for j in range(3):
                at = pl.ds((r % 2) * 8 + b, 1)
                sp[3 * (r // 2) + j, at, :] = lead[:, 128 * j:128 * (j + 1)]
                sp[3 * (2 + r // 2) + j, at, :] = second[:, 128 * j:128 * (j + 1)]
        return carry

    lax.fori_loop(0, NB_DEV, extract, 0)

    pl.semaphore_wait(barrier, (G - 1) + (D - 1))

    for i in range(1, D // 2):
        to = lax.rem(zpos + i, D // 2) * 2 + core
        dom_copy(w_all.at[d], w_all.at[d], w_send.at[i], w_recv.at[d], to).start()
    dom_copy(w_all.at[d], w_all.at[d], f_send.at[0], f_recv.at[d], sib).start()

    offset = 4 * core
    mine = lax.rem(g - offset + G, G)
    reduces = mine < NCH

    def sum_start(src, src_in, send, recv):
        for i in range(1, G):
            to = lax.rem(g + i, G)
            q = lax.rem(to - offset + G, G)

            @pl.when(q < NCH)
            def _():
                gz_copy(src.at[q], src_in.at[g], send.at[i], recv.at[g], to).start()

    def sum_reduce(src, src_in, out, recv, send2, recv2):
        @pl.when(reduces)
        def _():
            src_in[g] = src[mine]
            for i in range(1, G):
                frm = lax.rem(g + i, G)
                gz_copy(src.at[0], src_in.at[frm], recv.at[frm], recv.at[frm], frm).wait_recv()
            total = src_in[0]
            for i in range(1, G):
                total = total + src_in[i]
            out[mine] = total.astype(out.dtype)
            for i in range(1, G):
                to = lax.rem(g + i, G)
                gz_copy(out.at[mine], out.at[mine], send2.at[i], recv2.at[mine], to).start()

    def sum_wait(out, recv2):
        for q in range(NCH):
            @pl.when(mine != q)
            def _():
                gz_copy(out.at[q], out.at[q], recv2.at[q], recv2.at[q], lax.rem(g + 1, G)).wait_recv()

    def sum_finish(src, src_in, out, send, recv, send2):
        for i in range(1, G):
            to = lax.rem(g + i, G)
            q = lax.rem(to - offset + G, G)

            @pl.when(q < NCH)
            def _():
                gz_copy(src.at[q], src_in.at[g], send.at[i], recv.at[g], to).wait_send()

            @pl.when(reduces)
            def _():
                gz_copy(out.at[0], out.at[0], send2.at[i], send2.at[i], to).wait_send()

    sum_start(sp, sp_in, rs_send, rs_recv)
    sum_reduce(sp, sp_in, s_all, rs_recv, ag_send, ag_recv)

    for i in range(1, D // 2):
        frm = lax.rem(zpos + i, D // 2) * 2 + core
        dom_copy(w_all.at[frm], w_all.at[frm], w_recv.at[frm], w_recv.at[frm], sib).wait_recv()
        dom_copy(w_all.at[frm], w_all.at[frm], f_send.at[i], f_recv.at[frm], sib).start()

    sum_wait(s_all, ag_recv)

    def rows_of(kind, r):
        k = 2 * kind + r // 2
        half = (r % 2) * 8
        return jnp.concatenate(
            [s_all[3 * k + j].astype(F32)[half:half + 8, :] for j in range(3)], 1)

    lead = [rows_of(0, r) for r in range(R)]
    slope = [rows_of(1, r) for r in range(R)]
    curve = jnp.concatenate([slope[y] * slope[y] + slope[y + 2] * slope[y + 2] for y in range(2)], 1)
    cross = jnp.concatenate([lead[y] * slope[y] + lead[y + 2] * slope[y + 2] for y in range(2)], 1)
    quad = jnp.concatenate([curve, cross], 0)
    quad_high = quad.astype(BF16)
    quad_low = (quad - quad_high.astype(F32)).astype(BF16)
    first = lax.dot_general(jnp.concatenate([quad_high, quad_low], 0), c2h[...], NT,
                            preferred_element_type=F32)
    tables = first[:16] + first[16:] + lax.dot_general(quad_high, c2l[...], NT,
                                                       preferred_element_type=F32)
    tables_high = tables.astype(BF16)
    tables_low = (tables - tables_high.astype(F32)).astype(BF16)
    pick = (iota((8, EXT), 1) == NCTF).astype(F32).astype(BF16)
    zero = jnp.zeros((8, EXT), BF16)
    lookup = jnp.concatenate([tables_high, tables_low, pick, zero], 0)
    slope_rows = jnp.concatenate(slope, 1).astype(BF16)

    for i in range(0, D // 2):
        frm = lax.rem(zpos + i, D // 2) * 2 + 1 - core
        dom_copy(w_all.at[frm], w_all.at[frm], f_recv.at[frm], f_recv.at[frm], sib).wait_recv()

    images = w_all[:, :, :WC].reshape(ALLP, WC)
    marks = w_all[:, :, WC:].reshape(ALLP, EXT)
    looked = lax.dot_general(lookup, marks, NT, preferred_element_type=F32)
    along = lax.dot_general(slope_rows, images, NT, preferred_element_type=F32)
    held = looked[0:8] + looked[16:24]
    crossed = looked[8:16] + looked[24:32]
    own = (first_bin + iota((8, ALLP), 0)).astype(F32) == looked[32:40]
    mask = own.astype(F32)
    power = jnp.sum(mask * held, axis=0, keepdims=True)
    match = jnp.sum(mask * (along - crossed), axis=0, keepdims=True)
    curvature = power + EPS
    shift = jnp.zeros_like(power)
    for _ in range(ITERS):
        shift = shift + 0.5 * (match - shift * power) / curvature
    pose_s[...] = shift * jnp.sqrt(curvature)
    moved = mask * shift
    moved_high = moved.astype(BF16)
    moved_low = (moved - moved_high.astype(F32)).astype(BF16)
    spread = jnp.concatenate([mask.astype(BF16), moved_high, moved_low, jnp.zeros((8, ALLP), BF16)], 0)
    sums = jnp.dot(spread, images, preferred_element_type=F32)
    for q in range(NCH):
        part = sums[:, 128 * q:128 * (q + 1)]
        ss[q] = jnp.concatenate([part[:8], part[8:16] + part[16:24]], 0)

    sum_start(ss, ss_in, rs2_send, rs2_recv)
    for i in range(1, D):
        to = lax.rem(d + i, D)
        dom_copy(pose_s, pose_in.at[d], p_send.at[i], p_recv.at[d], to).start()
    sum_reduce(ss, ss_in, t_all, rs2_recv, ag2_send, ag2_recv)
    sum_wait(t_all, ag2_recv)

    for q in range(NCH):
        t32[:, 128 * q:128 * (q + 1)] = t_all[q]
    acc[...] = jnp.zeros_like(acc)

    def spread_back(b, carry):
        wz = kz[b]
        wd = kzd[b]
        for r in range(R):
            plain = t32[pl.ds(b, 1), r * U:(r + 1) * U]
            sloped = t32[pl.ds(8 + b, 1), r * U:(r + 1) * U]
            ls[r * SLAB:(r + 1) * SLAB, :U] = (wz * plain + wd * sloped).astype(BF16)
            ls[r * SLAB:(r + 1) * SLAB, U:] = (wz * sloped).astype(BF16)
        acc[...] += lax.dot_general(ls[...], kt[b], NT, preferred_element_type=F32)
        return carry

    lax.fori_loop(0, NB_DEV, spread_back, 0)

    row = iota((256, R * SLAB), 0)
    within = lax.rem(row, 16)
    source = lax.rem(row, 4) * SLAB + 3 * lax.div(row, 16) + lax.div(within, 4)
    order = ((iota((256, R * SLAB), 1) == source) & (within < 12)).astype(F32).astype(BF16)
    ordered = jnp.dot(order, acc[...].astype(BF16), preferred_element_type=F32)
    bk[...] = ordered.astype(BF16).reshape(D, 16, X)
    for i in range(1, D):
        to = lax.rem(d + i, D)
        dom_copy(bk.at[to], bk_in.at[d], b_send.at[i], b_recv.at[d], to).start()

    pose_in[d] = pose_s[...]
    for i in range(1, D):
        frm = lax.rem(d + i, D)
        dom_copy(pose_s, pose_in.at[frm], p_recv.at[frm], p_recv.at[frm], frm).wait_recv()
    pose = pose_in[0]
    for i in range(1, D):
        pose = pose + pose_in[i]
    lane = iota((8, ALLP), 1)
    kept = jnp.where(lax.div(lane, PART) == d, pose, 0.0)
    choose = (lax.rem(iota((ALLP, 128), 0), PART) == iota((ALLP, 128), 1)).astype(F32)
    picked = jnp.dot(kept, choose, precision=lax.Precision.HIGHEST, preferred_element_type=F32)
    pose_out[...] = picked[0:1, :PART]

    bk_in[d] = bk[d]
    for i in range(1, D):
        frm = lax.rem(d + i, D)
        dom_copy(bk.at[0], bk_in.at[frm], b_recv.at[frm], b_recv.at[frm], frm).wait_recv()
    total = bk_in[0].astype(F32)
    for i in range(1, D):
        total = total + bk_in[i].astype(F32)
    for k in range(3):
        back_out[k] = total[4 * k:4 * k + 4]

    sum_finish(sp, sp_in, s_all, rs_send, rs_recv, ag_send)
    sum_finish(ss, ss_in, t_all, rs2_send, rs2_recv, ag2_send)
    for i in range(1, D // 2):
        dom_copy(w_all.at[d], w_all.at[d], w_send.at[i], w_send.at[i], sib).wait_send()
    for i in range(0, D // 2):
        dom_copy(w_all.at[d], w_all.at[d], f_send.at[i], f_send.at[i], sib).wait_send()
    for i in range(1, D):
        dom_copy(bk.at[0], bk_in.at[d], b_send.at[i], b_send.at[i], sib).wait_send()
        dom_copy(pose_s, pose_in.at[d], p_send.at[i], p_send.at[i], sib).wait_send()


def local(volume, observed, ctf_table, ctf_class, bin_ids):
    vmem = pl.BlockSpec(memory_space=pltpu.VMEM)
    hbm = pl.BlockSpec(memory_space=pltpu.HBM)
    dma = pltpu.SemaphoreType.DMA
    pose, back = pl.pallas_call(
        body,
        out_shape=(jax.ShapeDtypeStruct((1, PART), F32), jax.ShapeDtypeStruct((3, R, X), F32)),
        in_specs=[hbm] * 5,
        out_specs=(vmem, vmem),
        scratch_shapes=[
            pltpu.VMEM((SLAB, R, X), F32),
            pltpu.VMEM((PART, R, U), BF16),
            pltpu.VMEM((NCTF, 2, U), F32),
            pltpu.SMEM((PART,), jnp.int32),
            pltpu.SMEM((PART,), jnp.int32),
            dma((5,)),
            pltpu.VMEM((2 * R * SLAB, X), BF16),
            pltpu.VMEM((NB_DEV, X, 2 * U), BF16),
            pltpu.VMEM((X, 2 * U), BF16),
            pltpu.VMEM((NB_DEV, SLAB, U), F32),
            pltpu.VMEM((NB_DEV, SLAB, U), F32),
            pltpu.VMEM((2 * NB_DEV, 128), F32),
            pltpu.VMEM((NCH, 16, 128), F32),
            pltpu.VMEM((G, 16, 128), F32),
            pltpu.VMEM((NCH, 16, 128), BF16),
            pltpu.VMEM((NCH, 16, 128), F32),
            pltpu.VMEM((G, 16, 128), F32),
            pltpu.VMEM((NCH, 16, 128), F32),
            pltpu.VMEM((16, WC), F32),
            pltpu.VMEM((D, PART, WC + EXT), BF16),
            pltpu.VMEM((EXT, 2 * U), BF16),
            pltpu.VMEM((EXT, 2 * U), BF16),
            pltpu.VMEM((R * SLAB, 2 * U), BF16),
            pltpu.VMEM((R * SLAB, X), F32),
            pltpu.VMEM((D, 16, X), BF16),
            pltpu.VMEM((D, 16, X), BF16),
            pltpu.VMEM((1, ALLP), F32),
            pltpu.VMEM((D, 1, ALLP), F32),
        ] + [dma((16,))] * 16,
        compiler_params=pltpu.CompilerParams(
            collective_id=0, has_side_effects=True, vmem_limit_bytes=60 << 20),
        name="tilt_refine",
    )(volume, observed, ctf_table, ctf_class, bin_ids)
    return (pose.reshape(PART), back)


def solution(mesh):
    return jax.shard_map(
        local,
        mesh=mesh,
        in_specs=(
            P("gz", None, None),
            P(("gz", "dom"), None, None),
            P(),
            P(("gz", "dom")),
            P(("gz", "dom")),
        ),
        out_specs=(P(("gz", "dom")), P(("gz", "dom"), None, None)),
        check_vma=False,
    )
```

```python
import math

import jax
import jax.numpy as jnp
from jax import lax
from jax.experimental import pallas as pl
from jax.experimental.pallas import tpu as pltpu
from jax.sharding import PartitionSpec as P

NZ = 768
NB = 128
NB_DEV = 8
NCTF = 32
ITERS = 3
EPS = 1e-05
G = 16
D = 16
SLAB = 48
R = 4
X = 384
U = 384
PART = 16
ALLP = PART * D
WC = R * U
EXT = 128
BLOCKS = 3
BL = 128
F32 = jnp.float32
BF16 = jnp.bfloat16
NT = (((1,), (1,)), ((), ()))


def slab_spans():
    spans = []
    for j in range(BLOCKS):
        row = []
        for k in range(D):
            sines = [math.sin(-0.5 * math.pi + math.pi * (b + 0.5) / NB)
                     for b in range(k * NB_DEV, (k + 1) * NB_DEV)]
            centres = [0.5 * NZ + u * sine for sine in sines for u in (j * BL, j * BL + BL - 1)]
            first = math.floor(min(centres) - 1e-3)
            last = math.floor(max(centres) + 1e-3) + 1
            row.append((max(first, 0) // SLAB, min(last, NZ - 1) // SLAB))
        spans.append(row)
    return spans


def iota(shape, dim):
    return lax.broadcasted_iota(jnp.int32, shape, dim)


def gz_copy(src, dst, send, recv, to):
    return pltpu.make_async_remote_copy(
        src_ref=src, dst_ref=dst, send_sem=send, recv_sem=recv,
        device_id={"gz": to}, device_id_type=pl.DeviceIdType.MESH)


def dom_copy(src, dst, send, recv, to):
    return pltpu.make_async_remote_copy(
        src_ref=src, dst_ref=dst, send_sem=send, recv_sem=recv,
        device_id={"dom": to}, device_id_type=pl.DeviceIdType.MESH)


def body(vol_hbm, obs_hbm, ctf_hbm, cls_hbm, bins_hbm, pose_out, back_out,
         vol, obs, ctf, cls, bins, in_sem, vb, kt, kz, kzd, sc, sp, spb, sp_in, s_all, ss, ss_in, t32,
         w_all, c2h, c2l, acc, bk, bk_in, pose_s, pose_in,
         w_send, w_recv, f_send, f_recv,
         rs_send, rs_recv, rs2_send, rs2_recv, b_send, b_recv, p_send, p_recv):
    g = lax.axis_index("gz")
    d = lax.axis_index("dom")
    core = lax.rem(d, 2)
    zpos = lax.div(d, 2)
    sib = d + 1 - 2 * core
    first_bin = d * NB_DEV

    barrier = pltpu.get_barrier_semaphore()
    for i in range(1, D):
        pl.semaphore_signal(barrier, inc=1, device_id={"dom": lax.rem(d + i, D)},
                            device_id_type=pl.DeviceIdType.MESH)
    for i in range(1, G):
        pl.semaphore_signal(barrier, inc=1, device_id={"gz": lax.rem(g + i, G)},
                            device_id_type=pl.DeviceIdType.MESH)

    low, high_slab = [], []
    for row in slab_spans():
        least, most = jnp.int32(row[0][0]), jnp.int32(row[0][1])
        for k in range(1, D):
            least = jnp.where(d == k, row[k][0], least)
            most = jnp.where(d == k, row[k][1], most)
        low.append(least)
        high_slab.append(most)

    def active(j, slab):
        return (low[j] <= slab) & (slab <= high_slab[j])

    fetches = [pltpu.make_async_copy(src, dst, in_sem.at[k]) for k, (src, dst) in enumerate(
        ((bins_hbm, bins), (cls_hbm, cls), (obs_hbm, obs), (ctf_hbm, ctf), (vol_hbm, vol)))]
    for fetch in fetches:
        fetch.start()
    for fetch in fetches[:4]:
        fetch.wait()

    rows = iota((PART, EXT), 0)
    lanes = iota((PART, EXT), 1)
    cls_col = jnp.zeros((PART, EXT), jnp.int32)
    bin_col = jnp.zeros((PART, EXT), jnp.int32)
    for i in range(PART):
        cls_col = jnp.where(rows == i, cls[i], cls_col)
        bin_col = jnp.where(rows == i, bins[i], bin_col)
    cls_hot = (cls_col == lanes).astype(F32)
    table = jnp.concatenate([ctf[:, 0, :], ctf[:, 1, :]], 1)
    contrast = jnp.dot(cls_hot[:, :NCTF], table, precision=lax.Precision.HIGHEST,
                       preferred_element_type=F32)
    for r in range(R):
        y = r % 2
        image = obs[:, r, :].astype(F32)
        w_all[d, :, r * U:(r + 1) * U] = (image * contrast[:, y * U:(y + 1) * U]).astype(BF16)
    extra = jnp.where(lanes == NCTF, bin_col.astype(F32), cls_hot)
    w_all[d, :, WC:] = extra.astype(BF16)

    square = table * table
    high = square.astype(BF16)
    c2h[...] = jnp.zeros_like(c2h)
    c2l[...] = jnp.zeros_like(c2l)
    c2h[:NCTF, :] = high
    c2l[:NCTF, :] = (square - high.astype(F32)).astype(BF16)

    fetches[4].wait()
    for r in range(R):
        plane_rows = vol[:, r, :]
        coarse = plane_rows.astype(BF16)
        vb[r * SLAB:(r + 1) * SLAB, :] = coarse
        vb[(R + r) * SLAB:(R + r + 1) * SLAB, :] = (plane_rows - coarse.astype(F32)).astype(BF16)
    bin_index = (first_bin + iota((NB_DEV, 128), 0)).astype(F32)
    theta = -0.5 * math.pi + math.pi * (bin_index + 0.5) / NB
    sc[:NB_DEV, :] = jnp.sin(theta)
    sc[NB_DEV:, :] = jnp.cos(theta)

    for j in range(BLOCKS):
        wide = BL * (j + 1)
        radius = (BL * j + iota((1, BL), 1)).astype(F32)
        plane = (g * SLAB + iota((SLAB, BL), 0)).astype(F32)
        column = iota((wide, BL), 0).astype(F32)

        def extract(b, carry, j=j, wide=wide, radius=radius, plane=plane, column=column):
            sine = sc[pl.ds(b, 1), :]
            cosine = sc[pl.ds(NB_DEV + b, 1), :]
            tx = column - radius * cosine
            fx = jnp.maximum(1.0 - tx * tx, 0.0)
            kx = jnp.concatenate([fx * fx, (tx * fx) * (radius * sine * (-4.0 / U))], 1)
            kx_high = kx.astype(BF16)
            kt[b, :wide, 2 * BL * j:2 * BL * (j + 1)] = kx_high
            kx_low = (kx - kx_high.astype(F32)).astype(BF16)
            tz = plane - (0.5 * NZ + radius * sine)
            fz = jnp.maximum(1.0 - tz * tz, 0.0)
            wz = fz * fz
            wd = (tz * fz) * (radius * cosine * (4.0 / U))
            kz[b, :, BL * j:BL * (j + 1)] = wz
            kzd[b, :, BL * j:BL * (j + 1)] = wd
            stacked = jnp.dot(vb[:, :wide], kx_high, preferred_element_type=F32)
            both = stacked[:R * SLAB] + stacked[R * SLAB:] + jnp.dot(
                vb[:R * SLAB, :wide], kx_low, preferred_element_type=F32)
            for r in range(R):
                direct = both[r * SLAB:(r + 1) * SLAB, :BL]
                tilted = both[r * SLAB:(r + 1) * SLAB, BL:]
                sp[j, pl.ds(r * 8 + b, 1), :] = jnp.sum(direct * wz, axis=0, keepdims=True)
                sp[j, pl.ds(32 + r * 8 + b, 1), :] = jnp.sum(
                    direct * wd + tilted * wz, axis=0, keepdims=True)
            return carry

        @pl.when(active(j, g))
        def _(j=j, extract=extract):
            lax.fori_loop(0, NB_DEV, extract, 0)
            spb[j] = sp[j].astype(BF16)

    pl.semaphore_wait(barrier, (G - 1) + (D - 1))

    for i in range(1, D // 2):
        to = lax.rem(zpos + i, D // 2) * 2 + core
        dom_copy(w_all.at[d], w_all.at[d], w_send.at[i], w_recv.at[d], to).start()
    dom_copy(w_all.at[d], w_all.at[d], f_send.at[0], f_recv.at[d], sib).start()

    for j in range(BLOCKS):
        @pl.when(active(j, g))
        def _(j=j):
            for i in range(1, G):
                gz_copy(spb.at[j], sp_in.at[j, g], rs_send.at[j, i], rs_recv.at[j, g], lax.rem(g + i, G)).start()
            sp_in[j, g] = spb[j]

    for i in range(1, D // 2):
        frm = lax.rem(zpos + i, D // 2) * 2 + core
        dom_copy(w_all.at[frm], w_all.at[frm], w_recv.at[frm], w_recv.at[frm], sib).wait_recv()
        dom_copy(w_all.at[frm], w_all.at[frm], f_send.at[i], f_recv.at[frm], sib).start()

    for j in range(BLOCKS):
        def gather(frm, total, j=j):
            @pl.when(frm != g)
            def _():
                gz_copy(spb.at[j], sp_in.at[j, frm], rs_recv.at[j, frm], rs_recv.at[j, frm],
                        lax.rem(g + 1, G)).wait_recv()
            return total + sp_in[j, frm].astype(F32)

        s_all[j] = lax.fori_loop(low[j], high_slab[j] + 1, gather, jnp.zeros((64, BL), F32))

    def rows_of(kind, r):
        at = 32 * kind + 8 * r
        rounded = jnp.concatenate([s_all[j, at:at + 8, :] for j in range(BLOCKS)], 1)
        return rounded.astype(BF16).astype(F32)

    lead = [rows_of(0, r) for r in range(R)]
    slope = [rows_of(1, r) for r in range(R)]
    curve = jnp.concatenate([slope[y] * slope[y] + slope[y + 2] * slope[y + 2] for y in range(2)], 1)
    cross = jnp.concatenate([lead[y] * slope[y] + lead[y + 2] * slope[y + 2] for y in range(2)], 1)
    quad = jnp.concatenate([curve, cross], 0)
    quad_high = quad.astype(BF16)
    quad_low = (quad - quad_high.astype(F32)).astype(BF16)
    first = lax.dot_general(jnp.concatenate([quad_high, quad_low], 0), c2h[...], NT,
                            preferred_element_type=F32)
    tables = first[:16] + first[16:] + lax.dot_general(quad_high, c2l[...], NT,
                                                       preferred_element_type=F32)
    tables_high = tables.astype(BF16)
    tables_low = (tables - tables_high.astype(F32)).astype(BF16)
    pick = (iota((8, EXT), 1) == NCTF).astype(F32).astype(BF16)
    zero = jnp.zeros((8, EXT), BF16)
    lookup = jnp.concatenate([tables_high, tables_low, pick, zero], 0)
    slope_rows = jnp.concatenate(slope, 1).astype(BF16)

    for i in range(0, D // 2):
        frm = lax.rem(zpos + i, D // 2) * 2 + 1 - core
        dom_copy(w_all.at[frm], w_all.at[frm], f_recv.at[frm], f_recv.at[frm], sib).wait_recv()

    images = w_all[:, :, :WC].reshape(ALLP, WC)
    marks = w_all[:, :, WC:].reshape(ALLP, EXT)
    looked = lax.dot_general(lookup, marks, NT, preferred_element_type=F32)
    along = lax.dot_general(slope_rows, images, NT, preferred_element_type=F32)
    held = looked[0:8] + looked[16:24]
    crossed = looked[8:16] + looked[24:32]
    own = (first_bin + iota((8, ALLP), 0)).astype(F32) == looked[32:40]
    mask = own.astype(F32)
    power = jnp.sum(mask * held, axis=0, keepdims=True)
    match = jnp.sum(mask * (along - crossed), axis=0, keepdims=True)
    curvature = power + EPS
    shift = jnp.zeros_like(power)
    for _ in range(ITERS):
        shift = shift + 0.5 * (match - shift * power) / curvature
    pose_s[...] = shift * jnp.sqrt(curvature)
    moved = mask * shift
    moved_high = moved.astype(BF16)
    moved_low = (moved - moved_high.astype(F32)).astype(BF16)
    spread = jnp.concatenate([mask.astype(BF16), moved_high, moved_low, jnp.zeros((8, ALLP), BF16)], 0)
    sums = jnp.dot(spread, images, preferred_element_type=F32)
    for r in range(R):
        part = sums[:, r * U:(r + 1) * U]
        part = jnp.concatenate([part[:8], part[8:16] + part[16:24]], 0).astype(BF16)
        for j in range(BLOCKS):
            ss[j, 16 * r:16 * (r + 1), :] = part[:, BL * j:BL * (j + 1)]

    for i in range(1, G):
        to = lax.rem(g + i, G)
        for j in range(BLOCKS):
            @pl.when(active(j, to))
            def _(i=i, j=j, to=to):
                gz_copy(ss.at[j], ss_in.at[j, g], rs2_send.at[j, i], rs2_recv.at[j, g], to).start()
    for i in range(1, D):
        to = lax.rem(d + i, D)
        dom_copy(pose_s, pose_in.at[d], p_send.at[i], p_recv.at[d], to).start()

    acc[...] = jnp.zeros_like(acc)
    row = iota((256, R * SLAB), 0)
    within = lax.rem(row, 16)
    source = lax.rem(row, 4) * SLAB + 3 * lax.div(row, 16) + lax.div(within, 4)
    order = ((iota((256, R * SLAB), 1) == source) & (within < 12)).astype(F32).astype(BF16)

    for j in reversed(range(BLOCKS)):
        wide = BL * (j + 1)

        def spread_back(b, carry, j=j, wide=wide):
            wz = kz[b, :, BL * j:BL * (j + 1)]
            wd = kzd[b, :, BL * j:BL * (j + 1)]
            parts = []
            for r in range(R):
                plain = t32[j, pl.ds(16 * r + b, 1), :]
                sloped = t32[j, pl.ds(16 * r + 8 + b, 1), :]
                parts.append(jnp.concatenate([wz * plain + wd * sloped, wz * sloped], 1))
            left = jnp.concatenate(parts, 0)
            left_high = left.astype(BF16)
            left_low = (left - left_high.astype(F32)).astype(BF16)
            both = lax.dot_general(
                jnp.concatenate([left_high, left_low], 0),
                kt[b, :wide, 2 * BL * j:2 * BL * (j + 1)], NT, preferred_element_type=F32)
            acc[:, :wide] += both[:R * SLAB] + both[R * SLAB:]
            return carry

        @pl.when(active(j, g))
        def _(j=j, spread_back=spread_back):
            ss_in[j, g] = ss[j]
            for i in range(1, G):
                frm = lax.rem(g + i, G)
                gz_copy(ss.at[j], ss_in.at[j, frm], rs2_recv.at[j, frm], rs2_recv.at[j, frm], frm).wait_recv()
            total = ss_in[j, 0].astype(F32)
            for i in range(1, G):
                total = total + ss_in[j, i].astype(F32)
            t32[j] = total
            lax.fori_loop(0, NB_DEV, spread_back, 0)

        ordered = jnp.dot(order, acc[:, BL * j:BL * (j + 1)].astype(BF16), preferred_element_type=F32)
        bk[j] = ordered.astype(BF16).reshape(D, 16, BL)
        for i in range(1, D):
            to = lax.rem(d + i, D)
            dom_copy(bk.at[j, to], bk_in.at[j, d], b_send.at[j, i], b_recv.at[j, d], to).start()

    pose_in[d] = pose_s[...]
    for i in range(1, D):
        frm = lax.rem(d + i, D)
        dom_copy(pose_s, pose_in.at[frm], p_recv.at[frm], p_recv.at[frm], frm).wait_recv()
    pose = pose_in[0]
    for i in range(1, D):
        pose = pose + pose_in[i]
    lane = iota((8, ALLP), 1)
    kept = jnp.where(lax.div(lane, PART) == d, pose, 0.0)
    choose = (lax.rem(iota((ALLP, 128), 0), PART) == iota((ALLP, 128), 1)).astype(F32)
    picked = jnp.dot(kept, choose, precision=lax.Precision.HIGHEST, preferred_element_type=F32)
    pose_out[...] = picked[0:1, :PART]

    for j in reversed(range(BLOCKS)):
        bk_in[j, d] = bk[j, d]
        for i in range(1, D):
            frm = lax.rem(d + i, D)
            dom_copy(bk.at[j, 0], bk_in.at[j, frm], b_recv.at[j, frm], b_recv.at[j, frm], frm).wait_recv()
        total = bk_in[j, 0].astype(F32)
        for i in range(1, D):
            total = total + bk_in[j, i].astype(F32)
        for k in range(3):
            back_out[k, :, BL * j:BL * (j + 1)] = total[4 * k:4 * k + 4]

    for i in range(1, G):
        to = lax.rem(g + i, G)
        for j in range(BLOCKS):
            @pl.when(active(j, g))
            def _(i=i, j=j, to=to):
                gz_copy(spb.at[j], sp_in.at[j, g], rs_send.at[j, i], rs_send.at[j, i], to).wait_send()

            @pl.when(active(j, to))
            def _(i=i, j=j, to=to):
                gz_copy(ss.at[j], ss_in.at[j, g], rs2_send.at[j, i], rs2_send.at[j, i], to).wait_send()
    for i in range(1, D // 2):
        dom_copy(w_all.at[d], w_all.at[d], w_send.at[i], w_send.at[i], sib).wait_send()
    for i in range(0, D // 2):
        dom_copy(w_all.at[d], w_all.at[d], f_send.at[i], f_send.at[i], sib).wait_send()
    for i in range(1, D):
        for j in range(BLOCKS):
            dom_copy(bk.at[j, 0], bk_in.at[j, d], b_send.at[j, i], b_send.at[j, i], sib).wait_send()
        dom_copy(pose_s, pose_in.at[d], p_send.at[i], p_send.at[i], sib).wait_send()


def local(volume, observed, ctf_table, ctf_class, bin_ids):
    vmem = pl.BlockSpec(memory_space=pltpu.VMEM)
    hbm = pl.BlockSpec(memory_space=pltpu.HBM)
    dma = pltpu.SemaphoreType.DMA
    pose, back = pl.pallas_call(
        body,
        out_shape=(jax.ShapeDtypeStruct((1, PART), F32), jax.ShapeDtypeStruct((3, R, X), F32)),
        in_specs=[hbm] * 5,
        out_specs=(vmem, vmem),
        scratch_shapes=[
            pltpu.VMEM((SLAB, R, X), F32),
            pltpu.VMEM((PART, R, U), BF16),
            pltpu.VMEM((NCTF, 2, U), F32),
            pltpu.SMEM((PART,), jnp.int32),
            pltpu.SMEM((PART,), jnp.int32),
            dma((5,)),
            pltpu.VMEM((2 * R * SLAB, X), BF16),
            pltpu.VMEM((NB_DEV, X, 2 * U), BF16),
            pltpu.VMEM((NB_DEV, SLAB, U), F32),
            pltpu.VMEM((NB_DEV, SLAB, U), F32),
            pltpu.VMEM((2 * NB_DEV, 128), F32),
            pltpu.VMEM((BLOCKS, 64, BL), F32),
            pltpu.VMEM((BLOCKS, 64, BL), BF16),
            pltpu.VMEM((BLOCKS, G, 64, BL), BF16),
            pltpu.VMEM((BLOCKS, 64, BL), F32),
            pltpu.VMEM((BLOCKS, 64, BL), BF16),
            pltpu.VMEM((BLOCKS, G, 64, BL), BF16),
            pltpu.VMEM((BLOCKS, 64, BL), F32),
            pltpu.VMEM((D, PART, WC + EXT), BF16),
            pltpu.VMEM((EXT, 2 * U), BF16),
            pltpu.VMEM((EXT, 2 * U), BF16),
            pltpu.VMEM((R * SLAB, X), F32),
            pltpu.VMEM((BLOCKS, D, 16, BL), BF16),
            pltpu.VMEM((BLOCKS, D, 16, BL), BF16),
            pltpu.VMEM((1, ALLP), F32),
            pltpu.VMEM((D, 1, ALLP), F32),
        ] + [dma((16,))] * 4 + [dma((BLOCKS, 16))] * 6 + [dma((16,))] * 2,
        compiler_params=pltpu.CompilerParams(
            collective_id=0, has_side_effects=True, vmem_limit_bytes=60 << 20),
        name="tilt_refine",
    )(volume, observed, ctf_table, ctf_class, bin_ids)
    return (pose.reshape(PART), back)


def solution(mesh):
    return jax.shard_map(
        local,
        mesh=mesh,
        in_specs=(
            P("gz", None, None),
            P(("gz", "dom"), None, None),
            P(),
            P(("gz", "dom")),
            P(("gz", "dom")),
        ),
        out_specs=(P(("gz", "dom")), P(("gz", "dom"), None, None)),
        check_vma=False,
    )
```

```python
import math

import jax
import jax.numpy as jnp
from jax import lax
from jax.experimental import pallas as pl
from jax.experimental.pallas import tpu as pltpu
from jax.sharding import PartitionSpec as P

NZ = 768
NB = 128
NB_DEV = 8
NCTF = 32
ITERS = 3
EPS = 1e-05
G = 16
D = 16
SLAB = 48
R = 4
X = 384
U = 384
PART = 16
ALLP = PART * D
WC = R * U
EXT = 128
BLOCKS = 3
BL = 128
PAIRS = 4
UNITS = [(k, j) for j in range(BLOCKS) for k in range(PAIRS)]
F32 = jnp.float32
BF16 = jnp.bfloat16
NT = (((1,), (1,)), ((), ()))


def slab_spans():
    spans = []
    for k, j in UNITS:
        row = []
        for dom in range(D):
            sines = [math.sin(-0.5 * math.pi + math.pi * (2 * (dom + D * k) + i + 0.5) / NB)
                     for i in range(2)]
            centres = [0.5 * NZ + u * sine for sine in sines for u in (j * BL, j * BL + BL - 1)]
            first = math.floor(min(centres) - 1e-3)
            last = math.floor(max(centres) + 1e-3) + 1
            row.append((max(first, 0) // SLAB, min(last, NZ - 1) // SLAB))
        spans.append(row)
    return spans


def iota(shape, dim):
    return lax.broadcasted_iota(jnp.int32, shape, dim)


def gz_copy(src, dst, send, recv, to):
    return pltpu.make_async_remote_copy(
        src_ref=src, dst_ref=dst, send_sem=send, recv_sem=recv,
        device_id={"gz": to}, device_id_type=pl.DeviceIdType.MESH)


def dom_copy(src, dst, send, recv, to):
    return pltpu.make_async_remote_copy(
        src_ref=src, dst_ref=dst, send_sem=send, recv_sem=recv,
        device_id={"dom": to}, device_id_type=pl.DeviceIdType.MESH)


def body(vol_hbm, obs_hbm, ctf_hbm, cls_hbm, bins_hbm, pose_out, back_out,
         vol, obs, ctf, cls, bins, in_sem, vb, kt, kz, kzd, sc, sp, spb, sp_in, s_all, sf, ss, ss_in,
         w_all, c2h, c2l, acc, bk, bk_in, pose_s, pose_in,
         w_send, w_recv, f_send, f_recv,
         rs_send, rs_recv, rs2_send, rs2_recv, b_send, b_recv, p_send, p_recv):
    g = lax.axis_index("gz")
    d = lax.axis_index("dom")
    core = lax.rem(d, 2)
    zpos = lax.div(d, 2)
    sib = d + 1 - 2 * core

    def bin_of(slot):
        return 2 * d + 2 * D * lax.div(slot, 2) + lax.rem(slot, 2)


    barrier = pltpu.get_barrier_semaphore()
    for i in range(1, D):
        pl.semaphore_signal(barrier, inc=1, device_id={"dom": lax.rem(d + i, D)},
                            device_id_type=pl.DeviceIdType.MESH)
    for i in range(1, G):
        pl.semaphore_signal(barrier, inc=1, device_id={"gz": lax.rem(g + i, G)},
                            device_id_type=pl.DeviceIdType.MESH)

    low, top = [], []
    for row in slab_spans():
        least, most = jnp.int32(row[0][0]), jnp.int32(row[0][1])
        for k in range(1, D):
            least = jnp.where(d == k, row[k][0], least)
            most = jnp.where(d == k, row[k][1], most)
        low.append(least)
        top.append(most)

    def active(n, slab):
        return (low[n] <= slab) & (slab <= top[n])

    fetches = [pltpu.make_async_copy(src, dst, in_sem.at[k]) for k, (src, dst) in enumerate(
        ((bins_hbm, bins), (cls_hbm, cls), (obs_hbm, obs), (ctf_hbm, ctf), (vol_hbm, vol)))]
    for fetch in fetches:
        fetch.start()
    for fetch in fetches[:4]:
        fetch.wait()

    rows = iota((PART, EXT), 0)
    lanes = iota((PART, EXT), 1)
    cls_col = jnp.zeros((PART, EXT), jnp.int32)
    bin_col = jnp.zeros((PART, EXT), jnp.int32)
    for i in range(PART):
        cls_col = jnp.where(rows == i, cls[i], cls_col)
        bin_col = jnp.where(rows == i, bins[i], bin_col)
    cls_hot = (cls_col == lanes).astype(F32)
    table = jnp.concatenate([ctf[:, 0, :], ctf[:, 1, :]], 1)
    contrast = jnp.dot(cls_hot[:, :NCTF], table, precision=lax.Precision.HIGHEST,
                       preferred_element_type=F32)
    for r in range(R):
        y = r % 2
        image = obs[:, r, :].astype(F32)
        w_all[d, :, r * U:(r + 1) * U] = (image * contrast[:, y * U:(y + 1) * U]).astype(BF16)
    extra = jnp.where(lanes == NCTF, bin_col.astype(F32), cls_hot)
    w_all[d, :, WC:] = extra.astype(BF16)

    square = table * table
    high = square.astype(BF16)
    c2h[...] = jnp.zeros_like(c2h)
    c2l[...] = jnp.zeros_like(c2l)
    c2h[:NCTF, :] = high
    c2l[:NCTF, :] = (square - high.astype(F32)).astype(BF16)

    fetches[4].wait()
    for r in range(R):
        plane_rows = vol[:, r, :]
        coarse = plane_rows.astype(BF16)
        vb[r * SLAB:(r + 1) * SLAB, :] = coarse
        vb[(R + r) * SLAB:(R + r + 1) * SLAB, :] = (plane_rows - coarse.astype(F32)).astype(BF16)
    bin_index = bin_of(iota((NB_DEV, 128), 0)).astype(F32)
    theta = -0.5 * math.pi + math.pi * (bin_index + 0.5) / NB
    sc[:NB_DEV, :] = jnp.sin(theta)
    sc[NB_DEV:, :] = jnp.cos(theta)

    for j in range(BLOCKS):
        wide = BL * (j + 1)
        radius = (BL * j + iota((1, BL), 1)).astype(F32)
        plane = (g * SLAB + iota((SLAB, BL), 0)).astype(F32)
        column = iota((wide, BL), 0).astype(F32)

        def extract(n, k, j=j, wide=wide, radius=radius, plane=plane, column=column):
            for i in range(2):
                b = 2 * k + i
                sine = sc[b:b + 1, :]
                cosine = sc[NB_DEV + b:NB_DEV + b + 1, :]
                tx = column - radius * cosine
                fx = jnp.maximum(1.0 - tx * tx, 0.0)
                kx = jnp.concatenate([fx * fx, (tx * fx) * (radius * sine * (-4.0 / U))], 1)
                kx_high = kx.astype(BF16)
                kt[b, :wide, 2 * BL * j:2 * BL * (j + 1)] = kx_high
                kx_low = (kx - kx_high.astype(F32)).astype(BF16)
                tz = plane - (0.5 * NZ + radius * sine)
                fz = jnp.maximum(1.0 - tz * tz, 0.0)
                wz = fz * fz
                wd = (tz * fz) * (radius * cosine * (4.0 / U))
                kz[b, :, BL * j:BL * (j + 1)] = wz
                kzd[b, :, BL * j:BL * (j + 1)] = wd
                stacked = jnp.dot(vb[:, :wide], kx_high, preferred_element_type=F32)
                both = stacked[:R * SLAB] + stacked[R * SLAB:] + jnp.dot(
                    vb[:R * SLAB, :wide], kx_low, preferred_element_type=F32)
                for r in range(R):
                    direct = both[r * SLAB:(r + 1) * SLAB, :BL]
                    tilted = both[r * SLAB:(r + 1) * SLAB, BL:]
                    at = 2 * r + i
                    sp[n, at:at + 1, :] = jnp.sum(direct * wz, axis=0, keepdims=True)
                    sp[n, 8 + at:8 + at + 1, :] = jnp.sum(
                        direct * wd + tilted * wz, axis=0, keepdims=True)
            spb[n] = sp[n].astype(BF16)

        for k in range(PAIRS):
            n = UNITS.index((k, j))

            @pl.when(active(n, g))
            def _(n=n, k=k, extract=extract):
                extract(n, k)

    pl.semaphore_wait(barrier, (G - 1) + (D - 1))

    for i in range(1, D // 2):
        to = lax.rem(zpos + i, D // 2) * 2 + core
        dom_copy(w_all.at[d], w_all.at[d], w_send.at[i], w_recv.at[d], to).start()
    dom_copy(w_all.at[d], w_all.at[d], f_send.at[0], f_recv.at[d], sib).start()

    for n in range(len(UNITS)):
        @pl.when(active(n, g))
        def _(n=n):
            for i in range(1, G):
                gz_copy(spb.at[n], sp_in.at[n, g], rs_send.at[n, i], rs_recv.at[n, g], lax.rem(g + i, G)).start()
            sp_in[n, g] = spb[n]

    for i in range(1, D // 2):
        frm = lax.rem(zpos + i, D // 2) * 2 + core
        dom_copy(w_all.at[frm], w_all.at[frm], w_recv.at[frm], w_recv.at[frm], sib).wait_recv()
        dom_copy(w_all.at[frm], w_all.at[frm], f_send.at[i], f_recv.at[frm], sib).start()

    for n, (k, j) in enumerate(UNITS):
        def gather(frm, total, n=n):
            @pl.when(frm != g)
            def _():
                gz_copy(spb.at[n], sp_in.at[n, frm], rs_recv.at[n, frm], rs_recv.at[n, frm],
                        lax.rem(g + 1, G)).wait_recv()
            return total + sp_in[n, frm].astype(F32)

        total = lax.fori_loop(low[n], top[n] + 1, gather, jnp.zeros((16, BL), F32))
        for m in range(8):
            s_all[j, 8 * m + 2 * k:8 * m + 2 * k + 2, :] = total[2 * m:2 * m + 2]

    def rows_of(kind, r):
        at = 32 * kind + 8 * r
        rounded = jnp.concatenate([s_all[j, at:at + 8, :] for j in range(BLOCKS)], 1)
        return rounded.astype(BF16).astype(F32)

    lead = [rows_of(0, r) for r in range(R)]
    slope = [rows_of(1, r) for r in range(R)]
    curve = jnp.concatenate([slope[y] * slope[y] + slope[y + 2] * slope[y + 2] for y in range(2)], 1)
    cross = jnp.concatenate([lead[y] * slope[y] + lead[y + 2] * slope[y + 2] for y in range(2)], 1)
    quad = jnp.concatenate([curve, cross], 0)
    quad_high = quad.astype(BF16)
    quad_low = (quad - quad_high.astype(F32)).astype(BF16)
    first = lax.dot_general(jnp.concatenate([quad_high, quad_low], 0), c2h[...], NT,
                            preferred_element_type=F32)
    tables = first[:16] + first[16:] + lax.dot_general(quad_high, c2l[...], NT,
                                                       preferred_element_type=F32)
    tables_high = tables.astype(BF16)
    tables_low = (tables - tables_high.astype(F32)).astype(BF16)
    pick = (iota((8, EXT), 1) == NCTF).astype(F32).astype(BF16)
    zero = jnp.zeros((8, EXT), BF16)
    lookup = jnp.concatenate([tables_high, tables_low, pick, zero], 0)
    slope_rows = jnp.concatenate(slope, 1).astype(BF16)

    for i in range(0, D // 2):
        frm = lax.rem(zpos + i, D // 2) * 2 + 1 - core
        dom_copy(w_all.at[frm], w_all.at[frm], f_recv.at[frm], f_recv.at[frm], sib).wait_recv()

    images = w_all[:, :, :WC].reshape(ALLP, WC)
    marks = w_all[:, :, WC:].reshape(ALLP, EXT)
    looked = lax.dot_general(lookup, marks, NT, preferred_element_type=F32)
    along = lax.dot_general(slope_rows, images, NT, preferred_element_type=F32)
    held = looked[0:8] + looked[16:24]
    crossed = looked[8:16] + looked[24:32]
    own = bin_of(iota((8, ALLP), 0)).astype(F32) == looked[32:40]
    mask = own.astype(F32)
    power = jnp.sum(mask * held, axis=0, keepdims=True)
    match = jnp.sum(mask * (along - crossed), axis=0, keepdims=True)
    curvature = power + EPS
    shift = jnp.zeros_like(power)
    for _ in range(ITERS):
        shift = shift + 0.5 * (match - shift * power) / curvature
    pose_s[...] = shift * jnp.sqrt(curvature)
    moved = mask * shift
    moved_high = moved.astype(BF16)
    moved_low = (moved - moved_high.astype(F32)).astype(BF16)
    spread = jnp.concatenate([mask.astype(BF16), moved_high, moved_low, jnp.zeros((8, ALLP), BF16)], 0)
    sums = jnp.dot(spread, images, preferred_element_type=F32)
    for r in range(R):
        part = sums[:, r * U:(r + 1) * U]
        plain = part[:8]
        sloped = part[8:16] + part[16:24]
        for n, (k, j) in enumerate(UNITS):
            sf[n, 4 * r:4 * r + 2, :] = plain[2 * k:2 * k + 2, BL * j:BL * (j + 1)]
            sf[n, 4 * r + 2:4 * r + 4, :] = sloped[2 * k:2 * k + 2, BL * j:BL * (j + 1)]
    ss[...] = sf[...].astype(BF16)

    def each_slab(n, act):
        def one(to, carry):
            @pl.when(to != g)
            def _():
                act(gz_copy(ss.at[n], ss_in.at[n, g], rs2_send.at[n, to], rs2_recv.at[n, g], to))
            return carry

        lax.fori_loop(low[n], top[n] + 1, one, 0)

    for n in reversed(range(len(UNITS))):
        each_slab(n, lambda copy: copy.start())
    for i in range(1, D):
        to = lax.rem(d + i, D)
        dom_copy(pose_s, pose_in.at[d], p_send.at[i], p_recv.at[d], to).start()

    acc[...] = jnp.zeros_like(acc)
    row = iota((256, R * SLAB), 0)
    within = lax.rem(row, 16)
    source = lax.rem(row, 4) * SLAB + 3 * lax.div(row, 16) + lax.div(within, 4)
    order = ((iota((256, R * SLAB), 1) == source) & (within < 12)).astype(F32).astype(BF16)

    for j in reversed(range(BLOCKS)):
        wide = BL * (j + 1)

        def spread_back(n, k, j=j, wide=wide):
            ss_in[n, g] = ss[n]
            for i in range(1, G):
                frm = lax.rem(g + i, G)
                gz_copy(ss.at[n], ss_in.at[n, frm], rs2_recv.at[n, frm], rs2_recv.at[n, frm], frm).wait_recv()
            total = ss_in[n, 0].astype(F32)
            for i in range(1, G):
                total = total + ss_in[n, i].astype(F32)
            for i in range(2):
                b = 2 * k + i
                wz = kz[b, :, BL * j:BL * (j + 1)]
                wd = kzd[b, :, BL * j:BL * (j + 1)]
                parts = []
                for r in range(R):
                    plain = total[4 * r + i:4 * r + i + 1]
                    sloped = total[4 * r + 2 + i:4 * r + 3 + i]
                    parts.append(jnp.concatenate([wz * plain + wd * sloped, wz * sloped], 1))
                left = jnp.concatenate(parts, 0)
                left_high = left.astype(BF16)
                left_low = (left - left_high.astype(F32)).astype(BF16)
                both = lax.dot_general(
                    jnp.concatenate([left_high, left_low], 0),
                    kt[b, :wide, 2 * BL * j:2 * BL * (j + 1)], NT, preferred_element_type=F32)
                acc[:, :wide] += both[:R * SLAB] + both[R * SLAB:]

        for k in range(PAIRS):
            n = UNITS.index((k, j))

            @pl.when(active(n, g))
            def _(n=n, k=k, spread_back=spread_back):
                spread_back(n, k)

        ordered = jnp.dot(order, acc[:, BL * j:BL * (j + 1)].astype(BF16), preferred_element_type=F32)
        bk[j] = ordered.astype(BF16).reshape(D, 16, BL)
        for i in range(1, D):
            to = lax.rem(d + i, D)
            dom_copy(bk.at[j, to], bk_in.at[j, d], b_send.at[j, i], b_recv.at[j, d], to).start()

    pose_in[d] = pose_s[...]
    for i in range(1, D):
        frm = lax.rem(d + i, D)
        dom_copy(pose_s, pose_in.at[frm], p_recv.at[frm], p_recv.at[frm], frm).wait_recv()
    pose = pose_in[0]
    for i in range(1, D):
        pose = pose + pose_in[i]
    lane = iota((8, ALLP), 1)
    kept = jnp.where(lax.div(lane, PART) == d, pose, 0.0)
    choose = (lax.rem(iota((ALLP, 128), 0), PART) == iota((ALLP, 128), 1)).astype(F32)
    picked = jnp.dot(kept, choose, precision=lax.Precision.HIGHEST, preferred_element_type=F32)
    pose_out[...] = picked[0:1, :PART]

    for j in reversed(range(BLOCKS)):
        bk_in[j, d] = bk[j, d]
        for i in range(1, D):
            frm = lax.rem(d + i, D)
            dom_copy(bk.at[j, 0], bk_in.at[j, frm], b_recv.at[j, frm], b_recv.at[j, frm], frm).wait_recv()
        total = bk_in[j, 0].astype(F32)
        for i in range(1, D):
            total = total + bk_in[j, i].astype(F32)
        for k in range(3):
            back_out[k, :, BL * j:BL * (j + 1)] = total[4 * k:4 * k + 4]

    for n in range(len(UNITS)):
        @pl.when(active(n, g))
        def _(n=n):
            for i in range(1, G):
                gz_copy(spb.at[n], sp_in.at[n, g], rs_send.at[n, i], rs_send.at[n, i], lax.rem(g + i, G)).wait_send()

        each_slab(n, lambda copy: copy.wait_send())
    for i in range(1, D // 2):
        dom_copy(w_all.at[d], w_all.at[d], w_send.at[i], w_send.at[i], sib).wait_send()
    for i in range(0, D // 2):
        dom_copy(w_all.at[d], w_all.at[d], f_send.at[i], f_send.at[i], sib).wait_send()
    for i in range(1, D):
        for j in range(BLOCKS):
            dom_copy(bk.at[j, 0], bk_in.at[j, d], b_send.at[j, i], b_send.at[j, i], sib).wait_send()
        dom_copy(pose_s, pose_in.at[d], p_send.at[i], p_send.at[i], sib).wait_send()


def local(volume, observed, ctf_table, ctf_class, bin_ids):
    vmem = pl.BlockSpec(memory_space=pltpu.VMEM)
    hbm = pl.BlockSpec(memory_space=pltpu.HBM)
    dma = pltpu.SemaphoreType.DMA
    pose, back = pl.pallas_call(
        body,
        out_shape=(jax.ShapeDtypeStruct((1, PART), F32), jax.ShapeDtypeStruct((3, R, X), F32)),
        in_specs=[hbm] * 5,
        out_specs=(vmem, vmem),
        scratch_shapes=[
            pltpu.VMEM((SLAB, R, X), F32),
            pltpu.VMEM((PART, R, U), BF16),
            pltpu.VMEM((NCTF, 2, U), F32),
            pltpu.SMEM((PART,), jnp.int32),
            pltpu.SMEM((PART,), jnp.int32),
            dma((5,)),
            pltpu.VMEM((2 * R * SLAB, X), BF16),
            pltpu.VMEM((NB_DEV, X, 2 * U), BF16),
            pltpu.VMEM((NB_DEV, SLAB, U), F32),
            pltpu.VMEM((NB_DEV, SLAB, U), F32),
            pltpu.VMEM((2 * NB_DEV, 128), F32),
            pltpu.VMEM((len(UNITS), 16, BL), F32),
            pltpu.VMEM((len(UNITS), 16, BL), BF16),
            pltpu.VMEM((len(UNITS), G, 16, BL), BF16),
            pltpu.VMEM((BLOCKS, 64, BL), F32),
            pltpu.VMEM((len(UNITS), 16, BL), F32),
            pltpu.VMEM((len(UNITS), 16, BL), BF16),
            pltpu.VMEM((len(UNITS), G, 16, BL), BF16),
            pltpu.VMEM((D, PART, WC + EXT), BF16),
            pltpu.VMEM((EXT, 2 * U), BF16),
            pltpu.VMEM((EXT, 2 * U), BF16),
            pltpu.VMEM((R * SLAB, X), F32),
            pltpu.VMEM((BLOCKS, D, 16, BL), BF16),
            pltpu.VMEM((BLOCKS, D, 16, BL), BF16),
            pltpu.VMEM((1, ALLP), F32),
            pltpu.VMEM((D, 1, ALLP), F32),
        ] + [dma((16,))] * 4 + [dma((len(UNITS), 16))] * 4 + [dma((BLOCKS, 16))] * 2 + [dma((16,))] * 2,
        compiler_params=pltpu.CompilerParams(
            collective_id=0, has_side_effects=True, vmem_limit_bytes=60 << 20),
        name="tilt_refine",
    )(volume, observed, ctf_table, ctf_class, bin_ids)
    return (pose.reshape(PART), back)


def solution(mesh):
    return jax.shard_map(
        local,
        mesh=mesh,
        in_specs=(
            P("gz", None, None),
            P(("gz", "dom"), None, None),
            P(),
            P(("gz", "dom")),
            P(("gz", "dom")),
        ),
        out_specs=(P(("gz", "dom")), P(("gz", "dom"), None, None)),
        check_vma=False,
    )
```

```python
import math

import jax
import jax.numpy as jnp
from jax import lax
from jax.experimental import pallas as pl
from jax.experimental.pallas import tpu as pltpu
from jax.sharding import PartitionSpec as P

NZ = 768
NB = 128
NB_DEV = 8
NCTF = 32
ITERS = 3
EPS = 1e-05
G = 16
D = 16
SLAB = 48
R = 4
X = 384
U = 384
PART = 16
ALLP = PART * D
WC = R * U
EXT = 128
BLOCKS = 3
BL = 128
PAIRS = 4
UNITS = [(k, j) for j in range(BLOCKS) for k in range(PAIRS)]
F32 = jnp.float32
BF16 = jnp.bfloat16
NU = len(UNITS)
NT = (((1,), (1,)), ((), ()))


def slab_spans():
    spans = []
    for k, j in UNITS:
        row = []
        for dom in range(D):
            sines = [math.sin(-0.5 * math.pi + math.pi * (2 * (dom + D * k) + i + 0.5) / NB)
                     for i in range(2)]
            centres = [0.5 * NZ + u * sine for sine in sines for u in (j * BL, j * BL + BL - 1)]
            first = math.floor(min(centres) - 1e-3)
            last = math.floor(max(centres) + 1e-3) + 1
            row.append((max(first, 0) // SLAB, min(last, NZ - 1) // SLAB))
        spans.append(row)
    return spans


def iota(shape, dim):
    return lax.broadcasted_iota(jnp.int32, shape, dim)


def gz_copy(src, dst, send, recv, to):
    return pltpu.make_async_remote_copy(
        src_ref=src, dst_ref=dst, send_sem=send, recv_sem=recv,
        device_id={"gz": to}, device_id_type=pl.DeviceIdType.MESH)


def dom_copy(src, dst, send, recv, to):
    return pltpu.make_async_remote_copy(
        src_ref=src, dst_ref=dst, send_sem=send, recv_sem=recv,
        device_id={"dom": to}, device_id_type=pl.DeviceIdType.MESH)


def each(first, last, act):
    def one(i, carry):
        act(i)
        return carry

    lax.fori_loop(first, last, one, 0)


def body(vol_hbm, obs_hbm, ctf_hbm, cls_hbm, bins_hbm, pose_out, back_out,
         vol, obs, ctf, cls, bins, low, top, in_sem, vb, kt, kz, kzd, sc, sp, spb, sp_in, s_all, sf, ss, ss_in, rows_t,
         w_all, c2h, c2l, acc, bk, bk_in, pose_s, pose_in,
         w_send, w_recv, f_send, f_recv,
         rs_send, rs_recv, rs2_send, rs2_recv, b_send, b_recv, p_send, p_recv):
    g = lax.axis_index("gz")
    d = lax.axis_index("dom")
    core = lax.rem(d, 2)
    zpos = lax.div(d, 2)
    sib = d + 1 - 2 * core

    def bin_of(slot):
        return 2 * d + 2 * D * lax.div(slot, 2) + lax.rem(slot, 2)


    barrier = pltpu.get_barrier_semaphore()
    each(1, D, lambda i: pl.semaphore_signal(
        barrier, inc=1, device_id={"dom": lax.rem(d + i, D)}, device_id_type=pl.DeviceIdType.MESH))
    each(1, G, lambda i: pl.semaphore_signal(
        barrier, inc=1, device_id={"gz": lax.rem(g + i, G)}, device_id_type=pl.DeviceIdType.MESH))

    for n, row in enumerate(slab_spans()):
        least, most = jnp.int32(row[0][0]), jnp.int32(row[0][1])
        for k in range(1, D):
            least = jnp.where(d == k, row[k][0], least)
            most = jnp.where(d == k, row[k][1], most)
        low[n] = least
        top[n] = most

    def active(n, slab):
        return (low[n] <= slab) & (slab <= top[n])

    fetches = [pltpu.make_async_copy(src, dst, in_sem.at[k]) for k, (src, dst) in enumerate(
        ((bins_hbm, bins), (cls_hbm, cls), (obs_hbm, obs), (ctf_hbm, ctf), (vol_hbm, vol)))]
    for fetch in fetches:
        fetch.start()
    for fetch in fetches[:4]:
        fetch.wait()

    rows = iota((PART, EXT), 0)
    lanes = iota((PART, EXT), 1)
    cls_col = jnp.zeros((PART, EXT), jnp.int32)
    bin_col = jnp.zeros((PART, EXT), jnp.int32)
    for i in range(PART):
        cls_col = jnp.where(rows == i, cls[i], cls_col)
        bin_col = jnp.where(rows == i, bins[i], bin_col)
    cls_hot = (cls_col == lanes).astype(F32)
    table = jnp.concatenate([ctf[:, 0, :], ctf[:, 1, :]], 1)
    contrast = jnp.dot(cls_hot[:, :NCTF], table, precision=lax.Precision.HIGHEST,
                       preferred_element_type=F32)
    for r in range(R):
        y = r % 2
        image = obs[:, r, :].astype(F32)
        w_all[d, :, r * U:(r + 1) * U] = (image * contrast[:, y * U:(y + 1) * U]).astype(BF16)
    extra = jnp.where(lanes == NCTF, bin_col.astype(F32), cls_hot)
    w_all[d, :, WC:] = extra.astype(BF16)

    square = table * table
    high = square.astype(BF16)
    c2h[...] = jnp.zeros_like(c2h)
    c2l[...] = jnp.zeros_like(c2l)
    c2h[:NCTF, :] = high
    c2l[:NCTF, :] = (square - high.astype(F32)).astype(BF16)

    fetches[4].wait()
    for r in range(R):
        plane_rows = vol[:, r, :]
        coarse = plane_rows.astype(BF16)
        vb[r * SLAB:(r + 1) * SLAB, :] = coarse
        vb[(R + r) * SLAB:(R + r + 1) * SLAB, :] = (plane_rows - coarse.astype(F32)).astype(BF16)
    bin_index = bin_of(iota((NB_DEV, 128), 0)).astype(F32)
    theta = -0.5 * math.pi + math.pi * (bin_index + 0.5) / NB
    sc[:NB_DEV, :] = jnp.sin(theta)
    sc[NB_DEV:, :] = jnp.cos(theta)

    for j in range(BLOCKS):
        wide = BL * (j + 1)
        radius = (BL * j + iota((1, BL), 1)).astype(F32)
        plane = (g * SLAB + iota((SLAB, BL), 0)).astype(F32)
        column = iota((wide, BL), 0).astype(F32)

        def extract(n, k, j=j, wide=wide, radius=radius, plane=plane, column=column):
            for i in range(2):
                b = 2 * k + i
                sine = sc[pl.ds(b, 1), :]
                cosine = sc[pl.ds(NB_DEV + b, 1), :]
                tx = column - radius * cosine
                fx = jnp.maximum(1.0 - tx * tx, 0.0)
                kx = jnp.concatenate([fx * fx, (tx * fx) * (radius * sine * (-4.0 / U))], 1)
                kx_high = kx.astype(BF16)
                kt[b, :wide, 2 * BL * j:2 * BL * (j + 1)] = kx_high
                kx_low = (kx - kx_high.astype(F32)).astype(BF16)
                tz = plane - (0.5 * NZ + radius * sine)
                fz = jnp.maximum(1.0 - tz * tz, 0.0)
                wz = fz * fz
                wd = (tz * fz) * (radius * cosine * (4.0 / U))
                kz[b, :, BL * j:BL * (j + 1)] = wz
                kzd[b, :, BL * j:BL * (j + 1)] = wd
                stacked = jnp.dot(vb[:, :wide], kx_high, preferred_element_type=F32)
                both = stacked[:R * SLAB] + stacked[R * SLAB:] + jnp.dot(
                    vb[:R * SLAB, :wide], kx_low, preferred_element_type=F32)
                for r in range(R):
                    direct = both[r * SLAB:(r + 1) * SLAB, :BL]
                    tilted = both[r * SLAB:(r + 1) * SLAB, BL:]
                    at = 2 * r + i
                    sp[n, at:at + 1, :] = jnp.sum(direct * wz, axis=0, keepdims=True)
                    sp[n, 8 + at:8 + at + 1, :] = jnp.sum(
                        direct * wd + tilted * wz, axis=0, keepdims=True)
            spb[n] = sp[n].astype(BF16)

        def unit(k, j=j, extract=extract):
            @pl.when(active(PAIRS * j + k, g))
            def _():
                extract(PAIRS * j + k, k)

        each(0, PAIRS, unit)

    pl.semaphore_wait(barrier, (G - 1) + (D - 1))

    each(1, D // 2, lambda i: dom_copy(
        w_all.at[d], w_all.at[d], w_send, w_recv.at[d], lax.rem(zpos + i, D // 2) * 2 + core).start())
    dom_copy(w_all.at[d], w_all.at[d], f_send, f_recv, sib).start()

    def send_slices(n):
        @pl.when(active(n, g))
        def _():
            each(1, G, lambda i: gz_copy(
                spb.at[n], sp_in.at[n, g], rs_send.at[n], rs_recv.at[n, g], lax.rem(g + i, G)).start())
            sp_in[n, g] = spb[n]

    each(0, NU, send_slices)

    def pass_on(i):
        frm = lax.rem(zpos + i, D // 2) * 2 + core
        dom_copy(w_all.at[frm], w_all.at[frm], w_recv.at[frm], w_recv.at[frm], sib).wait_recv()
        dom_copy(w_all.at[frm], w_all.at[frm], f_send, f_recv, sib).start()

    each(1, D // 2, pass_on)

    def gather_slices(n):
        def gather(frm, total):
            @pl.when(frm != g)
            def _():
                gz_copy(spb.at[n], sp_in.at[n, frm], rs_recv.at[n, frm], rs_recv.at[n, frm],
                        lax.rem(g + 1, G)).wait_recv()
            return total + sp_in[n, frm].astype(F32)

        total = lax.fori_loop(low[n], top[n] + 1, gather, jnp.zeros((16, BL), F32))
        j = lax.div(n, PAIRS)
        k = lax.rem(n, PAIRS)
        for m in range(8):
            for i in range(2):
                s_all[j, pl.ds(8 * m + 2 * k + i, 1), :] = total[2 * m + i:2 * m + i + 1]

    each(0, NU, gather_slices)

    def rows_of(kind, r):
        at = 32 * kind + 8 * r
        rounded = jnp.concatenate([s_all[j, at:at + 8, :] for j in range(BLOCKS)], 1)
        return rounded.astype(BF16).astype(F32)

    lead = [rows_of(0, r) for r in range(R)]
    slope = [rows_of(1, r) for r in range(R)]
    curve = jnp.concatenate([slope[y] * slope[y] + slope[y + 2] * slope[y + 2] for y in range(2)], 1)
    cross = jnp.concatenate([lead[y] * slope[y] + lead[y + 2] * slope[y + 2] for y in range(2)], 1)
    quad = jnp.concatenate([curve, cross], 0)
    quad_high = quad.astype(BF16)
    quad_low = (quad - quad_high.astype(F32)).astype(BF16)
    first = lax.dot_general(jnp.concatenate([quad_high, quad_low], 0), c2h[...], NT,
                            preferred_element_type=F32)
    tables = first[:16] + first[16:] + lax.dot_general(quad_high, c2l[...], NT,
                                                       preferred_element_type=F32)
    tables_high = tables.astype(BF16)
    tables_low = (tables - tables_high.astype(F32)).astype(BF16)
    pick = (iota((8, EXT), 1) == NCTF).astype(F32).astype(BF16)
    zero = jnp.zeros((8, EXT), BF16)
    lookup = jnp.concatenate([tables_high, tables_low, pick, zero], 0)
    slope_rows = jnp.concatenate(slope, 1).astype(BF16)

    half = w_all.at[0:D // 2]
    dom_copy(half, half, f_recv, f_recv, sib).wait_recv()

    images = w_all[:, :, :WC].reshape(ALLP, WC)
    marks = w_all[:, :, WC:].reshape(ALLP, EXT)
    looked = lax.dot_general(lookup, marks, NT, preferred_element_type=F32)
    along = lax.dot_general(slope_rows, images, NT, preferred_element_type=F32)
    held = looked[0:8] + looked[16:24]
    crossed = looked[8:16] + looked[24:32]
    own = bin_of(iota((8, ALLP), 0)).astype(F32) == looked[32:40]
    mask = own.astype(F32)
    power = jnp.sum(mask * held, axis=0, keepdims=True)
    match = jnp.sum(mask * (along - crossed), axis=0, keepdims=True)
    curvature = power + EPS
    shift = jnp.zeros_like(power)
    for _ in range(ITERS):
        shift = shift + 0.5 * (match - shift * power) / curvature
    pose_s[...] = shift * jnp.sqrt(curvature)
    moved = mask * shift
    moved_high = moved.astype(BF16)
    moved_low = (moved - moved_high.astype(F32)).astype(BF16)
    spread = jnp.concatenate([mask.astype(BF16), moved_high, moved_low, jnp.zeros((8, ALLP), BF16)], 0)
    sums = jnp.dot(spread, images, preferred_element_type=F32)
    for r in range(R):
        part = sums[:, r * U:(r + 1) * U]
        plain = part[:8]
        sloped = part[8:16] + part[16:24]
        for n, (k, j) in enumerate(UNITS):
            sf[n, 4 * r:4 * r + 2, :] = plain[2 * k:2 * k + 2, BL * j:BL * (j + 1)]
            sf[n, 4 * r + 2:4 * r + 4, :] = sloped[2 * k:2 * k + 2, BL * j:BL * (j + 1)]
    ss[...] = sf[...].astype(BF16)

    def each_slab(n, act):
        def one(to):
            @pl.when(to != g)
            def _():
                act(gz_copy(ss.at[n], ss_in.at[n, g], rs2_send.at[n, to], rs2_recv.at[n], to))

        each(low[n], top[n] + 1, one)

    each(0, NU, lambda n: each_slab(NU - 1 - n, lambda copy: copy.start()))
    each(1, D, lambda i: dom_copy(pose_s, pose_in.at[d], p_send, p_recv, lax.rem(d + i, D)).start())

    acc[...] = jnp.zeros_like(acc)
    row = iota((256, R * SLAB), 0)
    within = lax.rem(row, 16)
    source = lax.rem(row, 4) * SLAB + 3 * lax.div(row, 16) + lax.div(within, 4)
    order = ((iota((256, R * SLAB), 1) == source) & (within < 12)).astype(F32).astype(BF16)

    for j in reversed(range(BLOCKS)):
        wide = BL * (j + 1)

        def spread_back(n, k, j=j, wide=wide):
            ss_in[n, g] = ss[n]
            others = ss_in.at[n, 0:G - 1]
            gz_copy(others, others, rs2_recv.at[n], rs2_recv.at[n], lax.rem(g + 1, G)).wait_recv()
            rows_t[...] = jnp.sum(ss_in[n].astype(F32), axis=0)
            for i in range(2):
                b = 2 * k + i
                wz = kz[b, :, BL * j:BL * (j + 1)]
                wd = kzd[b, :, BL * j:BL * (j + 1)]
                parts = []
                for r in range(R):
                    plain = rows_t[4 * r + i:4 * r + i + 1, :]
                    sloped = rows_t[4 * r + 2 + i:4 * r + 3 + i, :]
                    parts.append(jnp.concatenate([wz * plain + wd * sloped, wz * sloped], 1))
                left = jnp.concatenate(parts, 0)
                left_high = left.astype(BF16)
                left_low = (left - left_high.astype(F32)).astype(BF16)
                both = lax.dot_general(
                    jnp.concatenate([left_high, left_low], 0),
                    kt[b, :wide, 2 * BL * j:2 * BL * (j + 1)], NT, preferred_element_type=F32)
                acc[:, :wide] += both[:R * SLAB] + both[R * SLAB:]

        def unit(k, j=j, spread_back=spread_back):
            @pl.when(active(PAIRS * j + k, g))
            def _():
                spread_back(PAIRS * j + k, k)

        each(0, PAIRS, unit)

        ordered = jnp.dot(order, acc[:, BL * j:BL * (j + 1)].astype(BF16), preferred_element_type=F32)
        bk[j] = ordered.astype(BF16).reshape(D, 16, BL)
        def send_block(i, j=j):
            to = lax.rem(d + i, D)
            dom_copy(bk.at[j, to], bk_in.at[j, d], b_send.at[j], b_recv.at[j], to).start()

        each(1, D, send_block)

    pose_in[d] = pose_s[...]
    others = pose_in.at[0:D - 1]
    dom_copy(others, others, p_recv, p_recv, sib).wait_recv()
    pose = jnp.sum(pose_in[...], axis=0)
    lane = iota((8, ALLP), 1)
    kept = jnp.where(lax.div(lane, PART) == d, pose, 0.0)
    choose = (lax.rem(iota((ALLP, 128), 0), PART) == iota((ALLP, 128), 1)).astype(F32)
    picked = jnp.dot(kept, choose, precision=lax.Precision.HIGHEST, preferred_element_type=F32)
    pose_out[...] = picked[0:1, :PART]

    for j in reversed(range(BLOCKS)):
        bk_in[j, d] = bk[j, d]
        others = bk_in.at[j, 0:D - 1]
        dom_copy(others, others, b_recv.at[j], b_recv.at[j], sib).wait_recv()
        total = jnp.sum(bk_in[j].astype(F32), axis=0)
        for k in range(3):
            back_out[k, :, BL * j:BL * (j + 1)] = total[4 * k:4 * k + 4]

    def finish(n):
        @pl.when(active(n, g))
        def _():
            sent = sp_in.at[n, 0:G - 1]
            gz_copy(sent, sent, rs_send.at[n], rs_send.at[n], lax.rem(g + 1, G)).wait_send()

        each_slab(n, lambda copy: copy.wait_send())

    each(0, NU, finish)
    sent = w_all.at[0:D // 2 - 1]
    dom_copy(sent, sent, w_send, w_send, sib).wait_send()
    dom_copy(half, half, f_send, f_send, sib).wait_send()
    sent = pose_in.at[0:D - 1]
    dom_copy(sent, sent, p_send, p_send, sib).wait_send()
    for j in range(BLOCKS):
        sent = bk_in.at[j, 0:D - 1]
        dom_copy(sent, sent, b_send.at[j], b_send.at[j], sib).wait_send()


def local(volume, observed, ctf_table, ctf_class, bin_ids):
    vmem = pl.BlockSpec(memory_space=pltpu.VMEM)
    hbm = pl.BlockSpec(memory_space=pltpu.HBM)
    dma = pltpu.SemaphoreType.DMA
    pose, back = pl.pallas_call(
        body,
        out_shape=(jax.ShapeDtypeStruct((1, PART), F32), jax.ShapeDtypeStruct((3, R, X), F32)),
        in_specs=[hbm] * 5,
        out_specs=(vmem, vmem),
        scratch_shapes=[
            pltpu.VMEM((SLAB, R, X), F32),
            pltpu.VMEM((PART, R, U), BF16),
            pltpu.VMEM((NCTF, 2, U), F32),
            pltpu.SMEM((PART,), jnp.int32),
            pltpu.SMEM((PART,), jnp.int32),
            pltpu.SMEM((NU,), jnp.int32),
            pltpu.SMEM((NU,), jnp.int32),
            dma((5,)),
            pltpu.VMEM((2 * R * SLAB, X), BF16),
            pltpu.VMEM((NB_DEV, X, 2 * U), BF16),
            pltpu.VMEM((NB_DEV, SLAB, U), F32),
            pltpu.VMEM((NB_DEV, SLAB, U), F32),
            pltpu.VMEM((2 * NB_DEV, 128), F32),
            pltpu.VMEM((NU, 16, BL), F32),
            pltpu.VMEM((NU, 16, BL), BF16),
            pltpu.VMEM((NU, G, 16, BL), BF16),
            pltpu.VMEM((BLOCKS, 64, BL), F32),
            pltpu.VMEM((NU, 16, BL), F32),
            pltpu.VMEM((NU, 16, BL), BF16),
            pltpu.VMEM((NU, G, 16, BL), BF16),
            pltpu.VMEM((16, BL), F32),
            pltpu.VMEM((D, PART, WC + EXT), BF16),
            pltpu.VMEM((EXT, 2 * U), BF16),
            pltpu.VMEM((EXT, 2 * U), BF16),
            pltpu.VMEM((R * SLAB, X), F32),
            pltpu.VMEM((BLOCKS, D, 16, BL), BF16),
            pltpu.VMEM((BLOCKS, D, 16, BL), BF16),
            pltpu.VMEM((1, ALLP), F32),
            pltpu.VMEM((D, 1, ALLP), F32),
        ] + [
            dma, dma((D,)), dma, dma,
            dma((NU,)), dma((NU, G)), dma((NU, G)), dma((NU,)),
            dma((BLOCKS,)), dma((BLOCKS,)), dma, dma,
        ],
        compiler_params=pltpu.CompilerParams(
            collective_id=0, has_side_effects=True, vmem_limit_bytes=60 << 20),
        name="tilt_refine",
    )(volume, observed, ctf_table, ctf_class, bin_ids)
    return (pose.reshape(PART), back)


def solution(mesh):
    return jax.shard_map(
        local,
        mesh=mesh,
        in_specs=(
            P("gz", None, None),
            P(("gz", "dom"), None, None),
            P(),
            P(("gz", "dom")),
            P(("gz", "dom")),
        ),
        out_specs=(P(("gz", "dom")), P(("gz", "dom"), None, None)),
        check_vma=False,
    )
```

```python
import math

import jax
import jax.numpy as jnp
from jax import lax
from jax.experimental import pallas as pl
from jax.experimental.pallas import tpu as pltpu
from jax.sharding import PartitionSpec as P

NZ = 768
NB = 128
NB_DEV = 8
NCTF = 32
ITERS = 3
EPS = 1e-05
G = 16
D = 16
SLAB = 48
R = 4
X = 384
U = 384
PART = 16
ALLP = PART * D
WC = R * U
EXT = 128
BLOCKS = 3
BL = 128
PAIRS = 4
UNITS = [(k, j) for j in range(BLOCKS) for k in range(PAIRS)]
F32 = jnp.float32
BF16 = jnp.bfloat16
NU = len(UNITS)
NT = (((1,), (1,)), ((), ()))


def slab_spans():
    spans = []
    for k, j in UNITS:
        row = []
        for dom in range(D):
            sines = [math.sin(-0.5 * math.pi + math.pi * (2 * (dom + D * k) + i + 0.5) / NB)
                     for i in range(2)]
            centres = [0.5 * NZ + u * sine for sine in sines for u in (j * BL, j * BL + BL - 1)]
            first = math.floor(min(centres) - 1e-3)
            last = math.floor(max(centres) + 1e-3) + 1
            row.append((max(first, 0) // SLAB, min(last, NZ - 1) // SLAB))
        spans.append(row)
    return spans


def iota(shape, dim):
    return lax.broadcasted_iota(jnp.int32, shape, dim)


def gz_copy(src, dst, send, recv, to):
    return pltpu.make_async_remote_copy(
        src_ref=src, dst_ref=dst, send_sem=send, recv_sem=recv,
        device_id={"gz": to}, device_id_type=pl.DeviceIdType.MESH)


def dom_copy(src, dst, send, recv, to):
    return pltpu.make_async_remote_copy(
        src_ref=src, dst_ref=dst, send_sem=send, recv_sem=recv,
        device_id={"dom": to}, device_id_type=pl.DeviceIdType.MESH)


def each(first, last, act):
    def one(i, carry):
        act(i)
        return carry

    lax.fori_loop(first, last, one, 0)


def body(vol_hbm, obs_hbm, ctf_hbm, cls_hbm, bins_hbm, pose_out, back_out,
         vol, obs, ctf, cls, bins, low, top, in_sem, vb, kt, kz, kzd, sc, sp, spb, sp_in, s_all, sf, ss, ss_in, rows_t,
         w_all, c2h, c2l, acc, bk, bk_in, pose_s, pose_in,
         w_send, w_recv, f_send, f_recv,
         rs_send, rs_recv, rs2_send, rs2_recv, b_send, b_recv, p_send, p_recv):
    g = lax.axis_index("gz")
    d = lax.axis_index("dom")
    core = lax.rem(d, 2)
    zpos = lax.div(d, 2)
    sib = d + 1 - 2 * core

    def bin_of(slot):
        return 2 * d + 2 * D * lax.div(slot, 2) + lax.rem(slot, 2)


    barrier = pltpu.get_barrier_semaphore()
    each(1, D, lambda i: pl.semaphore_signal(
        barrier, inc=1, device_id={"dom": lax.rem(d + i, D)}, device_id_type=pl.DeviceIdType.MESH))
    each(1, G, lambda i: pl.semaphore_signal(
        barrier, inc=1, device_id={"gz": lax.rem(g + i, G)}, device_id_type=pl.DeviceIdType.MESH))

    for n, row in enumerate(slab_spans()):
        least, most = jnp.int32(row[0][0]), jnp.int32(row[0][1])
        for k in range(1, D):
            least = jnp.where(d == k, row[k][0], least)
            most = jnp.where(d == k, row[k][1], most)
        low[n] = least
        top[n] = most

    def active(n, slab):
        return (low[n] <= slab) & (slab <= top[n])

    fetches = [pltpu.make_async_copy(src, dst, in_sem.at[k]) for k, (src, dst) in enumerate(
        ((bins_hbm, bins), (cls_hbm, cls), (obs_hbm, obs), (ctf_hbm, ctf), (vol_hbm, vol)))]
    for fetch in fetches:
        fetch.start()
    for fetch in fetches[:4]:
        fetch.wait()

    rows = iota((PART, EXT), 0)
    lanes = iota((PART, EXT), 1)
    cls_col = jnp.zeros((PART, EXT), jnp.int32)
    bin_col = jnp.zeros((PART, EXT), jnp.int32)
    for i in range(PART):
        cls_col = jnp.where(rows == i, cls[i], cls_col)
        bin_col = jnp.where(rows == i, bins[i], bin_col)
    cls_hot = (cls_col == lanes).astype(F32)
    table = jnp.concatenate([ctf[:, 0, :], ctf[:, 1, :]], 1)
    contrast = jnp.dot(cls_hot[:, :NCTF], table, precision=lax.Precision.HIGHEST,
                       preferred_element_type=F32)
    for r in range(R):
        y = r % 2
        image = obs[:, r, :].astype(F32)
        w_all[d, :, r * U:(r + 1) * U] = (image * contrast[:, y * U:(y + 1) * U]).astype(BF16)
    extra = jnp.where(lanes == NCTF, bin_col.astype(F32), cls_hot)
    w_all[d, :, WC:] = extra.astype(BF16)

    square = table * table
    high = square.astype(BF16)
    c2h[...] = jnp.zeros_like(c2h)
    c2l[...] = jnp.zeros_like(c2l)
    c2h[:NCTF, :] = high
    c2l[:NCTF, :] = (square - high.astype(F32)).astype(BF16)

    fetches[4].wait()
    def split_planes(part):
        for r in range(R):
            plane_rows = vol[pl.ds(16 * part, 16), r, :]
            coarse = plane_rows.astype(BF16)
            at = pl.multiple_of(r * SLAB + 16 * part, 16)
            vb[pl.ds(at, 16), :] = coarse
            vb[pl.ds(R * SLAB + at, 16), :] = (plane_rows - coarse.astype(F32)).astype(BF16)

    each(0, SLAB // 16, split_planes)
    bin_index = bin_of(iota((NB_DEV, 128), 0)).astype(F32)
    theta = -0.5 * math.pi + math.pi * (bin_index + 0.5) / NB
    sc[:NB_DEV, :] = jnp.sin(theta)
    sc[NB_DEV:, :] = jnp.cos(theta)
    plane = (g * SLAB + iota((SLAB, BL), 0)).astype(F32)
    column = iota((X, BL), 0).astype(F32)

    def extract(n, i):
        j = lax.div(n, PAIRS)
        b = 2 * lax.rem(n, PAIRS) + i
        radius = (BL * j + iota((1, BL), 1)).astype(F32)
        sine = sc[pl.ds(b, 1), :]
        cosine = sc[pl.ds(NB_DEV + b, 1), :]
        tx = column - radius * cosine
        fx = jnp.maximum(1.0 - tx * tx, 0.0)
        kx = jnp.concatenate([fx * fx, (tx * fx) * (radius * sine * (-4.0 / U))], 1)
        kx_high = kx.astype(BF16)
        kt[n, i] = kx_high
        kx_low = (kx - kx_high.astype(F32)).astype(BF16)
        tz = plane - (0.5 * NZ + radius * sine)
        fz = jnp.maximum(1.0 - tz * tz, 0.0)
        wz = fz * fz
        wd = (tz * fz) * (radius * cosine * (4.0 / U))
        kz[n, i] = wz
        kzd[n, i] = wd
        stacked = jnp.dot(vb[...], kx_high, preferred_element_type=F32)
        both = stacked[:R * SLAB] + stacked[R * SLAB:] + jnp.dot(
            vb[:R * SLAB, :], kx_low, preferred_element_type=F32)
        for r in range(R):
            direct = both[r * SLAB:(r + 1) * SLAB, :BL]
            tilted = both[r * SLAB:(r + 1) * SLAB, BL:]
            sp[n, pl.ds(2 * r + i, 1), :] = jnp.sum(direct * wz, axis=0, keepdims=True)
            sp[n, pl.ds(8 + 2 * r + i, 1), :] = jnp.sum(
                direct * wd + tilted * wz, axis=0, keepdims=True)

    def extract_unit(n):
        @pl.when(active(n, g))
        def _():
            each(0, 2, lambda i: extract(n, i))
            spb[n] = sp[n].astype(BF16)

    each(0, NU, extract_unit)

    pl.semaphore_wait(barrier, (G - 1) + (D - 1))

    each(1, D // 2, lambda i: dom_copy(
        w_all.at[d], w_all.at[d], w_send, w_recv.at[d], lax.rem(zpos + i, D // 2) * 2 + core).start())
    dom_copy(w_all.at[d], w_all.at[d], f_send, f_recv, sib).start()

    def send_slices(n):
        @pl.when(active(n, g))
        def _():
            each(1, G, lambda i: gz_copy(
                spb.at[n], sp_in.at[n, g], rs_send.at[n], rs_recv.at[n, g], lax.rem(g + i, G)).start())
            sp_in[n, g] = spb[n]

    each(0, NU, send_slices)

    def pass_on(i):
        frm = lax.rem(zpos + i, D // 2) * 2 + core
        dom_copy(w_all.at[frm], w_all.at[frm], w_recv.at[frm], w_recv.at[frm], sib).wait_recv()
        dom_copy(w_all.at[frm], w_all.at[frm], f_send, f_recv, sib).start()

    each(1, D // 2, pass_on)

    def gather_slices(n):
        def gather(frm, total):
            @pl.when(frm != g)
            def _():
                gz_copy(spb.at[n], sp_in.at[n, frm], rs_recv.at[n, frm], rs_recv.at[n, frm],
                        lax.rem(g + 1, G)).wait_recv()
            return total + sp_in[n, frm].astype(F32)

        total = lax.fori_loop(low[n], top[n] + 1, gather, jnp.zeros((16, BL), F32))
        j = lax.div(n, PAIRS)
        k = lax.rem(n, PAIRS)
        for m in range(8):
            for i in range(2):
                s_all[j, pl.ds(8 * m + 2 * k + i, 1), :] = total[2 * m + i:2 * m + i + 1]

    each(0, NU, gather_slices)

    def rows_of(kind, r):
        at = 32 * kind + 8 * r
        rounded = jnp.concatenate([s_all[j, at:at + 8, :] for j in range(BLOCKS)], 1)
        return rounded.astype(BF16).astype(F32)

    lead = [rows_of(0, r) for r in range(R)]
    slope = [rows_of(1, r) for r in range(R)]
    curve = jnp.concatenate([slope[y] * slope[y] + slope[y + 2] * slope[y + 2] for y in range(2)], 1)
    cross = jnp.concatenate([lead[y] * slope[y] + lead[y + 2] * slope[y + 2] for y in range(2)], 1)
    quad = jnp.concatenate([curve, cross], 0)
    quad_high = quad.astype(BF16)
    quad_low = (quad - quad_high.astype(F32)).astype(BF16)
    first = lax.dot_general(jnp.concatenate([quad_high, quad_low], 0), c2h[...], NT,
                            preferred_element_type=F32)
    tables = first[:16] + first[16:] + lax.dot_general(quad_high, c2l[...], NT,
                                                       preferred_element_type=F32)
    tables_high = tables.astype(BF16)
    tables_low = (tables - tables_high.astype(F32)).astype(BF16)
    pick = (iota((8, EXT), 1) == NCTF).astype(F32).astype(BF16)
    zero = jnp.zeros((8, EXT), BF16)
    lookup = jnp.concatenate([tables_high, tables_low, pick, zero], 0)
    slope_rows = jnp.concatenate(slope, 1).astype(BF16)

    half = w_all.at[0:D // 2]
    dom_copy(half, half, f_recv, f_recv, sib).wait_recv()

    images = w_all[:, :, :WC].reshape(ALLP, WC)
    marks = w_all[:, :, WC:].reshape(ALLP, EXT)
    looked = lax.dot_general(lookup, marks, NT, preferred_element_type=F32)
    along = lax.dot_general(slope_rows, images, NT, preferred_element_type=F32)
    held = looked[0:8] + looked[16:24]
    crossed = looked[8:16] + looked[24:32]
    own = bin_of(iota((8, ALLP), 0)).astype(F32) == looked[32:40]
    mask = own.astype(F32)
    power = jnp.sum(mask * held, axis=0, keepdims=True)
    match = jnp.sum(mask * (along - crossed), axis=0, keepdims=True)
    curvature = power + EPS
    shift = jnp.zeros_like(power)
    for _ in range(ITERS):
        shift = shift + 0.5 * (match - shift * power) / curvature
    pose_s[...] = shift * jnp.sqrt(curvature)
    moved = mask * shift
    moved_high = moved.astype(BF16)
    moved_low = (moved - moved_high.astype(F32)).astype(BF16)
    spread = jnp.concatenate([mask.astype(BF16), moved_high, moved_low, jnp.zeros((8, ALLP), BF16)], 0)
    sums = jnp.dot(spread, images, preferred_element_type=F32)
    for r in range(R):
        part = sums[:, r * U:(r + 1) * U]
        plain = part[:8]
        sloped = part[8:16] + part[16:24]
        for n, (k, j) in enumerate(UNITS):
            sf[n, 4 * r:4 * r + 2, :] = plain[2 * k:2 * k + 2, BL * j:BL * (j + 1)]
            sf[n, 4 * r + 2:4 * r + 4, :] = sloped[2 * k:2 * k + 2, BL * j:BL * (j + 1)]
    ss[...] = sf[...].astype(BF16)

    def each_slab(n, act):
        def one(to):
            @pl.when(to != g)
            def _():
                act(gz_copy(ss.at[n], ss_in.at[n, g], rs2_send.at[n, to], rs2_recv.at[n], to))

        each(low[n], top[n] + 1, one)

    each(0, NU, lambda n: each_slab(NU - 1 - n, lambda copy: copy.start()))
    each(1, D, lambda i: dom_copy(pose_s, pose_in.at[d], p_send, p_recv, lax.rem(d + i, D)).start())

    acc[...] = jnp.zeros_like(acc)
    row = iota((256, R * SLAB), 0)
    within = lax.rem(row, 16)
    source = lax.rem(row, 4) * SLAB + 3 * lax.div(row, 16) + lax.div(within, 4)
    order = ((iota((256, R * SLAB), 1) == source) & (within < 12)).astype(F32).astype(BF16)

    def spread_back(n, i):
        wz = kz[n, i]
        wd = kzd[n, i]
        parts = []
        for r in range(R):
            plain = rows_t[pl.ds(4 * r + i, 1), :]
            sloped = rows_t[pl.ds(4 * r + 2 + i, 1), :]
            parts.append(jnp.concatenate([wz * plain + wd * sloped, wz * sloped], 1))
        left = jnp.concatenate(parts, 0)
        left_high = left.astype(BF16)
        left_low = (left - left_high.astype(F32)).astype(BF16)
        both = lax.dot_general(
            jnp.concatenate([left_high, left_low], 0), kt[n, i], NT, preferred_element_type=F32)
        acc[...] += both[:R * SLAB] + both[R * SLAB:]

    def spread_unit(n):
        @pl.when(active(n, g))
        def _():
            ss_in[n, g] = ss[n]
            others = ss_in.at[n, 0:G - 1]
            gz_copy(others, others, rs2_recv.at[n], rs2_recv.at[n], lax.rem(g + 1, G)).wait_recv()
            rows_t[...] = jnp.sum(ss_in[n].astype(F32), axis=0)
            each(0, 2, lambda i: spread_back(n, i))

    def send_block(j):
        at = pl.ds(pl.multiple_of(BL * j, BL), BL)
        ordered = jnp.dot(order, acc[:, at].astype(BF16), preferred_element_type=F32)
        bk[j] = ordered.astype(BF16).reshape(D, 16, BL)

        def send(i):
            to = lax.rem(d + i, D)
            dom_copy(bk.at[j, to], bk_in.at[j, d], b_send.at[j], b_recv.at[j], to).start()

        each(1, D, send)

    def finish_block(back):
        j = BLOCKS - 1 - back
        each(0, PAIRS, lambda k: spread_unit(PAIRS * j + k))
        send_block(j)

    each(0, BLOCKS, finish_block)

    pose_in[d] = pose_s[...]
    others = pose_in.at[0:D - 1]
    dom_copy(others, others, p_recv, p_recv, sib).wait_recv()
    pose = jnp.sum(pose_in[...], axis=0)
    lane = iota((8, ALLP), 1)
    kept = jnp.where(lax.div(lane, PART) == d, pose, 0.0)
    choose = (lax.rem(iota((ALLP, 128), 0), PART) == iota((ALLP, 128), 1)).astype(F32)
    picked = jnp.dot(kept, choose, precision=lax.Precision.HIGHEST, preferred_element_type=F32)
    pose_out[...] = picked[0:1, :PART]

    for j in reversed(range(BLOCKS)):
        bk_in[j, d] = bk[j, d]
        others = bk_in.at[j, 0:D - 1]
        dom_copy(others, others, b_recv.at[j], b_recv.at[j], sib).wait_recv()
        total = jnp.sum(bk_in[j].astype(F32), axis=0)
        for k in range(3):
            back_out[k, :, BL * j:BL * (j + 1)] = total[4 * k:4 * k + 4]

    def finish(n):
        @pl.when(active(n, g))
        def _():
            sent = sp_in.at[n, 0:G - 1]
            gz_copy(sent, sent, rs_send.at[n], rs_send.at[n], lax.rem(g + 1, G)).wait_send()

        each_slab(n, lambda copy: copy.wait_send())

    each(0, NU, finish)
    sent = w_all.at[0:D // 2 - 1]
    dom_copy(sent, sent, w_send, w_send, sib).wait_send()
    dom_copy(half, half, f_send, f_send, sib).wait_send()
    sent = pose_in.at[0:D - 1]
    dom_copy(sent, sent, p_send, p_send, sib).wait_send()
    for j in range(BLOCKS):
        sent = bk_in.at[j, 0:D - 1]
        dom_copy(sent, sent, b_send.at[j], b_send.at[j], sib).wait_send()


def local(volume, observed, ctf_table, ctf_class, bin_ids):
    vmem = pl.BlockSpec(memory_space=pltpu.VMEM)
    hbm = pl.BlockSpec(memory_space=pltpu.HBM)
    dma = pltpu.SemaphoreType.DMA
    pose, back = pl.pallas_call(
        body,
        out_shape=(jax.ShapeDtypeStruct((1, PART), F32), jax.ShapeDtypeStruct((3, R, X), F32)),
        in_specs=[hbm] * 5,
        out_specs=(vmem, vmem),
        scratch_shapes=[
            pltpu.VMEM((SLAB, R, X), F32),
            pltpu.VMEM((PART, R, U), BF16),
            pltpu.VMEM((NCTF, 2, U), F32),
            pltpu.SMEM((PART,), jnp.int32),
            pltpu.SMEM((PART,), jnp.int32),
            pltpu.SMEM((NU,), jnp.int32),
            pltpu.SMEM((NU,), jnp.int32),
            dma((5,)),
            pltpu.VMEM((2 * R * SLAB, X), BF16),
            pltpu.VMEM((NU, 2, X, 2 * BL), BF16),
            pltpu.VMEM((NU, 2, SLAB, BL), F32),
            pltpu.VMEM((NU, 2, SLAB, BL), F32),
            pltpu.VMEM((2 * NB_DEV, 128), F32),
            pltpu.VMEM((NU, 16, BL), F32),
            pltpu.VMEM((NU, 16, BL), BF16),
            pltpu.VMEM((NU, G, 16, BL), BF16),
            pltpu.VMEM((BLOCKS, 64, BL), F32),
            pltpu.VMEM((NU, 16, BL), F32),
            pltpu.VMEM((NU, 16, BL), BF16),
            pltpu.VMEM((NU, G, 16, BL), BF16),
            pltpu.VMEM((16, BL), F32),
            pltpu.VMEM((D, PART, WC + EXT), BF16),
            pltpu.VMEM((EXT, 2 * U), BF16),
            pltpu.VMEM((EXT, 2 * U), BF16),
            pltpu.VMEM((R * SLAB, X), F32),
            pltpu.VMEM((BLOCKS, D, 16, BL), BF16),
            pltpu.VMEM((BLOCKS, D, 16, BL), BF16),
            pltpu.VMEM((1, ALLP), F32),
            pltpu.VMEM((D, 1, ALLP), F32),
        ] + [
            dma, dma((D,)), dma, dma,
            dma((NU,)), dma((NU, G)), dma((NU, G)), dma((NU,)),
            dma((BLOCKS,)), dma((BLOCKS,)), dma, dma,
        ],
        compiler_params=pltpu.CompilerParams(
            collective_id=0, has_side_effects=True, vmem_limit_bytes=60 << 20),
        name="tilt_refine",
    )(volume, observed, ctf_table, ctf_class, bin_ids)
    return (pose.reshape(PART), back)


def solution(mesh):
    return jax.shard_map(
        local,
        mesh=mesh,
        in_specs=(
            P("gz", None, None),
            P(("gz", "dom"), None, None),
            P(),
            P(("gz", "dom")),
            P(("gz", "dom")),
        ),
        out_specs=(P(("gz", "dom")), P(("gz", "dom"), None, None)),
        check_vma=False,
    )
```

```python
import math

import jax
import jax.numpy as jnp
from jax import lax
from jax.experimental import pallas as pl
from jax.experimental.pallas import tpu as pltpu
from jax.sharding import PartitionSpec as P

NZ = 768
NB = 128
NB_DEV = 8
NCTF = 32
ITERS = 3
EPS = 1e-05
G = 16
D = 16
SLAB = 48
R = 4
X = 384
U = 384
PART = 16
ALLP = PART * D
WC = R * U
EXT = 128
BLOCKS = 3
BL = 128
PAIRS = 4
UNITS = [(k, j) for j in range(BLOCKS) for k in range(PAIRS)]
F32 = jnp.float32
BF16 = jnp.bfloat16
NU = len(UNITS)
NT = (((1,), (1,)), ((), ()))


def slab_spans():
    spans = []
    for k, j in UNITS:
        row = []
        for dom in range(D):
            sines = [math.sin(-0.5 * math.pi + math.pi * (2 * (dom + D * k) + i + 0.5) / NB)
                     for i in range(2)]
            centres = [0.5 * NZ + u * sine for sine in sines for u in (j * BL, j * BL + BL - 1)]
            first = math.floor(min(centres) - 1e-3)
            last = math.floor(max(centres) + 1e-3) + 1
            row.append((max(first, 0) // SLAB, min(last, NZ - 1) // SLAB))
        spans.append(row)
    return spans


def iota(shape, dim):
    return lax.broadcasted_iota(jnp.int32, shape, dim)


def gz_copy(src, dst, send, recv, to):
    return pltpu.make_async_remote_copy(
        src_ref=src, dst_ref=dst, send_sem=send, recv_sem=recv,
        device_id={"gz": to}, device_id_type=pl.DeviceIdType.MESH)


def dom_copy(src, dst, send, recv, to):
    return pltpu.make_async_remote_copy(
        src_ref=src, dst_ref=dst, send_sem=send, recv_sem=recv,
        device_id={"dom": to}, device_id_type=pl.DeviceIdType.MESH)


def each(first, last, act):
    def one(i, carry):
        act(i)
        return carry

    lax.fori_loop(first, last, one, 0)


def body(vol_hbm, obs_hbm, ctf_hbm, cls_hbm, bins_hbm, pose_out, back_out,
         vol, obs, ctf, cls, bins, low, top, in_sem, vb, kt, kz, kzd, sc, sp, spb, sp_in, s_all, sf, ss, ss_in, rows_t,
         w_all, c2h, c2l, acc, bk, bk_in, pose_s, pose_in,
         ids, ids_in, w_send, w_recv, f_send, f_recv, i_send, i_recv,
         rs_send, rs_recv, rs2_send, rs2_recv, b_send, b_recv, p_send, p_recv):
    g = lax.axis_index("gz")
    d = lax.axis_index("dom")
    core = lax.rem(d, 2)
    zpos = lax.div(d, 2)
    sib = d + 1 - 2 * core

    def bin_of(slot):
        return 2 * d + 2 * D * lax.div(slot, 2) + lax.rem(slot, 2)


    barrier = pltpu.get_barrier_semaphore()
    each(1, D, lambda i: pl.semaphore_signal(
        barrier, inc=1, device_id={"dom": lax.rem(d + i, D)}, device_id_type=pl.DeviceIdType.MESH))
    each(1, G, lambda i: pl.semaphore_signal(
        barrier, inc=1, device_id={"gz": lax.rem(g + i, G)}, device_id_type=pl.DeviceIdType.MESH))

    for n, row in enumerate(slab_spans()):
        least, most = jnp.int32(row[0][0]), jnp.int32(row[0][1])
        for k in range(1, D):
            least = jnp.where(d == k, row[k][0], least)
            most = jnp.where(d == k, row[k][1], most)
        low[n] = least
        top[n] = most

    def active(n, slab):
        return (low[n] <= slab) & (slab <= top[n])

    fetches = [pltpu.make_async_copy(src, dst, in_sem.at[k]) for k, (src, dst) in enumerate(
        ((bins_hbm, bins), (cls_hbm, cls), (obs_hbm, obs), (ctf_hbm, ctf), (vol_hbm, vol)))]
    for fetch in fetches:
        fetch.start()
    for fetch in fetches[:4]:
        fetch.wait()

    rows = iota((PART, NCTF), 0)
    along_row = iota((1, ALLP), 1) - PART * d
    cls_col = jnp.zeros((PART, NCTF), jnp.int32)
    id_row = jnp.zeros((1, ALLP), jnp.int32)
    for i in range(PART):
        cls_col = jnp.where(rows == i, cls[i], cls_col)
        id_row = jnp.where(along_row == i, NCTF * bins[i] + cls[i], id_row)
    cls_hot = (cls_col == iota((PART, NCTF), 1)).astype(F32)
    ids[...] = id_row.astype(F32)
    table = jnp.concatenate([ctf[:, 0, :], ctf[:, 1, :]], 1)
    contrast = jnp.dot(cls_hot, table, precision=lax.Precision.HIGHEST,
                       preferred_element_type=F32)
    for r in range(R):
        y = r % 2
        image = obs[:, r, :].astype(F32)
        w_all[d, :, r * U:(r + 1) * U] = (image * contrast[:, y * U:(y + 1) * U]).astype(BF16)

    pl.semaphore_wait(barrier, (G - 1) + (D - 1))

    each(1, D // 2, lambda i: dom_copy(
        w_all.at[d], w_all.at[d], w_send, w_recv.at[d], lax.rem(zpos + i, D // 2) * 2 + core).start())
    dom_copy(w_all.at[d], w_all.at[d], f_send, f_recv, sib).start()
    each(1, D, lambda i: dom_copy(ids, ids_in.at[d], i_send, i_recv, lax.rem(d + i, D)).start())

    square = table * table
    high = square.astype(BF16)
    c2h[...] = jnp.zeros_like(c2h)
    c2l[...] = jnp.zeros_like(c2l)
    c2h[:NCTF, :] = high
    c2l[:NCTF, :] = (square - high.astype(F32)).astype(BF16)

    fetches[4].wait()
    def split_planes(part):
        for r in range(R):
            plane_rows = vol[pl.ds(16 * part, 16), r, :]
            coarse = plane_rows.astype(BF16)
            at = pl.multiple_of(r * SLAB + 16 * part, 16)
            vb[pl.ds(at, 16), :] = coarse
            vb[pl.ds(R * SLAB + at, 16), :] = (plane_rows - coarse.astype(F32)).astype(BF16)

    each(0, SLAB // 16, split_planes)
    bin_index = bin_of(iota((NB_DEV, 128), 0)).astype(F32)
    theta = -0.5 * math.pi + math.pi * (bin_index + 0.5) / NB
    sc[:NB_DEV, :] = jnp.sin(theta)
    sc[NB_DEV:, :] = jnp.cos(theta)

    for j in range(BLOCKS):
        wide = BL * (j + 1)
        radius = (BL * j + iota((1, BL), 1)).astype(F32)
        plane = (g * SLAB + iota((SLAB, BL), 0)).astype(F32)
        column = iota((wide, BL), 0).astype(F32)

        def extract(n, k, j=j, wide=wide, radius=radius, plane=plane, column=column):
            for i in range(2):
                b = 2 * k + i
                sine = sc[pl.ds(b, 1), :]
                cosine = sc[pl.ds(NB_DEV + b, 1), :]
                tx = column - radius * cosine
                fx = jnp.maximum(1.0 - tx * tx, 0.0)
                kx = jnp.concatenate([fx * fx, (tx * fx) * (radius * sine * (-4.0 / U))], 1)
                kx_high = kx.astype(BF16)
                kt[b, :wide, 2 * BL * j:2 * BL * (j + 1)] = kx_high
                kx_low = (kx - kx_high.astype(F32)).astype(BF16)
                tz = plane - (0.5 * NZ + radius * sine)
                fz = jnp.maximum(1.0 - tz * tz, 0.0)
                wz = fz * fz
                wd = (tz * fz) * (radius * cosine * (4.0 / U))
                kz[b, :, BL * j:BL * (j + 1)] = wz
                kzd[b, :, BL * j:BL * (j + 1)] = wd
                stacked = jnp.dot(vb[:, :wide], kx_high, preferred_element_type=F32)
                both = stacked[:R * SLAB] + stacked[R * SLAB:] + jnp.dot(
                    vb[:R * SLAB, :wide], kx_low, preferred_element_type=F32)
                for r in range(R):
                    direct = both[r * SLAB:(r + 1) * SLAB, :BL]
                    tilted = both[r * SLAB:(r + 1) * SLAB, BL:]
                    at = 2 * r + i
                    sp[n, at:at + 1, :] = jnp.sum(direct * wz, axis=0, keepdims=True)
                    sp[n, 8 + at:8 + at + 1, :] = jnp.sum(
                        direct * wd + tilted * wz, axis=0, keepdims=True)
            spb[n] = sp[n].astype(BF16)

        def unit(k, j=j, extract=extract):
            @pl.when(active(PAIRS * j + k, g))
            def _():
                extract(PAIRS * j + k, k)

        each(0, PAIRS, unit)

    def send_slices(n):
        @pl.when(active(n, g))
        def _():
            each(1, G, lambda i: gz_copy(
                spb.at[n], sp_in.at[n, g], rs_send.at[n], rs_recv.at[n, g], lax.rem(g + i, G)).start())
            sp_in[n, g] = spb[n]

    each(0, NU, send_slices)

    def gather_slices(n):
        def gather(frm, total):
            @pl.when(frm != g)
            def _():
                gz_copy(spb.at[n], sp_in.at[n, frm], rs_recv.at[n, frm], rs_recv.at[n, frm],
                        lax.rem(g + 1, G)).wait_recv()
            return total + sp_in[n, frm].astype(F32)

        total = lax.fori_loop(low[n], top[n] + 1, gather, jnp.zeros((16, BL), F32))
        j = lax.div(n, PAIRS)
        k = lax.rem(n, PAIRS)
        for m in range(8):
            for i in range(2):
                s_all[j, pl.ds(8 * m + 2 * k + i, 1), :] = total[2 * m + i:2 * m + i + 1]

    each(0, NU, gather_slices)

    def rows_of(kind, r):
        at = 32 * kind + 8 * r
        rounded = jnp.concatenate([s_all[j, at:at + 8, :] for j in range(BLOCKS)], 1)
        return rounded.astype(BF16).astype(F32)

    lead = [rows_of(0, r) for r in range(R)]
    slope = [rows_of(1, r) for r in range(R)]
    curve = jnp.concatenate([slope[y] * slope[y] + slope[y + 2] * slope[y + 2] for y in range(2)], 1)
    cross = jnp.concatenate([lead[y] * slope[y] + lead[y + 2] * slope[y + 2] for y in range(2)], 1)
    quad = jnp.concatenate([curve, cross], 0)
    quad_high = quad.astype(BF16)
    quad_low = (quad - quad_high.astype(F32)).astype(BF16)
    first = lax.dot_general(jnp.concatenate([quad_high, quad_low], 0), c2h[...], NT,
                            preferred_element_type=F32)
    tables = first[:16] + first[16:] + lax.dot_general(quad_high, c2l[...], NT,
                                                       preferred_element_type=F32)
    tables_high = tables.astype(BF16)
    tables_low = (tables - tables_high.astype(F32)).astype(BF16)
    lookup = jnp.concatenate([tables_high, tables_low], 0)[:, :NCTF]
    slope_rows = jnp.concatenate(slope, 1).astype(BF16)

    ids_in[d] = ids[...]
    others = ids_in.at[0:D - 1]
    dom_copy(others, others, i_recv, i_recv, sib).wait_recv()
    id_row = jnp.sum(ids_in[...], axis=0).astype(jnp.int32)
    bin_row = lax.div(id_row, NCTF)
    cls_rows = (iota((NCTF, ALLP), 0) == lax.rem(id_row, NCTF)).astype(F32).astype(BF16)
    looked = jnp.dot(lookup, cls_rows, preferred_element_type=F32)
    held = looked[0:8] + looked[16:24]
    crossed = looked[8:16] + looked[24:32]
    mask = (bin_of(iota((8, ALLP), 0)) == bin_row).astype(F32)
    power = jnp.sum(mask * held, axis=0, keepdims=True)
    cross_row = jnp.sum(mask * crossed, axis=0, keepdims=True)
    curvature = power + EPS
    slot = iota((16, ALLP), 0)
    sloped_row = lax.rem(lax.div(slot, 2), 2) == 1
    mask_rows = (2 * d + 2 * D * lax.div(slot, 4) + lax.rem(slot, 2) == bin_row).astype(F32)

    def pass_on(i):
        step = lax.div(i + 1, 2) * (1 - 2 * lax.rem(i, 2))
        frm = lax.rem(zpos + step + D // 2, D // 2) * 2 + core
        dom_copy(w_all.at[frm], w_all.at[frm], w_recv.at[frm], w_recv.at[frm], sib).wait_recv()
        dom_copy(w_all.at[frm], w_all.at[frm], f_send, f_recv, sib).start()

    each(1, D // 2, pass_on)
    half = w_all.at[0:D // 2]
    dom_copy(half, half, f_recv, f_recv, sib).wait_recv()

    images = w_all[...].reshape(ALLP, WC)
    along = lax.dot_general(slope_rows, images, NT, preferred_element_type=F32)
    match = jnp.sum(mask * along, axis=0, keepdims=True) - cross_row
    shift = jnp.zeros_like(power)
    for _ in range(ITERS):
        shift = shift + 0.5 * (match - shift * power) / curvature
    pose_s[...] = shift * jnp.sqrt(curvature)
    spread = mask_rows * jnp.where(sloped_row, shift, 1.0)
    spread_high = spread.astype(BF16)
    spread_low = (spread - spread_high.astype(F32)).astype(BF16)
    sums = jnp.dot(jnp.concatenate([spread_high, spread_low], 0), images, preferred_element_type=F32)
    sums = sums[:16] + sums[16:]
    for n, (k, j) in enumerate(UNITS):
        for r in range(R):
            at = r * U + BL * j
            sf[n, 4 * r:4 * r + 4, :] = sums[4 * k:4 * k + 4, at:at + BL]
    ss[...] = sf[...].astype(BF16)

    def each_slab(n, act):
        def one(to):
            @pl.when(to != g)
            def _():
                act(gz_copy(ss.at[n], ss_in.at[n, g], rs2_send.at[n, to], rs2_recv.at[n], to))

        each(low[n], top[n] + 1, one)

    each(0, NU, lambda n: each_slab(NU - 1 - n, lambda copy: copy.start()))
    each(1, D, lambda i: dom_copy(pose_s, pose_in.at[d], p_send, p_recv, lax.rem(d + i, D)).start())

    acc[...] = jnp.zeros_like(acc)
    row = iota((256, R * SLAB), 0)
    within = lax.rem(row, 16)
    source = lax.rem(row, 4) * SLAB + 3 * lax.div(row, 16) + lax.div(within, 4)
    order = ((iota((256, R * SLAB), 1) == source) & (within < 12)).astype(F32).astype(BF16)

    for j in reversed(range(BLOCKS)):
        wide = BL * (j + 1)

        def spread_back(n, k, j=j, wide=wide):
            ss_in[n, g] = ss[n]
            others = ss_in.at[n, 0:G - 1]
            gz_copy(others, others, rs2_recv.at[n], rs2_recv.at[n], lax.rem(g + 1, G)).wait_recv()
            rows_t[...] = jnp.sum(ss_in[n].astype(F32), axis=0)
            for i in range(2):
                b = 2 * k + i
                wz = kz[b, :, BL * j:BL * (j + 1)]
                wd = kzd[b, :, BL * j:BL * (j + 1)]
                parts = []
                for r in range(R):
                    plain = rows_t[4 * r + i:4 * r + i + 1, :]
                    sloped = rows_t[4 * r + 2 + i:4 * r + 3 + i, :]
                    parts.append(jnp.concatenate([wz * plain + wd * sloped, wz * sloped], 1))
                left = jnp.concatenate(parts, 0)
                left_high = left.astype(BF16)
                left_low = (left - left_high.astype(F32)).astype(BF16)
                both = lax.dot_general(
                    jnp.concatenate([left_high, left_low], 0),
                    kt[b, :wide, 2 * BL * j:2 * BL * (j + 1)], NT, preferred_element_type=F32)
                acc[:, :wide] += both[:R * SLAB] + both[R * SLAB:]

        def unit(k, j=j, spread_back=spread_back):
            @pl.when(active(PAIRS * j + k, g))
            def _():
                spread_back(PAIRS * j + k, k)

        each(0, PAIRS, unit)

        ordered = jnp.dot(order, acc[:, BL * j:BL * (j + 1)].astype(BF16), preferred_element_type=F32)
        bk[j] = ordered.astype(BF16).reshape(D, 16, BL)
        def send_block(i, j=j):
            to = lax.rem(d + i, D)
            dom_copy(bk.at[j, to], bk_in.at[j, d], b_send.at[j], b_recv.at[j], to).start()

        each(1, D, send_block)

    pose_in[d] = pose_s[...]
    others = pose_in.at[0:D - 1]
    dom_copy(others, others, p_recv, p_recv, sib).wait_recv()
    pose = jnp.sum(pose_in[...], axis=0)
    lane = iota((8, ALLP), 1)
    kept = jnp.where(lax.div(lane, PART) == d, pose, 0.0)
    choose = (lax.rem(iota((ALLP, 128), 0), PART) == iota((ALLP, 128), 1)).astype(F32)
    picked = jnp.dot(kept, choose, precision=lax.Precision.HIGHEST, preferred_element_type=F32)
    pose_out[...] = picked[0:1, :PART]

    def finish(n):
        @pl.when(active(n, g))
        def _():
            sent = sp_in.at[n, 0:G - 1]
            gz_copy(sent, sent, rs_send.at[n], rs_send.at[n], lax.rem(g + 1, G)).wait_send()

        each_slab(n, lambda copy: copy.wait_send())

    each(0, NU, finish)
    sent = w_all.at[0:D // 2 - 1]
    dom_copy(sent, sent, w_send, w_send, sib).wait_send()
    dom_copy(half, half, f_send, f_send, sib).wait_send()
    sent = pose_in.at[0:D - 1]
    dom_copy(sent, sent, p_send, p_send, sib).wait_send()
    sent = ids_in.at[0:D - 1]
    dom_copy(sent, sent, i_send, i_send, sib).wait_send()

    for j in reversed(range(BLOCKS)):
        bk_in[j, d] = bk[j, d]
        others = bk_in.at[j, 0:D - 1]
        dom_copy(others, others, b_recv.at[j], b_recv.at[j], sib).wait_recv()
        total = jnp.sum(bk_in[j].astype(F32), axis=0)
        for k in range(3):
            back_out[k, :, BL * j:BL * (j + 1)] = total[4 * k:4 * k + 4]

    for j in range(BLOCKS):
        sent = bk_in.at[j, 0:D - 1]
        dom_copy(sent, sent, b_send.at[j], b_send.at[j], sib).wait_send()


def local(volume, observed, ctf_table, ctf_class, bin_ids):
    vmem = pl.BlockSpec(memory_space=pltpu.VMEM)
    hbm = pl.BlockSpec(memory_space=pltpu.HBM)
    dma = pltpu.SemaphoreType.DMA
    pose, back = pl.pallas_call(
        body,
        out_shape=(jax.ShapeDtypeStruct((1, PART), F32), jax.ShapeDtypeStruct((3, R, X), F32)),
        in_specs=[hbm] * 5,
        out_specs=(vmem, vmem),
        scratch_shapes=[
            pltpu.VMEM((SLAB, R, X), F32),
            pltpu.VMEM((PART, R, U), BF16),
            pltpu.VMEM((NCTF, 2, U), F32),
            pltpu.SMEM((PART,), jnp.int32),
            pltpu.SMEM((PART,), jnp.int32),
            pltpu.SMEM((NU,), jnp.int32),
            pltpu.SMEM((NU,), jnp.int32),
            dma((5,)),
            pltpu.VMEM((2 * R * SLAB, X), BF16),
            pltpu.VMEM((NB_DEV, X, 2 * U), BF16),
            pltpu.VMEM((NB_DEV, SLAB, U), F32),
            pltpu.VMEM((NB_DEV, SLAB, U), F32),
            pltpu.VMEM((2 * NB_DEV, 128), F32),
            pltpu.VMEM((NU, 16, BL), F32),
            pltpu.VMEM((NU, 16, BL), BF16),
            pltpu.VMEM((NU, G, 16, BL), BF16),
            pltpu.VMEM((BLOCKS, 64, BL), F32),
            pltpu.VMEM((NU, 16, BL), F32),
            pltpu.VMEM((NU, 16, BL), BF16),
            pltpu.VMEM((NU, G, 16, BL), BF16),
            pltpu.VMEM((16, BL), F32),
            pltpu.VMEM((D, PART, WC), BF16),
            pltpu.VMEM((EXT, 2 * U), BF16),
            pltpu.VMEM((EXT, 2 * U), BF16),
            pltpu.VMEM((R * SLAB, X), F32),
            pltpu.VMEM((BLOCKS, D, 16, BL), BF16),
            pltpu.VMEM((BLOCKS, D, 16, BL), BF16),
            pltpu.VMEM((1, ALLP), F32),
            pltpu.VMEM((D, 1, ALLP), F32),
        ] + [
            pltpu.VMEM((1, ALLP), F32),
            pltpu.VMEM((D, 1, ALLP), F32),
            dma, dma((D,)), dma, dma, dma, dma,
            dma((NU,)), dma((NU, G)), dma((NU, G)), dma((NU,)),
            dma((BLOCKS,)), dma((BLOCKS,)), dma, dma,
        ],
        compiler_params=pltpu.CompilerParams(
            collective_id=0, has_side_effects=True, vmem_limit_bytes=60 << 20),
        name="tilt_refine",
    )(volume, observed, ctf_table, ctf_class, bin_ids)
    return (pose.reshape(PART), back)


def solution(mesh):
    return jax.shard_map(
        local,
        mesh=mesh,
        in_specs=(
            P("gz", None, None),
            P(("gz", "dom"), None, None),
            P(),
            P(("gz", "dom")),
            P(("gz", "dom")),
        ),
        out_specs=(P(("gz", "dom")), P(("gz", "dom"), None, None)),
        check_vma=False,
    )
```

```python
import math

import jax
import jax.numpy as jnp
from jax import lax
from jax.experimental import pallas as pl
from jax.experimental.pallas import tpu as pltpu
from jax.sharding import PartitionSpec as P

NZ = 768
NB = 128
NB_DEV = 8
NCTF = 32
ITERS = 3
EPS = 1e-05
G = 16
D = 16
SLAB = 48
R = 4
X = 384
U = 384
PART = 16
ALLP = PART * D
WC = R * U
EXT = 128
BLOCKS = 3
BL = 128
PAIRS = 4
UNITS = [(k, j) for j in range(BLOCKS) for k in range(PAIRS)]
F32 = jnp.float32
BF16 = jnp.bfloat16
NU = len(UNITS)
NT = (((1,), (1,)), ((), ()))


def slab_spans():
    spans = []
    for k, j in UNITS:
        row = []
        for dom in range(D):
            sines = [math.sin(-0.5 * math.pi + math.pi * (2 * (dom + D * k) + i + 0.5) / NB)
                     for i in range(2)]
            centres = [0.5 * NZ + u * sine for sine in sines for u in (j * BL, j * BL + BL - 1)]
            first = math.floor(min(centres) - 1e-3)
            last = math.floor(max(centres) + 1e-3) + 1
            row.append((max(first, 0) // SLAB, min(last, NZ - 1) // SLAB))
        spans.append(row)
    return spans


def iota(shape, dim):
    return lax.broadcasted_iota(jnp.int32, shape, dim)


def gz_copy(src, dst, send, recv, to):
    return pltpu.make_async_remote_copy(
        src_ref=src, dst_ref=dst, send_sem=send, recv_sem=recv,
        device_id={"gz": to}, device_id_type=pl.DeviceIdType.MESH)


def dom_copy(src, dst, send, recv, to):
    return pltpu.make_async_remote_copy(
        src_ref=src, dst_ref=dst, send_sem=send, recv_sem=recv,
        device_id={"dom": to}, device_id_type=pl.DeviceIdType.MESH)


def each(first, last, act):
    def one(i, carry):
        act(i)
        return carry

    lax.fori_loop(first, last, one, 0)


def far_first(i, n):
    return n // 2 + lax.div(i, 2) * (2 * lax.rem(i, 2) - 1)


def body(vol_hbm, obs_hbm, ctf_hbm, mark_hbm, pose_out, back_out,
         vol, obs, ctf, mark, low, top, in_sem, vb, kt, kz, kzd, sc, sp, spb, sp_in, s_all, sf, ss, ss_in, rows_t,
         w_all, c2h, c2l, acc, bk, bk_in, pose_s, pose_in,
         ids, ids_in, w_send, w_recv, f_send, f_recv, i_send, i_recv,
         rs_send, rs_recv, rs2_send, rs2_recv, b_send, b_recv, p_send, p_recv):
    g = lax.axis_index("gz")
    d = lax.axis_index("dom")
    core = lax.rem(d, 2)
    zpos = lax.div(d, 2)
    sib = d + 1 - 2 * core

    def bin_of(slot):
        return 2 * d + 2 * D * lax.div(slot, 2) + lax.rem(slot, 2)


    barrier = pltpu.get_barrier_semaphore()
    each(1, D, lambda i: pl.semaphore_signal(
        barrier, inc=1, device_id={"dom": lax.rem(d + i, D)}, device_id_type=pl.DeviceIdType.MESH))
    each(1, G, lambda i: pl.semaphore_signal(
        barrier, inc=1, device_id={"gz": lax.rem(g + i, G)}, device_id_type=pl.DeviceIdType.MESH))

    for n, row in enumerate(slab_spans()):
        least, most = jnp.int32(row[0][0]), jnp.int32(row[0][1])
        for k in range(1, D):
            least = jnp.where(d == k, row[k][0], least)
            most = jnp.where(d == k, row[k][1], most)
        low[n] = least
        top[n] = most

    def active(n, slab):
        return (low[n] <= slab) & (slab <= top[n])

    fetches = [pltpu.make_async_copy(src, dst, in_sem.at[k]) for k, (src, dst) in enumerate(
        ((mark_hbm, mark), (obs_hbm, obs), (ctf_hbm, ctf), (vol_hbm, vol)))]
    for fetch in fetches:
        fetch.start()
    for fetch in fetches[:3]:
        fetch.wait()

    rows = iota((PART, NCTF), 0)
    along_row = iota((1, ALLP), 1) - PART * d
    cls_col = jnp.zeros((PART, NCTF), jnp.int32)
    id_row = jnp.zeros((1, ALLP), jnp.int32)
    for i in range(PART):
        cls_col = jnp.where(rows == i, lax.rem(mark[i], NCTF), cls_col)
        id_row = jnp.where(along_row == i, mark[i], id_row)
    cls_hot = (cls_col == iota((PART, NCTF), 1)).astype(F32)
    ids[...] = id_row.astype(F32)
    table = jnp.concatenate([ctf[:, 0, :], ctf[:, 1, :]], 1)
    contrast = jnp.dot(cls_hot, table, precision=lax.Precision.HIGHEST,
                       preferred_element_type=F32)
    for r in range(R):
        y = r % 2
        image = obs[:, r, :].astype(F32)
        w_all[d, :, r * U:(r + 1) * U] = (image * contrast[:, y * U:(y + 1) * U]).astype(BF16)

    pl.semaphore_wait(barrier, (G - 1) + (D - 1))

    each(1, D // 2, lambda i: dom_copy(
        w_all.at[d], w_all.at[d], w_send, w_recv.at[d], lax.rem(zpos + far_first(i, D // 2), D // 2) * 2 + core).start())
    dom_copy(w_all.at[d], w_all.at[d], f_send, f_recv, sib).start()
    each(1, D, lambda i: dom_copy(ids, ids_in.at[d], i_send, i_recv, lax.rem(d + i, D)).start())

    square = table * table
    high = square.astype(BF16)
    c2h[...] = jnp.zeros_like(c2h)
    c2l[...] = jnp.zeros_like(c2l)
    c2h[:NCTF, :] = high
    c2l[:NCTF, :] = (square - high.astype(F32)).astype(BF16)

    fetches[3].wait()
    def split_planes(part):
        for r in range(R):
            plane_rows = vol[pl.ds(16 * part, 16), r, :]
            coarse = plane_rows.astype(BF16)
            at = pl.multiple_of(r * SLAB + 16 * part, 16)
            vb[pl.ds(at, 16), :] = coarse
            vb[pl.ds(R * SLAB + at, 16), :] = (plane_rows - coarse.astype(F32)).astype(BF16)

    each(0, SLAB // 16, split_planes)
    bin_index = bin_of(iota((NB_DEV, 128), 0)).astype(F32)
    theta = -0.5 * math.pi + math.pi * (bin_index + 0.5) / NB
    sc[:NB_DEV, :] = jnp.sin(theta)
    sc[NB_DEV:, :] = jnp.cos(theta)

    for j in range(BLOCKS):
        wide = BL * (j + 1)
        radius = (BL * j + iota((1, BL), 1)).astype(F32)
        plane = (g * SLAB + iota((SLAB, BL), 0)).astype(F32)
        column = iota((wide, BL), 0).astype(F32)

        def extract(n, k, j=j, wide=wide, radius=radius, plane=plane, column=column):
            for i in range(2):
                b = 2 * k + i
                sine = sc[pl.ds(b, 1), :]
                cosine = sc[pl.ds(NB_DEV + b, 1), :]
                tx = column - radius * cosine
                fx = jnp.maximum(1.0 - tx * tx, 0.0)
                kx = jnp.concatenate([fx * fx, (tx * fx) * (radius * sine * (-4.0 / U))], 1)
                kx_high = kx.astype(BF16)
                kt[b, :wide, 2 * BL * j:2 * BL * (j + 1)] = kx_high
                kx_low = (kx - kx_high.astype(F32)).astype(BF16)
                tz = plane - (0.5 * NZ + radius * sine)
                fz = jnp.maximum(1.0 - tz * tz, 0.0)
                wz = fz * fz
                wd = (tz * fz) * (radius * cosine * (4.0 / U))
                kz[b, :, BL * j:BL * (j + 1)] = wz
                kzd[b, :, BL * j:BL * (j + 1)] = wd
                stacked = jnp.dot(vb[:, :wide], kx_high, preferred_element_type=F32)
                both = stacked[:R * SLAB] + stacked[R * SLAB:] + jnp.dot(
                    vb[:R * SLAB, :wide], kx_low, preferred_element_type=F32)
                for r in range(R):
                    direct = both[r * SLAB:(r + 1) * SLAB, :BL]
                    tilted = both[r * SLAB:(r + 1) * SLAB, BL:]
                    at = 2 * r + i
                    sp[n, at:at + 1, :] = jnp.sum(direct * wz, axis=0, keepdims=True)
                    sp[n, 8 + at:8 + at + 1, :] = jnp.sum(
                        direct * wd + tilted * wz, axis=0, keepdims=True)
            spb[n] = sp[n].astype(BF16)

        def unit(k, j=j, extract=extract):
            @pl.when(active(PAIRS * j + k, g))
            def _():
                extract(PAIRS * j + k, k)

        each(0, PAIRS, unit)

    def send_slices(n):
        @pl.when(active(n, g))
        def _():
            each(1, G, lambda i: gz_copy(
                spb.at[n], sp_in.at[n, g], rs_send.at[n], rs_recv.at[n, g], lax.rem(g + i, G)).start())
            sp_in[n, g] = spb[n]

    each(0, NU, send_slices)

    def pass_on(i):
        frm = lax.rem(zpos + far_first(i, D // 2), D // 2) * 2 + core
        dom_copy(w_all.at[frm], w_all.at[frm], w_recv.at[frm], w_recv.at[frm], sib).wait_recv()
        dom_copy(w_all.at[frm], w_all.at[frm], f_send, f_recv, sib).start()

    each(1, D // 2, pass_on)
    def gather_slices(n):
        def gather(frm, total):
            @pl.when(frm != g)
            def _():
                gz_copy(spb.at[n], sp_in.at[n, frm], rs_recv.at[n, frm], rs_recv.at[n, frm],
                        lax.rem(g + 1, G)).wait_recv()
            return total + sp_in[n, frm].astype(F32)

        total = lax.fori_loop(low[n], top[n] + 1, gather, jnp.zeros((16, BL), F32))
        j = lax.div(n, PAIRS)
        k = lax.rem(n, PAIRS)
        for m in range(8):
            for i in range(2):
                s_all[j, pl.ds(8 * m + 2 * k + i, 1), :] = total[2 * m + i:2 * m + i + 1]

    each(0, NU, gather_slices)

    def rows_of(kind, r):
        at = 32 * kind + 8 * r
        rounded = jnp.concatenate([s_all[j, at:at + 8, :] for j in range(BLOCKS)], 1)
        return rounded.astype(BF16).astype(F32)

    lead = [rows_of(0, r) for r in range(R)]
    slope = [rows_of(1, r) for r in range(R)]
    curve = jnp.concatenate([slope[y] * slope[y] + slope[y + 2] * slope[y + 2] for y in range(2)], 1)
    cross = jnp.concatenate([lead[y] * slope[y] + lead[y + 2] * slope[y + 2] for y in range(2)], 1)
    quad = jnp.concatenate([curve, cross], 0)
    quad_high = quad.astype(BF16)
    quad_low = (quad - quad_high.astype(F32)).astype(BF16)
    first = lax.dot_general(jnp.concatenate([quad_high, quad_low], 0), c2h[...], NT,
                            preferred_element_type=F32)
    tables = first[:16] + first[16:] + lax.dot_general(quad_high, c2l[...], NT,
                                                       preferred_element_type=F32)
    tables_high = tables.astype(BF16)
    tables_low = (tables - tables_high.astype(F32)).astype(BF16)
    lookup = jnp.concatenate([tables_high, tables_low], 0)[:, :NCTF]
    slope_rows = jnp.concatenate(slope, 1).astype(BF16)

    ids_in[d] = ids[...]
    others = ids_in.at[0:D - 1]
    dom_copy(others, others, i_recv, i_recv, sib).wait_recv()
    id_row = jnp.sum(ids_in[...], axis=0).astype(jnp.int32)
    bin_row = lax.div(id_row, NCTF)
    cls_rows = (iota((NCTF, ALLP), 0) == lax.rem(id_row, NCTF)).astype(F32).astype(BF16)
    looked = jnp.dot(lookup, cls_rows, preferred_element_type=F32)
    held = looked[0:8] + looked[16:24]
    crossed = looked[8:16] + looked[24:32]
    mask = (bin_of(iota((8, ALLP), 0)) == bin_row).astype(F32)
    power = jnp.sum(mask * held, axis=0, keepdims=True)
    cross_row = jnp.sum(mask * crossed, axis=0, keepdims=True)
    curvature = power + EPS
    slot = iota((16, ALLP), 0)
    sloped_row = lax.rem(lax.div(slot, 2), 2) == 1
    mask_rows = (2 * d + 2 * D * lax.div(slot, 4) + lax.rem(slot, 2) == bin_row).astype(F32)

    half = w_all.at[0:D // 2]
    dom_copy(half, half, f_recv, f_recv, sib).wait_recv()

    images = w_all[...].reshape(ALLP, WC)
    along = lax.dot_general(slope_rows, images, NT, preferred_element_type=F32)
    match = jnp.sum(mask * along, axis=0, keepdims=True) - cross_row
    shift = jnp.zeros_like(power)
    for _ in range(ITERS):
        shift = shift + 0.5 * (match - shift * power) / curvature
    pose_s[...] = shift * jnp.sqrt(curvature)
    spread = mask_rows * jnp.where(sloped_row, shift, 1.0)
    spread_high = spread.astype(BF16)
    spread_low = (spread - spread_high.astype(F32)).astype(BF16)
    sums = jnp.dot(jnp.concatenate([spread_high, spread_low], 0), images, preferred_element_type=F32)
    sums = sums[:16] + sums[16:]
    for n, (k, j) in enumerate(UNITS):
        for r in range(R):
            at = r * U + BL * j
            sf[n, 4 * r:4 * r + 4, :] = sums[4 * k:4 * k + 4, at:at + BL]
    ss[...] = sf[...].astype(BF16)

    def each_slab(n, act):
        def one(to):
            @pl.when(to != g)
            def _():
                act(gz_copy(ss.at[n], ss_in.at[n, g], rs2_send.at[n, to], rs2_recv.at[n], to))

        each(low[n], top[n] + 1, one)

    each(0, NU, lambda n: each_slab(NU - 1 - n, lambda copy: copy.start()))
    each(1, D, lambda i: dom_copy(pose_s, pose_in.at[d], p_send, p_recv, lax.rem(d + i, D)).start())

    acc[...] = jnp.zeros_like(acc)
    row = iota((256, R * SLAB), 0)
    within = lax.rem(row, 16)
    source = lax.rem(row, 4) * SLAB + 3 * lax.div(row, 16) + lax.div(within, 4)
    order = ((iota((256, R * SLAB), 1) == source) & (within < 12)).astype(F32).astype(BF16)

    for j in reversed(range(BLOCKS)):
        wide = BL * (j + 1)

        def spread_back(n, k, j=j, wide=wide):
            ss_in[n, g] = ss[n]
            others = ss_in.at[n, 0:G - 1]
            gz_copy(others, others, rs2_recv.at[n], rs2_recv.at[n], lax.rem(g + 1, G)).wait_recv()
            rows_t[...] = jnp.sum(ss_in[n].astype(F32), axis=0)
            for i in range(2):
                b = 2 * k + i
                wz = kz[b, :, BL * j:BL * (j + 1)]
                wd = kzd[b, :, BL * j:BL * (j + 1)]
                parts = []
                for r in range(R):
                    plain = rows_t[4 * r + i:4 * r + i + 1, :]
                    sloped = rows_t[4 * r + 2 + i:4 * r + 3 + i, :]
                    parts.append(jnp.concatenate([wz * plain + wd * sloped, wz * sloped], 1))
                left = jnp.concatenate(parts, 0)
                left_high = left.astype(BF16)
                left_low = (left - left_high.astype(F32)).astype(BF16)
                both = lax.dot_general(
                    jnp.concatenate([left_high, left_low], 0),
                    kt[b, :wide, 2 * BL * j:2 * BL * (j + 1)], NT, preferred_element_type=F32)
                acc[:, :wide] += both[:R * SLAB] + both[R * SLAB:]

        def unit(k, j=j, spread_back=spread_back):
            @pl.when(active(PAIRS * j + k, g))
            def _():
                spread_back(PAIRS * j + k, k)

        each(0, PAIRS, unit)

        ordered = jnp.dot(order, acc[:, BL * j:BL * (j + 1)].astype(BF16), preferred_element_type=F32)
        bk[j] = ordered.astype(BF16).reshape(D, 16, BL)
        def send_block(i, j=j):
            to = lax.rem(d + far_first(i, D), D)
            dom_copy(bk.at[j, to], bk_in.at[j, d], b_send.at[j], b_recv.at[j], to).start()

        each(1, D, send_block)

    pose_in[d] = pose_s[...]
    others = pose_in.at[0:D - 1]
    dom_copy(others, others, p_recv, p_recv, sib).wait_recv()
    pose = jnp.sum(pose_in[...], axis=0)
    lane = iota((8, ALLP), 1)
    kept = jnp.where(lax.div(lane, PART) == d, pose, 0.0)
    choose = (lax.rem(iota((ALLP, 128), 0), PART) == iota((ALLP, 128), 1)).astype(F32)
    picked = jnp.dot(kept, choose, precision=lax.Precision.HIGHEST, preferred_element_type=F32)
    pose_out[...] = picked[0:1, :PART]

    def finish(n):
        @pl.when(active(n, g))
        def _():
            sent = sp_in.at[n, 0:G - 1]
            gz_copy(sent, sent, rs_send.at[n], rs_send.at[n], lax.rem(g + 1, G)).wait_send()

        each_slab(n, lambda copy: copy.wait_send())

    each(0, NU, finish)
    sent = w_all.at[0:D // 2 - 1]
    dom_copy(sent, sent, w_send, w_send, sib).wait_send()
    dom_copy(half, half, f_send, f_send, sib).wait_send()
    sent = pose_in.at[0:D - 1]
    dom_copy(sent, sent, p_send, p_send, sib).wait_send()
    sent = ids_in.at[0:D - 1]
    dom_copy(sent, sent, i_send, i_send, sib).wait_send()

    for j in reversed(range(BLOCKS)):
        bk_in[j, d] = bk[j, d]
        others = bk_in.at[j, 0:D - 1]
        dom_copy(others, others, b_recv.at[j], b_recv.at[j], sib).wait_recv()
        total = jnp.sum(bk_in[j].astype(F32), axis=0)
        for k in range(3):
            back_out[k, :, BL * j:BL * (j + 1)] = total[4 * k:4 * k + 4]

    for j in range(BLOCKS):
        sent = bk_in.at[j, 0:D - 1]
        dom_copy(sent, sent, b_send.at[j], b_send.at[j], sib).wait_send()


def local(volume, observed, ctf_table, ctf_class, bin_ids):
    vmem = pl.BlockSpec(memory_space=pltpu.VMEM)
    hbm = pl.BlockSpec(memory_space=pltpu.HBM)
    dma = pltpu.SemaphoreType.DMA
    pose, back = pl.pallas_call(
        body,
        out_shape=(jax.ShapeDtypeStruct((1, PART), F32), jax.ShapeDtypeStruct((3, R, X), F32)),
        in_specs=[hbm] * 4,
        out_specs=(vmem, vmem),
        scratch_shapes=[
            pltpu.VMEM((SLAB, R, X), F32),
            pltpu.VMEM((PART, R, U), BF16),
            pltpu.VMEM((NCTF, 2, U), F32),
            pltpu.SMEM((PART,), jnp.int32),
            pltpu.SMEM((NU,), jnp.int32),
            pltpu.SMEM((NU,), jnp.int32),
            dma((4,)),
            pltpu.VMEM((2 * R * SLAB, X), BF16),
            pltpu.VMEM((NB_DEV, X, 2 * U), BF16),
            pltpu.VMEM((NB_DEV, SLAB, U), F32),
            pltpu.VMEM((NB_DEV, SLAB, U), F32),
            pltpu.VMEM((2 * NB_DEV, 128), F32),
            pltpu.VMEM((NU, 16, BL), F32),
            pltpu.VMEM((NU, 16, BL), BF16),
            pltpu.VMEM((NU, G, 16, BL), BF16),
            pltpu.VMEM((BLOCKS, 64, BL), F32),
            pltpu.VMEM((NU, 16, BL), F32),
            pltpu.VMEM((NU, 16, BL), BF16),
            pltpu.VMEM((NU, G, 16, BL), BF16),
            pltpu.VMEM((16, BL), F32),
            pltpu.VMEM((D, PART, WC), BF16),
            pltpu.VMEM((EXT, 2 * U), BF16),
            pltpu.VMEM((EXT, 2 * U), BF16),
            pltpu.VMEM((R * SLAB, X), F32),
            pltpu.VMEM((BLOCKS, D, 16, BL), BF16),
            pltpu.VMEM((BLOCKS, D, 16, BL), BF16),
            pltpu.VMEM((1, ALLP), F32),
            pltpu.VMEM((D, 1, ALLP), F32),
        ] + [
            pltpu.VMEM((1, ALLP), F32),
            pltpu.VMEM((D, 1, ALLP), F32),
            dma, dma((D,)), dma, dma, dma, dma,
            dma((NU,)), dma((NU, G)), dma((NU, G)), dma((NU,)),
            dma((BLOCKS,)), dma((BLOCKS,)), dma, dma,
        ],
        compiler_params=pltpu.CompilerParams(
            collective_id=0, has_side_effects=True, vmem_limit_bytes=55200 << 10),
        name="tilt_refine",
    )(volume, observed, ctf_table, NCTF * bin_ids + ctf_class)
    return (pose.reshape(PART), back)


def solution(mesh):
    return jax.shard_map(
        local,
        mesh=mesh,
        in_specs=(
            P("gz", None, None),
            P(("gz", "dom"), None, None),
            P(),
            P(("gz", "dom")),
            P(("gz", "dom")),
        ),
        out_specs=(P(("gz", "dom")), P(("gz", "dom"), None, None)),
        check_vma=False,
    )
```

```python
import math

import jax
import jax.numpy as jnp
from jax import lax
from jax.experimental import pallas as pl
from jax.experimental.pallas import tpu as pltpu
from jax.sharding import PartitionSpec as P

NZ = 768
NB = 128
NB_DEV = 8
NCTF = 32
ITERS = 3
EPS = 1e-05
G = 16
D = 16
SLAB = 48
R = 4
X = 384
U = 384
PART = 16
ALLP = PART * D
WC = R * U
EXT = 128
BLOCKS = 3
BL = 128
PAIRS = 4
UNITS = [(k, j) for j in range(BLOCKS) for k in range(PAIRS)]
F32 = jnp.float32
BF16 = jnp.bfloat16
NU = len(UNITS)
NT = (((1,), (1,)), ((), ()))


def slab_spans():
    spans = []
    for k, j in UNITS:
        row = []
        for dom in range(D):
            sines = [math.sin(-0.5 * math.pi + math.pi * (2 * (dom + D * k) + i + 0.5) / NB)
                     for i in range(2)]
            centres = [0.5 * NZ + u * sine for sine in sines for u in (j * BL, j * BL + BL - 1)]
            first = math.floor(min(centres) - 1e-3)
            last = math.floor(max(centres) + 1e-3) + 1
            row.append((max(first, 0) // SLAB, min(last, NZ - 1) // SLAB))
        spans.append(row)
    return spans


def iota(shape, dim):
    return lax.broadcasted_iota(jnp.int32, shape, dim)


def gz_copy(src, dst, send, recv, to):
    return pltpu.make_async_remote_copy(
        src_ref=src, dst_ref=dst, send_sem=send, recv_sem=recv,
        device_id={"gz": to}, device_id_type=pl.DeviceIdType.MESH)


def dom_copy(src, dst, send, recv, to):
    return pltpu.make_async_remote_copy(
        src_ref=src, dst_ref=dst, send_sem=send, recv_sem=recv,
        device_id={"dom": to}, device_id_type=pl.DeviceIdType.MESH)


def each(first, last, act):
    def one(i, carry):
        act(i)
        return carry

    lax.fori_loop(first, last, one, 0)


def far_first(i, n):
    return n // 2 + lax.div(i, 2) * (2 * lax.rem(i, 2) - 1)


def body(vol_hbm, obs_hbm, ctf_hbm, mark_hbm, pose_out, back_out,
         vol, obs, ctf, mark, low, top, in_sem, vb, kt, kz, kzd, sc, sp, spb, sp_in, s_all, sf, ss, ss_in, rows_t,
         w_all, c2h, c2l, acc, bk, bk_in, pose_s, pose_in,
         ids, ids_in, w_send, w_recv, f_send, f_recv, i_send, i_recv,
         rs_send, rs_recv, rs2_send, rs2_recv, b_send, b_recv, p_send, p_recv):
    g = lax.axis_index("gz")
    d = lax.axis_index("dom")
    core = lax.rem(d, 2)
    zpos = lax.div(d, 2)
    sib = d + 1 - 2 * core

    def bin_of(slot):
        return 2 * d + 2 * D * lax.div(slot, 2) + lax.rem(slot, 2)


    barrier = pltpu.get_barrier_semaphore()
    each(1, D, lambda i: pl.semaphore_signal(
        barrier, inc=1, device_id={"dom": lax.rem(d + i, D)}, device_id_type=pl.DeviceIdType.MESH))
    each(1, G, lambda i: pl.semaphore_signal(
        barrier, inc=1, device_id={"gz": lax.rem(g + i, G)}, device_id_type=pl.DeviceIdType.MESH))

    for n, row in enumerate(slab_spans()):
        least, most = jnp.int32(row[0][0]), jnp.int32(row[0][1])
        for k in range(1, D):
            least = jnp.where(d == k, row[k][0], least)
            most = jnp.where(d == k, row[k][1], most)
        low[n] = least
        top[n] = most

    def active(n, slab):
        return (low[n] <= slab) & (slab <= top[n])

    fetches = [pltpu.make_async_copy(src, dst, in_sem.at[k]) for k, (src, dst) in enumerate(
        ((mark_hbm, mark), (obs_hbm, obs), (ctf_hbm, ctf), (vol_hbm, vol)))]
    for fetch in fetches:
        fetch.start()
    for fetch in fetches[:3]:
        fetch.wait()

    rows = iota((PART, NCTF), 0)
    along_row = iota((1, ALLP), 1) - PART * d
    cls_col = jnp.zeros((PART, NCTF), jnp.int32)
    id_row = jnp.zeros((1, ALLP), jnp.int32)
    for i in range(PART):
        cls_col = jnp.where(rows == i, lax.rem(mark[i], NCTF), cls_col)
        id_row = jnp.where(along_row == i, mark[i], id_row)
    cls_hot = (cls_col == iota((PART, NCTF), 1)).astype(F32)
    ids[...] = id_row.astype(F32)
    table = jnp.concatenate([ctf[:, 0, :], ctf[:, 1, :]], 1)
    contrast = jnp.dot(cls_hot, table, precision=lax.Precision.HIGHEST,
                       preferred_element_type=F32)
    for r in range(R):
        y = r % 2
        image = obs[:, r, :].astype(F32)
        w_all[d, :, r * U:(r + 1) * U] = (image * contrast[:, y * U:(y + 1) * U]).astype(BF16)

    pl.semaphore_wait(barrier, (G - 1) + (D - 1))

    def device_at(step, on):
        return lax.rem(zpos + step, D // 2) * 2 + on

    def step_of(i):
        return D // 4 + lax.div(i + 1, 2) * (2 * lax.rem(i, 2) - 1)

    each(1, D // 2 - 1, lambda i: dom_copy(
        w_all.at[d], w_all.at[d], w_send, w_recv.at[d], device_at(step_of(i), core)).start())
    dom_copy(w_all.at[d], w_all.at[d], f_send, f_recv, sib).start()
    each(1, D, lambda i: dom_copy(ids, ids_in.at[d], i_send, i_recv, lax.rem(d + i, D)).start())

    square = table * table
    high = square.astype(BF16)
    c2h[...] = jnp.zeros_like(c2h)
    c2l[...] = jnp.zeros_like(c2l)
    c2h[:NCTF, :] = high
    c2l[:NCTF, :] = (square - high.astype(F32)).astype(BF16)

    fetches[3].wait()
    def split_planes(part):
        for r in range(R):
            plane_rows = vol[pl.ds(16 * part, 16), r, :]
            coarse = plane_rows.astype(BF16)
            at = pl.multiple_of(r * SLAB + 16 * part, 16)
            vb[pl.ds(at, 16), :] = coarse
            vb[pl.ds(R * SLAB + at, 16), :] = (plane_rows - coarse.astype(F32)).astype(BF16)

    each(0, SLAB // 16, split_planes)
    bin_index = bin_of(iota((NB_DEV, 128), 0)).astype(F32)
    theta = -0.5 * math.pi + math.pi * (bin_index + 0.5) / NB
    sc[:NB_DEV, :] = jnp.sin(theta)
    sc[NB_DEV:, :] = jnp.cos(theta)

    for j in range(BLOCKS):
        wide = BL * (j + 1)
        radius = (BL * j + iota((1, BL), 1)).astype(F32)
        plane = (g * SLAB + iota((SLAB, BL), 0)).astype(F32)
        column = iota((wide, BL), 0).astype(F32)

        def extract(n, k, j=j, wide=wide, radius=radius, plane=plane, column=column):
            for i in range(2):
                b = 2 * k + i
                sine = sc[pl.ds(b, 1), :]
                cosine = sc[pl.ds(NB_DEV + b, 1), :]
                tx = column - radius * cosine
                fx = jnp.maximum(1.0 - tx * tx, 0.0)
                kx = jnp.concatenate([fx * fx, (tx * fx) * (radius * sine * (-4.0 / U))], 1)
                kx_high = kx.astype(BF16)
                kt[b, :wide, 2 * BL * j:2 * BL * (j + 1)] = kx_high
                kx_low = (kx - kx_high.astype(F32)).astype(BF16)
                tz = plane - (0.5 * NZ + radius * sine)
                fz = jnp.maximum(1.0 - tz * tz, 0.0)
                wz = fz * fz
                wd = (tz * fz) * (radius * cosine * (4.0 / U))
                kz[b, :, BL * j:BL * (j + 1)] = wz
                kzd[b, :, BL * j:BL * (j + 1)] = wd
                stacked = jnp.dot(vb[:, :wide], kx_high, preferred_element_type=F32)
                both = stacked[:R * SLAB] + stacked[R * SLAB:] + jnp.dot(
                    vb[:R * SLAB, :wide], kx_low, preferred_element_type=F32)
                for r in range(R):
                    direct = both[r * SLAB:(r + 1) * SLAB, :BL]
                    tilted = both[r * SLAB:(r + 1) * SLAB, BL:]
                    at = 2 * r + i
                    sp[n, at:at + 1, :] = jnp.sum(direct * wz, axis=0, keepdims=True)
                    sp[n, 8 + at:8 + at + 1, :] = jnp.sum(
                        direct * wd + tilted * wz, axis=0, keepdims=True)
            spb[n] = sp[n].astype(BF16)

        def unit(k, j=j, extract=extract):
            @pl.when(active(PAIRS * j + k, g))
            def _():
                extract(PAIRS * j + k, k)

        each(0, PAIRS, unit)

    def send_slices(n):
        @pl.when(active(n, g))
        def _():
            each(1, G, lambda i: gz_copy(
                spb.at[n], sp_in.at[n, g], rs_send.at[n], rs_recv.at[n, g], lax.rem(g + i, G)).start())
            sp_in[n, g] = spb[n]

    each(0, NU, send_slices)

    def pass_on(i, relay=None):
        frm = device_at(step_of(i), core)
        block = w_all.at[frm]
        dom_copy(block, block, w_recv.at[frm], w_recv.at[frm], sib).wait_recv()
        if relay is not None:
            dom_copy(block, block, w_send, w_recv.at[frm], relay).start()
        dom_copy(block, block, f_send, f_recv, sib).start()

    pass_on(jnp.int32(1), device_at(1, core))
    pass_on(jnp.int32(2), device_at(D // 2 - 1, 1 - core))
    each(3, D // 2 - 1, pass_on)

    def gather_slices(n):
        def gather(frm, total):
            @pl.when(frm != g)
            def _():
                gz_copy(spb.at[n], sp_in.at[n, frm], rs_recv.at[n, frm], rs_recv.at[n, frm],
                        lax.rem(g + 1, G)).wait_recv()
            return total + sp_in[n, frm].astype(F32)

        total = lax.fori_loop(low[n], top[n] + 1, gather, jnp.zeros((16, BL), F32))
        j = lax.div(n, PAIRS)
        k = lax.rem(n, PAIRS)
        for m in range(8):
            for i in range(2):
                s_all[j, pl.ds(8 * m + 2 * k + i, 1), :] = total[2 * m + i:2 * m + i + 1]

    each(0, NU, gather_slices)

    def rows_of(kind, r):
        at = 32 * kind + 8 * r
        rounded = jnp.concatenate([s_all[j, at:at + 8, :] for j in range(BLOCKS)], 1)
        return rounded.astype(BF16).astype(F32)

    lead = [rows_of(0, r) for r in range(R)]
    slope = [rows_of(1, r) for r in range(R)]
    curve = jnp.concatenate([slope[y] * slope[y] + slope[y + 2] * slope[y + 2] for y in range(2)], 1)
    cross = jnp.concatenate([lead[y] * slope[y] + lead[y + 2] * slope[y + 2] for y in range(2)], 1)
    quad = jnp.concatenate([curve, cross], 0)
    quad_high = quad.astype(BF16)
    quad_low = (quad - quad_high.astype(F32)).astype(BF16)
    first = lax.dot_general(jnp.concatenate([quad_high, quad_low], 0), c2h[...], NT,
                            preferred_element_type=F32)
    tables = first[:16] + first[16:] + lax.dot_general(quad_high, c2l[...], NT,
                                                       preferred_element_type=F32)
    tables_high = tables.astype(BF16)
    tables_low = (tables - tables_high.astype(F32)).astype(BF16)
    lookup = jnp.concatenate([tables_high, tables_low], 0)[:, :NCTF]
    slope_rows = jnp.concatenate(slope, 1).astype(BF16)

    ids_in[d] = ids[...]
    others = ids_in.at[0:D - 1]
    dom_copy(others, others, i_recv, i_recv, sib).wait_recv()
    id_row = jnp.sum(ids_in[...], axis=0).astype(jnp.int32)
    bin_row = lax.div(id_row, NCTF)
    cls_rows = (iota((NCTF, ALLP), 0) == lax.rem(id_row, NCTF)).astype(F32).astype(BF16)
    looked = jnp.dot(lookup, cls_rows, preferred_element_type=F32)
    held = looked[0:8] + looked[16:24]
    crossed = looked[8:16] + looked[24:32]
    mask = (bin_of(iota((8, ALLP), 0)) == bin_row).astype(F32)
    power = jnp.sum(mask * held, axis=0, keepdims=True)
    cross_row = jnp.sum(mask * crossed, axis=0, keepdims=True)
    curvature = power + EPS
    slot = iota((16, ALLP), 0)
    sloped_row = lax.rem(lax.div(slot, 2), 2) == 1
    mask_rows = (2 * d + 2 * D * lax.div(slot, 4) + lax.rem(slot, 2) == bin_row).astype(F32)

    for on in (core, 1 - core):
        frm = device_at(D // 4, on)
        block = w_all.at[frm]
        dom_copy(block, block, w_recv.at[frm], w_recv.at[frm], sib).wait_recv()
    passed = w_all.at[0:D // 2 - 1]
    dom_copy(passed, passed, f_recv, f_recv, sib).wait_recv()

    images = w_all[...].reshape(ALLP, WC)
    along = lax.dot_general(slope_rows, images, NT, preferred_element_type=F32)
    match = jnp.sum(mask * along, axis=0, keepdims=True) - cross_row
    shift = jnp.zeros_like(power)
    for _ in range(ITERS):
        shift = shift + 0.5 * (match - shift * power) / curvature
    pose_s[...] = shift * jnp.sqrt(curvature)
    spread = mask_rows * jnp.where(sloped_row, shift, 1.0)
    spread_high = spread.astype(BF16)
    spread_low = (spread - spread_high.astype(F32)).astype(BF16)
    sums = jnp.dot(jnp.concatenate([spread_high, spread_low], 0), images, preferred_element_type=F32)
    sums = sums[:16] + sums[16:]
    for n, (k, j) in enumerate(UNITS):
        for r in range(R):
            at = r * U + BL * j
            sf[n, 4 * r:4 * r + 4, :] = sums[4 * k:4 * k + 4, at:at + BL]
    ss[...] = sf[...].astype(BF16)

    def each_slab(n, act):
        def one(to):
            @pl.when(to != g)
            def _():
                act(gz_copy(ss.at[n], ss_in.at[n, g], rs2_send.at[n, to], rs2_recv.at[n], to))

        each(low[n], top[n] + 1, one)

    each(0, NU, lambda n: each_slab(NU - 1 - n, lambda copy: copy.start()))
    each(1, D, lambda i: dom_copy(pose_s, pose_in.at[d], p_send, p_recv, lax.rem(d + i, D)).start())

    acc[...] = jnp.zeros_like(acc)
    row = iota((256, R * SLAB), 0)
    within = lax.rem(row, 16)
    source = lax.rem(row, 4) * SLAB + 3 * lax.div(row, 16) + lax.div(within, 4)
    order = ((iota((256, R * SLAB), 1) == source) & (within < 12)).astype(F32).astype(BF16)

    for j in reversed(range(BLOCKS)):
        wide = BL * (j + 1)

        def spread_back(n, k, j=j, wide=wide):
            ss_in[n, g] = ss[n]
            others = ss_in.at[n, 0:G - 1]
            gz_copy(others, others, rs2_recv.at[n], rs2_recv.at[n], lax.rem(g + 1, G)).wait_recv()
            rows_t[...] = jnp.sum(ss_in[n].astype(F32), axis=0)
            for i in range(2):
                b = 2 * k + i
                wz = kz[b, :, BL * j:BL * (j + 1)]
                wd = kzd[b, :, BL * j:BL * (j + 1)]
                parts = []
                for r in range(R):
                    plain = rows_t[4 * r + i:4 * r + i + 1, :]
                    sloped = rows_t[4 * r + 2 + i:4 * r + 3 + i, :]
                    parts.append(jnp.concatenate([wz * plain + wd * sloped, wz * sloped], 1))
                left = jnp.concatenate(parts, 0)
                left_high = left.astype(BF16)
                left_low = (left - left_high.astype(F32)).astype(BF16)
                both = lax.dot_general(
                    jnp.concatenate([left_high, left_low], 0),
                    kt[b, :wide, 2 * BL * j:2 * BL * (j + 1)], NT, preferred_element_type=F32)
                acc[:, :wide] += both[:R * SLAB] + both[R * SLAB:]

        def unit(k, j=j, spread_back=spread_back):
            @pl.when(active(PAIRS * j + k, g))
            def _():
                spread_back(PAIRS * j + k, k)

        each(0, PAIRS, unit)

        ordered = jnp.dot(order, acc[:, BL * j:BL * (j + 1)].astype(BF16), preferred_element_type=F32)
        bk[j] = ordered.astype(BF16).reshape(D, 16, BL)
        def send_block(i, j=j):
            to = lax.rem(d + far_first(i, D), D)
            dom_copy(bk.at[j, to], bk_in.at[j, d], b_send.at[j], b_recv.at[j], to).start()

        each(1, D, send_block)

    pose_in[d] = pose_s[...]
    others = pose_in.at[0:D - 1]
    dom_copy(others, others, p_recv, p_recv, sib).wait_recv()
    pose = jnp.sum(pose_in[...], axis=0)
    lane = iota((8, ALLP), 1)
    kept = jnp.where(lax.div(lane, PART) == d, pose, 0.0)
    choose = (lax.rem(iota((ALLP, 128), 0), PART) == iota((ALLP, 128), 1)).astype(F32)
    picked = jnp.dot(kept, choose, precision=lax.Precision.HIGHEST, preferred_element_type=F32)
    pose_out[...] = picked[0:1, :PART]

    def finish(n):
        @pl.when(active(n, g))
        def _():
            sent = sp_in.at[n, 0:G - 1]
            gz_copy(sent, sent, rs_send.at[n], rs_send.at[n], lax.rem(g + 1, G)).wait_send()

        each_slab(n, lambda copy: copy.wait_send())

    each(0, NU, finish)
    sent = w_all.at[0:D // 2]
    dom_copy(sent, sent, w_send, w_send, sib).wait_send()
    dom_copy(passed, passed, f_send, f_send, sib).wait_send()
    sent = pose_in.at[0:D - 1]
    dom_copy(sent, sent, p_send, p_send, sib).wait_send()
    sent = ids_in.at[0:D - 1]
    dom_copy(sent, sent, i_send, i_send, sib).wait_send()

    for j in reversed(range(BLOCKS)):
        bk_in[j, d] = bk[j, d]
        others = bk_in.at[j, 0:D - 1]
        dom_copy(others, others, b_recv.at[j], b_recv.at[j], sib).wait_recv()
        total = jnp.sum(bk_in[j].astype(F32), axis=0)
        for k in range(3):
            back_out[k, :, BL * j:BL * (j + 1)] = total[4 * k:4 * k + 4]

    for j in range(BLOCKS):
        sent = bk_in.at[j, 0:D - 1]
        dom_copy(sent, sent, b_send.at[j], b_send.at[j], sib).wait_send()


def local(volume, observed, ctf_table, ctf_class, bin_ids):
    vmem = pl.BlockSpec(memory_space=pltpu.VMEM)
    hbm = pl.BlockSpec(memory_space=pltpu.HBM)
    dma = pltpu.SemaphoreType.DMA
    pose, back = pl.pallas_call(
        body,
        out_shape=(jax.ShapeDtypeStruct((1, PART), F32), jax.ShapeDtypeStruct((3, R, X), F32)),
        in_specs=[hbm] * 4,
        out_specs=(vmem, vmem),
        scratch_shapes=[
            pltpu.VMEM((SLAB, R, X), F32),
            pltpu.VMEM((PART, R, U), BF16),
            pltpu.VMEM((NCTF, 2, U), F32),
            pltpu.SMEM((PART,), jnp.int32),
            pltpu.SMEM((NU,), jnp.int32),
            pltpu.SMEM((NU,), jnp.int32),
            dma((4,)),
            pltpu.VMEM((2 * R * SLAB, X), BF16),
            pltpu.VMEM((NB_DEV, X, 2 * U), BF16),
            pltpu.VMEM((NB_DEV, SLAB, U), F32),
            pltpu.VMEM((NB_DEV, SLAB, U), F32),
            pltpu.VMEM((2 * NB_DEV, 128), F32),
            pltpu.VMEM((NU, 16, BL), F32),
            pltpu.VMEM((NU, 16, BL), BF16),
            pltpu.VMEM((NU, G, 16, BL), BF16),
            pltpu.VMEM((BLOCKS, 64, BL), F32),
            pltpu.VMEM((NU, 16, BL), F32),
            pltpu.VMEM((NU, 16, BL), BF16),
            pltpu.VMEM((NU, G, 16, BL), BF16),
            pltpu.VMEM((16, BL), F32),
            pltpu.VMEM((D, PART, WC), BF16),
            pltpu.VMEM((EXT, 2 * U), BF16),
            pltpu.VMEM((EXT, 2 * U), BF16),
            pltpu.VMEM((R * SLAB, X), F32),
            pltpu.VMEM((BLOCKS, D, 16, BL), BF16),
            pltpu.VMEM((BLOCKS, D, 16, BL), BF16),
            pltpu.VMEM((1, ALLP), F32),
            pltpu.VMEM((D, 1, ALLP), F32),
        ] + [
            pltpu.VMEM((1, ALLP), F32),
            pltpu.VMEM((D, 1, ALLP), F32),
            dma, dma((D,)), dma, dma, dma, dma,
            dma((NU,)), dma((NU, G)), dma((NU, G)), dma((NU,)),
            dma((BLOCKS,)), dma((BLOCKS,)), dma, dma,
        ],
        compiler_params=pltpu.CompilerParams(
            collective_id=0, has_side_effects=True, vmem_limit_bytes=55200 << 10),
        name="tilt_refine",
    )(volume, observed, ctf_table, NCTF * bin_ids + ctf_class)
    return (pose.reshape(PART), back)


def solution(mesh):
    return jax.shard_map(
        local,
        mesh=mesh,
        in_specs=(
            P("gz", None, None),
            P(("gz", "dom"), None, None),
            P(),
            P(("gz", "dom")),
            P(("gz", "dom")),
        ),
        out_specs=(P(("gz", "dom")), P(("gz", "dom"), None, None)),
        check_vma=False,
    )
```

```python
import math

import jax
import jax.numpy as jnp
from jax import lax
from jax.experimental import pallas as pl
from jax.experimental.pallas import tpu as pltpu
from jax.sharding import PartitionSpec as P

NZ = 768
NB = 128
NB_DEV = 8
NCTF = 32
ITERS = 3
EPS = 1e-05
G = 16
D = 16
SLAB = 48
R = 4
X = 384
U = 384
PART = 16
ALLP = PART * D
WC = R * U
EXT = 128
BLOCKS = 3
BL = 128
PAIRS = 4
UNITS = [(k, j) for j in range(BLOCKS) for k in range(PAIRS)]
F32 = jnp.float32
BF16 = jnp.bfloat16
NU = len(UNITS)
NT = (((1,), (1,)), ((), ()))


def slab_spans():
    spans = []
    for k, j in UNITS:
        row = []
        for dom in range(D):
            sines = [math.sin(-0.5 * math.pi + math.pi * (2 * (dom + D * k) + i + 0.5) / NB)
                     for i in range(2)]
            centres = [0.5 * NZ + u * sine for sine in sines for u in (j * BL, j * BL + BL - 1)]
            first = math.floor(min(centres) - 1e-3)
            last = math.floor(max(centres) + 1e-3) + 1
            row.append((max(first, 0) // SLAB, min(last, NZ - 1) // SLAB))
        spans.append(row)
    return spans


def iota(shape, dim):
    return lax.broadcasted_iota(jnp.int32, shape, dim)


def gz_copy(src, dst, send, recv, to):
    return pltpu.make_async_remote_copy(
        src_ref=src, dst_ref=dst, send_sem=send, recv_sem=recv,
        device_id={"gz": to}, device_id_type=pl.DeviceIdType.MESH)


def dom_copy(src, dst, send, recv, to):
    return pltpu.make_async_remote_copy(
        src_ref=src, dst_ref=dst, send_sem=send, recv_sem=recv,
        device_id={"dom": to}, device_id_type=pl.DeviceIdType.MESH)


def each(first, last, act):
    def one(i, carry):
        act(i)
        return carry

    lax.fori_loop(first, last, one, 0)


def far_first(i, n):
    return n // 2 + lax.div(i, 2) * (2 * lax.rem(i, 2) - 1)


def body(vol_hbm, obs_hbm, ctf_hbm, mark_hbm, pose_out, back_out,
         vol, obs, ctf, mark, low, top, in_sem, vb, kt, kz, kzd, sc, sp, spb, sp_in, s_all, sf, ss, ss_in, rows_t,
         w_all, c2h, c2l, acc, bk, bk_in, pose_s, pose_in,
         ids, ids_in, w_send, w_recv, f_send, f_recv, i_send, i_recv,
         rs_send, rs_recv, rs2_send, rs2_recv, b_send, b_recv, p_send, p_recv):
    g = lax.axis_index("gz")
    d = lax.axis_index("dom")
    core = lax.rem(d, 2)
    zpos = lax.div(d, 2)
    sib = d + 1 - 2 * core

    def bin_of(slot):
        return 2 * d + 2 * D * lax.div(slot, 2) + lax.rem(slot, 2)


    barrier = pltpu.get_barrier_semaphore()
    each(1, D, lambda i: pl.semaphore_signal(
        barrier, inc=1, device_id={"dom": lax.rem(d + far_first(i, D), D)}, device_id_type=pl.DeviceIdType.MESH))
    each(1, G, lambda i: pl.semaphore_signal(
        barrier, inc=1, device_id={"gz": lax.rem(g + i, G)}, device_id_type=pl.DeviceIdType.MESH))

    for n, row in enumerate(slab_spans()):
        least, most = jnp.int32(row[0][0]), jnp.int32(row[0][1])
        for k in range(1, D):
            least = jnp.where(d == k, row[k][0], least)
            most = jnp.where(d == k, row[k][1], most)
        low[n] = least
        top[n] = most

    def active(n, slab):
        return (low[n] <= slab) & (slab <= top[n])

    fetches = [pltpu.make_async_copy(src, dst, in_sem.at[k]) for k, (src, dst) in enumerate(
        ((mark_hbm, mark), (obs_hbm, obs), (ctf_hbm, ctf), (vol_hbm, vol)))]
    for fetch in fetches:
        fetch.start()
    for fetch in fetches[:3]:
        fetch.wait()

    rows = iota((PART, NCTF), 0)
    along_row = iota((1, ALLP), 1) - PART * d
    cls_col = jnp.zeros((PART, NCTF), jnp.int32)
    id_row = jnp.zeros((1, ALLP), jnp.int32)
    for i in range(PART):
        cls_col = jnp.where(rows == i, lax.rem(mark[i], NCTF), cls_col)
        id_row = jnp.where(along_row == i, mark[i], id_row)
    cls_hot = (cls_col == iota((PART, NCTF), 1)).astype(F32)
    ids[...] = id_row.astype(F32)
    table = jnp.concatenate([ctf[:, 0, :], ctf[:, 1, :]], 1)
    contrast = jnp.dot(cls_hot, table, precision=lax.Precision.HIGHEST,
                       preferred_element_type=F32)
    for r in range(R):
        y = r % 2
        image = obs[:, r, :].astype(F32)
        w_all[d, :, r * U:(r + 1) * U] = (image * contrast[:, y * U:(y + 1) * U]).astype(BF16)

    pl.semaphore_wait(barrier, (G - 1) + (D - 1))

    def device_at(step, on):
        return lax.rem(zpos + step, D // 2) * 2 + on

    def step_of(i):
        return D // 4 + lax.div(i + 1, 2) * (2 * lax.rem(i, 2) - 1)

    each(1, D // 2 - 1, lambda i: dom_copy(
        w_all.at[d], w_all.at[d], w_send, w_recv.at[d], device_at(step_of(i), core)).start())
    dom_copy(w_all.at[d], w_all.at[d], f_send, f_recv, sib).start()
    each(1, D, lambda i: dom_copy(ids, ids_in.at[d], i_send, i_recv, lax.rem(d + i, D)).start())

    square = table * table
    high = square.astype(BF16)
    c2h[...] = jnp.zeros_like(c2h)
    c2l[...] = jnp.zeros_like(c2l)
    c2h[:NCTF, :] = high
    c2l[:NCTF, :] = (square - high.astype(F32)).astype(BF16)

    fetches[3].wait()
    def split_planes(part):
        for r in range(R):
            plane_rows = vol[pl.ds(16 * part, 16), r, :]
            coarse = plane_rows.astype(BF16)
            at = pl.multiple_of(r * SLAB + 16 * part, 16)
            vb[pl.ds(at, 16), :] = coarse
            vb[pl.ds(R * SLAB + at, 16), :] = (plane_rows - coarse.astype(F32)).astype(BF16)

    each(0, SLAB // 16, split_planes)
    bin_index = bin_of(iota((NB_DEV, 128), 0)).astype(F32)
    theta = -0.5 * math.pi + math.pi * (bin_index + 0.5) / NB
    sc[:NB_DEV, :] = jnp.sin(theta)
    sc[NB_DEV:, :] = jnp.cos(theta)

    for j in reversed(range(BLOCKS)):
        wide = BL * (j + 1)
        radius = (BL * j + iota((1, BL), 1)).astype(F32)
        plane = (g * SLAB + iota((SLAB, BL), 0)).astype(F32)
        column = iota((wide, BL), 0).astype(F32)

        def extract(n, k, j=j, wide=wide, radius=radius, plane=plane, column=column):
            for i in range(2):
                b = 2 * k + i
                sine = sc[pl.ds(b, 1), :]
                cosine = sc[pl.ds(NB_DEV + b, 1), :]
                tx = column - radius * cosine
                fx = jnp.maximum(1.0 - tx * tx, 0.0)
                kx = jnp.concatenate([fx * fx, (tx * fx) * (radius * sine * (-4.0 / U))], 1)
                kx_high = kx.astype(BF16)
                kt[b, :wide, 2 * BL * j:2 * BL * (j + 1)] = kx_high
                kx_low = (kx - kx_high.astype(F32)).astype(BF16)
                tz = plane - (0.5 * NZ + radius * sine)
                fz = jnp.maximum(1.0 - tz * tz, 0.0)
                wz = fz * fz
                wd = (tz * fz) * (radius * cosine * (4.0 / U))
                kz[b, :, BL * j:BL * (j + 1)] = wz
                kzd[b, :, BL * j:BL * (j + 1)] = wd
                stacked = jnp.dot(vb[:, :wide], kx_high, preferred_element_type=F32)
                both = stacked[:R * SLAB] + stacked[R * SLAB:] + jnp.dot(
                    vb[:R * SLAB, :wide], kx_low, preferred_element_type=F32)
                for r in range(R):
                    direct = both[r * SLAB:(r + 1) * SLAB, :BL]
                    tilted = both[r * SLAB:(r + 1) * SLAB, BL:]
                    at = 2 * r + i
                    sp[n, at:at + 1, :] = jnp.sum(direct * wz, axis=0, keepdims=True)
                    sp[n, 8 + at:8 + at + 1, :] = jnp.sum(
                        direct * wd + tilted * wz, axis=0, keepdims=True)
            spb[n] = sp[n].astype(BF16)

        def unit(k, j=j, extract=extract):
            n = PAIRS * j + k

            @pl.when(active(n, g))
            def _():
                extract(n, k)
                each(1, G, lambda i: gz_copy(
                    spb.at[n], sp_in.at[n, g], rs_send.at[n], rs_recv.at[n, g], lax.rem(g + i, G)).start())
                sp_in[n, g] = spb[n]

        each(0, PAIRS, unit)

    def pass_on(i, relay=None):
        frm = device_at(step_of(i), core)
        block = w_all.at[frm]
        dom_copy(block, block, w_recv.at[frm], w_recv.at[frm], sib).wait_recv()
        if relay is not None:
            dom_copy(block, block, w_send, w_recv.at[frm], relay).start()
        dom_copy(block, block, f_send, f_recv, sib).start()

    pass_on(jnp.int32(1), device_at(1, core))
    pass_on(jnp.int32(2), device_at(D // 2 - 1, 1 - core))
    each(3, D // 2 - 1, pass_on)

    def gather_slices(n):
        def gather(frm, total):
            @pl.when(frm != g)
            def _():
                gz_copy(spb.at[n], sp_in.at[n, frm], rs_recv.at[n, frm], rs_recv.at[n, frm],
                        lax.rem(g + 1, G)).wait_recv()
            return total + sp_in[n, frm].astype(F32)

        total = lax.fori_loop(low[n], top[n] + 1, gather, jnp.zeros((16, BL), F32))
        j = lax.div(n, PAIRS)
        k = lax.rem(n, PAIRS)
        for m in range(8):
            for i in range(2):
                s_all[j, pl.ds(8 * m + 2 * k + i, 1), :] = total[2 * m + i:2 * m + i + 1]

    each(0, NU, gather_slices)

    def rows_of(kind, r):
        at = 32 * kind + 8 * r
        rounded = jnp.concatenate([s_all[j, at:at + 8, :] for j in range(BLOCKS)], 1)
        return rounded.astype(BF16).astype(F32)

    lead = [rows_of(0, r) for r in range(R)]
    slope = [rows_of(1, r) for r in range(R)]
    curve = jnp.concatenate([slope[y] * slope[y] + slope[y + 2] * slope[y + 2] for y in range(2)], 1)
    cross = jnp.concatenate([lead[y] * slope[y] + lead[y + 2] * slope[y + 2] for y in range(2)], 1)
    quad = jnp.concatenate([curve, cross], 0)
    quad_high = quad.astype(BF16)
    quad_low = (quad - quad_high.astype(F32)).astype(BF16)
    first = lax.dot_general(jnp.concatenate([quad_high, quad_low], 0), c2h[...], NT,
                            preferred_element_type=F32)
    tables = first[:16] + first[16:] + lax.dot_general(quad_high, c2l[...], NT,
                                                       preferred_element_type=F32)
    tables_high = tables.astype(BF16)
    tables_low = (tables - tables_high.astype(F32)).astype(BF16)
    lookup = jnp.concatenate([tables_high, tables_low], 0)[:, :NCTF]
    slope_rows = jnp.concatenate(slope, 1).astype(BF16)

    ids_in[d] = ids[...]
    others = ids_in.at[0:D - 1]
    dom_copy(others, others, i_recv, i_recv, sib).wait_recv()
    id_row = jnp.sum(ids_in[...], axis=0).astype(jnp.int32)
    bin_row = lax.div(id_row, NCTF)
    cls_rows = (iota((NCTF, ALLP), 0) == lax.rem(id_row, NCTF)).astype(F32).astype(BF16)
    looked = jnp.dot(lookup, cls_rows, preferred_element_type=F32)
    held = looked[0:8] + looked[16:24]
    crossed = looked[8:16] + looked[24:32]
    mask = (bin_of(iota((8, ALLP), 0)) == bin_row).astype(F32)
    power = jnp.sum(mask * held, axis=0, keepdims=True)
    cross_row = jnp.sum(mask * crossed, axis=0, keepdims=True)
    curvature = power + EPS
    slot = iota((16, ALLP), 0)
    sloped_row = lax.rem(lax.div(slot, 2), 2) == 1
    mask_rows = (2 * d + 2 * D * lax.div(slot, 4) + lax.rem(slot, 2) == bin_row).astype(F32)

    for on in (core, 1 - core):
        frm = device_at(D // 4, on)
        block = w_all.at[frm]
        dom_copy(block, block, w_recv.at[frm], w_recv.at[frm], sib).wait_recv()
    passed = w_all.at[0:D // 2 - 1]
    dom_copy(passed, passed, f_recv, f_recv, sib).wait_recv()

    images = w_all[...].reshape(ALLP, WC)
    along = lax.dot_general(slope_rows, images, NT, preferred_element_type=F32)
    match = jnp.sum(mask * along, axis=0, keepdims=True) - cross_row
    shift = jnp.zeros_like(power)
    for _ in range(ITERS):
        shift = shift + 0.5 * (match - shift * power) / curvature
    pose_s[...] = shift * jnp.sqrt(curvature)
    spread = mask_rows * jnp.where(sloped_row, shift, 1.0)
    spread_high = spread.astype(BF16)
    spread_low = (spread - spread_high.astype(F32)).astype(BF16)
    sums = jnp.dot(jnp.concatenate([spread_high, spread_low], 0), images, preferred_element_type=F32)
    sums = sums[:16] + sums[16:]
    for n, (k, j) in enumerate(UNITS):
        for r in range(R):
            at = r * U + BL * j
            sf[n, 4 * r:4 * r + 4, :] = sums[4 * k:4 * k + 4, at:at + BL]
    ss[...] = sf[...].astype(BF16)

    def each_slab(n, act):
        def one(to):
            @pl.when(to != g)
            def _():
                act(gz_copy(ss.at[n], ss_in.at[n, g], rs2_send.at[n, to], rs2_recv.at[n], to))

        each(low[n], top[n] + 1, one)

    each(0, NU, lambda n: each_slab(NU - 1 - n, lambda copy: copy.start()))
    each(1, D, lambda i: dom_copy(pose_s, pose_in.at[d], p_send, p_recv, lax.rem(d + i, D)).start())

    acc[...] = jnp.zeros_like(acc)
    row = iota((256, R * SLAB), 0)
    within = lax.rem(row, 16)
    source = lax.rem(row, 4) * SLAB + 3 * lax.div(row, 16) + lax.div(within, 4)
    order = ((iota((256, R * SLAB), 1) == source) & (within < 12)).astype(F32).astype(BF16)

    for j in reversed(range(BLOCKS)):
        wide = BL * (j + 1)

        def spread_back(n, k, j=j, wide=wide):
            ss_in[n, g] = ss[n]
            others = ss_in.at[n, 0:G - 1]
            gz_copy(others, others, rs2_recv.at[n], rs2_recv.at[n], lax.rem(g + 1, G)).wait_recv()
            rows_t[...] = jnp.sum(ss_in[n].astype(F32), axis=0)
            for i in range(2):
                b = 2 * k + i
                wz = kz[b, :, BL * j:BL * (j + 1)]
                wd = kzd[b, :, BL * j:BL * (j + 1)]
                parts = []
                for r in range(R):
                    plain = rows_t[4 * r + i:4 * r + i + 1, :]
                    sloped = rows_t[4 * r + 2 + i:4 * r + 3 + i, :]
                    parts.append(jnp.concatenate([wz * plain + wd * sloped, wz * sloped], 1))
                left = jnp.concatenate(parts, 0)
                left_high = left.astype(BF16)
                left_low = (left - left_high.astype(F32)).astype(BF16)
                both = lax.dot_general(
                    jnp.concatenate([left_high, left_low], 0),
                    kt[b, :wide, 2 * BL * j:2 * BL * (j + 1)], NT, preferred_element_type=F32)
                acc[:, :wide] += both[:R * SLAB] + both[R * SLAB:]

        def unit(k, j=j, spread_back=spread_back):
            @pl.when(active(PAIRS * j + k, g))
            def _():
                spread_back(PAIRS * j + k, k)

        each(0, PAIRS, unit)

        ordered = jnp.dot(order, acc[:, BL * j:BL * (j + 1)].astype(BF16), preferred_element_type=F32)
        bk[j] = ordered.astype(BF16).reshape(D, 16, BL)
        def send_block(i, j=j):
            to = lax.rem(d + far_first(i, D), D)
            dom_copy(bk.at[j, to, 0:12], bk_in.at[j, d, 0:12], b_send.at[j], b_recv.at[j], to).start()

        each(1, D, send_block)

    pose_in[d] = pose_s[...]
    others = pose_in.at[0:D - 1]
    dom_copy(others, others, p_recv, p_recv, sib).wait_recv()
    pose = jnp.sum(pose_in[...], axis=0)
    lane = iota((8, ALLP), 1)
    kept = jnp.where(lax.div(lane, PART) == d, pose, 0.0)
    choose = (lax.rem(iota((ALLP, 128), 0), PART) == iota((ALLP, 128), 1)).astype(F32)
    picked = jnp.dot(kept, choose, precision=lax.Precision.HIGHEST, preferred_element_type=F32)
    pose_out[...] = picked[0:1, :PART]

    def finish(n):
        @pl.when(active(n, g))
        def _():
            sent = sp_in.at[n, 0:G - 1]
            gz_copy(sent, sent, rs_send.at[n], rs_send.at[n], lax.rem(g + 1, G)).wait_send()

        each_slab(n, lambda copy: copy.wait_send())

    each(0, NU, finish)
    sent = w_all.at[0:D // 2]
    dom_copy(sent, sent, w_send, w_send, sib).wait_send()
    dom_copy(passed, passed, f_send, f_send, sib).wait_send()
    sent = pose_in.at[0:D - 1]
    dom_copy(sent, sent, p_send, p_send, sib).wait_send()
    sent = ids_in.at[0:D - 1]
    dom_copy(sent, sent, i_send, i_send, sib).wait_send()

    for j in reversed(range(BLOCKS)):
        bk_in[j, d] = bk[j, d]
        others = bk_in.at[j, 0:D - 1, 0:12]
        dom_copy(others, others, b_recv.at[j], b_recv.at[j], sib).wait_recv()
        total = jnp.sum(bk_in[j].astype(F32), axis=0)
        for k in range(3):
            back_out[k, :, BL * j:BL * (j + 1)] = total[4 * k:4 * k + 4]

    for j in range(BLOCKS):
        sent = bk_in.at[j, 0:D - 1, 0:12]
        dom_copy(sent, sent, b_send.at[j], b_send.at[j], sib).wait_send()


def local(volume, observed, ctf_table, ctf_class, bin_ids):
    vmem = pl.BlockSpec(memory_space=pltpu.VMEM)
    hbm = pl.BlockSpec(memory_space=pltpu.HBM)
    dma = pltpu.SemaphoreType.DMA
    pose, back = pl.pallas_call(
        body,
        out_shape=(jax.ShapeDtypeStruct((1, PART), F32), jax.ShapeDtypeStruct((3, R, X), F32)),
        in_specs=[hbm] * 4,
        out_specs=(vmem, vmem),
        scratch_shapes=[
            pltpu.VMEM((SLAB, R, X), F32),
            pltpu.VMEM((PART, R, U), BF16),
            pltpu.VMEM((NCTF, 2, U), F32),
            pltpu.SMEM((PART,), jnp.int32),
            pltpu.SMEM((NU,), jnp.int32),
            pltpu.SMEM((NU,), jnp.int32),
            dma((4,)),
            pltpu.VMEM((2 * R * SLAB, X), BF16),
            pltpu.VMEM((NB_DEV, X, 2 * U), BF16),
            pltpu.VMEM((NB_DEV, SLAB, U), F32),
            pltpu.VMEM((NB_DEV, SLAB, U), F32),
            pltpu.VMEM((2 * NB_DEV, 128), F32),
            pltpu.VMEM((NU, 16, BL), F32),
            pltpu.VMEM((NU, 16, BL), BF16),
            pltpu.VMEM((NU, G, 16, BL), BF16),
            pltpu.VMEM((BLOCKS, 64, BL), F32),
            pltpu.VMEM((NU, 16, BL), F32),
            pltpu.VMEM((NU, 16, BL), BF16),
            pltpu.VMEM((NU, G, 16, BL), BF16),
            pltpu.VMEM((16, BL), F32),
            pltpu.VMEM((D, PART, WC), BF16),
            pltpu.VMEM((EXT, 2 * U), BF16),
            pltpu.VMEM((EXT, 2 * U), BF16),
            pltpu.VMEM((R * SLAB, X), F32),
            pltpu.VMEM((BLOCKS, D, 16, BL), BF16),
            pltpu.VMEM((BLOCKS, D, 16, BL), BF16),
            pltpu.VMEM((1, ALLP), F32),
            pltpu.VMEM((D, 1, ALLP), F32),
        ] + [
            pltpu.VMEM((1, ALLP), F32),
            pltpu.VMEM((D, 1, ALLP), F32),
            dma, dma((D,)), dma, dma, dma, dma,
            dma((NU,)), dma((NU, G)), dma((NU, G)), dma((NU,)),
            dma((BLOCKS,)), dma((BLOCKS,)), dma, dma,
        ],
        compiler_params=pltpu.CompilerParams(
            collective_id=0, has_side_effects=True, vmem_limit_bytes=55200 << 10),
        name="tilt_refine",
    )(volume, observed, ctf_table, NCTF * bin_ids + ctf_class)
    return (pose.reshape(PART), back)


def solution(mesh):
    return jax.shard_map(
        local,
        mesh=mesh,
        in_specs=(
            P("gz", None, None),
            P(("gz", "dom"), None, None),
            P(),
            P(("gz", "dom")),
            P(("gz", "dom")),
        ),
        out_specs=(P(("gz", "dom")), P(("gz", "dom"), None, None)),
        check_vma=False,
    )
```

```python
import math

import jax
import jax.numpy as jnp
from jax import lax
from jax.experimental import pallas as pl
from jax.experimental.pallas import tpu as pltpu
from jax.sharding import PartitionSpec as P

NZ = 768
NB = 128
NB_DEV = 8
NCTF = 32
ITERS = 3
EPS = 1e-05
G = 16
D = 16
SLAB = 48
R = 4
X = 384
U = 384
PART = 16
ALLP = PART * D
WC = R * U
EXT = 128
BLOCKS = 3
BL = 128
PAIRS = 4
UNITS = [(k, j) for j in range(BLOCKS) for k in range(PAIRS)]
F32 = jnp.float32
BF16 = jnp.bfloat16
NU = len(UNITS)
NT = (((1,), (1,)), ((), ()))


def slab_spans():
    spans = []
    for k, j in UNITS:
        row = []
        for dom in range(D):
            sines = [math.sin(-0.5 * math.pi + math.pi * (2 * (dom + D * k) + i + 0.5) / NB)
                     for i in range(2)]
            centres = [0.5 * NZ + u * sine for sine in sines for u in (j * BL, j * BL + BL - 1)]
            first = math.floor(min(centres) - 1e-3)
            last = math.floor(max(centres) + 1e-3) + 1
            row.append((max(first, 0) // SLAB, min(last, NZ - 1) // SLAB))
        spans.append(row)
    return spans


def iota(shape, dim):
    return lax.broadcasted_iota(jnp.int32, shape, dim)


def gz_copy(src, dst, send, recv, to):
    return pltpu.make_async_remote_copy(
        src_ref=src, dst_ref=dst, send_sem=send, recv_sem=recv,
        device_id={"gz": to}, device_id_type=pl.DeviceIdType.MESH)


def dom_copy(src, dst, send, recv, to):
    return pltpu.make_async_remote_copy(
        src_ref=src, dst_ref=dst, send_sem=send, recv_sem=recv,
        device_id={"dom": to}, device_id_type=pl.DeviceIdType.MESH)


def each(first, last, act, unroll=1):
    def one(i, carry):
        act(i)
        return carry

    lax.fori_loop(first, last, one, 0, unroll=unroll)


def far_first(i, n):
    return n // 2 + lax.div(i, 2) * (2 * lax.rem(i, 2) - 1)


def body(vol_hbm, obs_hbm, ctf_hbm, mark_hbm, pose_out, back_out,
         vol, obs, ctf, mark, low, top, in_sem, vb, kt, kz, kzd, sc, sp, spb, sp_in, s_all, sf, ss, ss_in, rows_t,
         w_all, c2h, c2l, acc, bk, bk_in, pose_s, pose_in,
         ids, ids_in, w_send, w_recv, f_send, f_recv, i_send, i_recv,
         rs_send, rs_recv, rs2_send, rs2_recv, b_send, b_recv, p_send, p_recv):
    g = lax.axis_index("gz")
    d = lax.axis_index("dom")
    core = lax.rem(d, 2)
    zpos = lax.div(d, 2)
    sib = d + 1 - 2 * core

    def bin_of(slot):
        return 2 * d + 2 * D * lax.div(slot, 2) + lax.rem(slot, 2)


    barrier = pltpu.get_barrier_semaphore()
    each(1, D, lambda i: pl.semaphore_signal(
        barrier, inc=1, device_id={"dom": lax.rem(d + far_first(i, D), D)}, device_id_type=pl.DeviceIdType.MESH))
    each(1, G, lambda i: pl.semaphore_signal(
        barrier, inc=1, device_id={"gz": lax.rem(g + i, G)}, device_id_type=pl.DeviceIdType.MESH))

    for n, row in enumerate(slab_spans()):
        least, most = jnp.int32(row[0][0]), jnp.int32(row[0][1])
        for k in range(1, D):
            least = jnp.where(d == k, row[k][0], least)
            most = jnp.where(d == k, row[k][1], most)
        low[n] = least
        top[n] = most

    def active(n, slab):
        return (low[n] <= slab) & (slab <= top[n])

    fetches = [pltpu.make_async_copy(src, dst, in_sem.at[k]) for k, (src, dst) in enumerate(
        ((mark_hbm, mark), (obs_hbm, obs), (ctf_hbm, ctf), (vol_hbm, vol)))]
    for fetch in fetches:
        fetch.start()
    for fetch in fetches[:3]:
        fetch.wait()

    rows = iota((PART, NCTF), 0)
    along_row = iota((1, ALLP), 1) - PART * d
    cls_col = jnp.zeros((PART, NCTF), jnp.int32)
    id_row = jnp.zeros((1, ALLP), jnp.int32)
    for i in range(PART):
        cls_col = jnp.where(rows == i, lax.rem(mark[i], NCTF), cls_col)
        id_row = jnp.where(along_row == i, mark[i], id_row)
    cls_hot = (cls_col == iota((PART, NCTF), 1)).astype(F32)
    ids[...] = id_row.astype(F32)
    table = jnp.concatenate([ctf[:, 0, :], ctf[:, 1, :]], 1)
    contrast = jnp.dot(cls_hot, table, precision=lax.Precision.HIGHEST,
                       preferred_element_type=F32)
    for r in range(R):
        y = r % 2
        image = obs[:, r, :].astype(F32)
        w_all[d, :, r * U:(r + 1) * U] = (image * contrast[:, y * U:(y + 1) * U]).astype(BF16)

    pl.semaphore_wait(barrier, (G - 1) + (D - 1))

    def device_at(step, on):
        return lax.rem(zpos + step, D // 2) * 2 + on

    def step_of(i):
        return D // 4 + (1 + lax.div(i + 1, 2)) * (2 * lax.rem(i, 2) - 1)

    each(1, 5, lambda i: dom_copy(
        w_all.at[d], w_all.at[d], w_send, w_recv.at[d], device_at(step_of(i), core)).start())
    dom_copy(w_all.at[d], w_all.at[d], f_send, f_recv, sib).start()
    each(1, D, lambda i: dom_copy(ids, ids_in.at[d], i_send, i_recv, lax.rem(d + i, D)).start())

    square = table * table
    high = square.astype(BF16)
    c2h[...] = jnp.zeros_like(c2h)
    c2l[...] = jnp.zeros_like(c2l)
    c2h[:NCTF, :] = high
    c2l[:NCTF, :] = (square - high.astype(F32)).astype(BF16)

    fetches[3].wait()
    def split_planes(part):
        for r in range(R):
            plane_rows = vol[pl.ds(16 * part, 16), r, :]
            coarse = plane_rows.astype(BF16)
            at = pl.multiple_of(r * SLAB + 16 * part, 16)
            vb[pl.ds(at, 16), :] = coarse
            vb[pl.ds(R * SLAB + at, 16), :] = (plane_rows - coarse.astype(F32)).astype(BF16)

    each(0, SLAB // 16, split_planes)
    bin_index = bin_of(iota((NB_DEV, 128), 0)).astype(F32)
    theta = -0.5 * math.pi + math.pi * (bin_index + 0.5) / NB
    sc[:NB_DEV, :] = jnp.sin(theta)
    sc[NB_DEV:, :] = jnp.cos(theta)

    for j in reversed(range(BLOCKS)):
        wide = BL * (j + 1)
        radius = (BL * j + iota((1, BL), 1)).astype(F32)
        plane = (g * SLAB + iota((SLAB, BL), 0)).astype(F32)
        column = iota((wide, BL), 0).astype(F32)

        def extract(n, k, j=j, wide=wide, radius=radius, plane=plane, column=column):
            for i in range(2):
                b = 2 * k + i
                sine = sc[pl.ds(b, 1), :]
                cosine = sc[pl.ds(NB_DEV + b, 1), :]
                tx = column - radius * cosine
                fx = jnp.maximum(1.0 - tx * tx, 0.0)
                kx = jnp.concatenate([fx * fx, (tx * fx) * (radius * sine * (-4.0 / U))], 1)
                kx_high = kx.astype(BF16)
                kt[b, :wide, 2 * BL * j:2 * BL * (j + 1)] = kx_high
                kx_low = (kx - kx_high.astype(F32)).astype(BF16)
                tz = plane - (0.5 * NZ + radius * sine)
                fz = jnp.maximum(1.0 - tz * tz, 0.0)
                wz = fz * fz
                wd = (tz * fz) * (radius * cosine * (4.0 / U))
                kz[b, :, BL * j:BL * (j + 1)] = wz
                kzd[b, :, BL * j:BL * (j + 1)] = wd
                stacked = jnp.dot(vb[:, :wide], kx_high, preferred_element_type=F32)
                both = stacked[:R * SLAB] + stacked[R * SLAB:] + jnp.dot(
                    vb[:R * SLAB, :wide], kx_low, preferred_element_type=F32)
                for r in range(R):
                    direct = both[r * SLAB:(r + 1) * SLAB, :BL]
                    tilted = both[r * SLAB:(r + 1) * SLAB, BL:]
                    at = 2 * r + i
                    sp[n, at:at + 1, :] = jnp.sum(direct * wz, axis=0, keepdims=True)
                    sp[n, 8 + at:8 + at + 1, :] = jnp.sum(
                        direct * wd + tilted * wz, axis=0, keepdims=True)
            spb[n] = sp[n].astype(BF16)

        def unit(k, j=j, extract=extract):
            n = PAIRS * j + k

            @pl.when(active(n, g))
            def _():
                extract(n, k)
                each(1, G, lambda i: gz_copy(
                    spb.at[n], sp_in.at[n, g], rs_send.at[n], rs_recv.at[n, g], lax.rem(g + i, G)).start())
                sp_in[n, g] = spb[n]

        each(0, PAIRS, unit)

    def pass_on(step, relays=()):
        frm = device_at(step, core)
        block = w_all.at[frm]
        dom_copy(block, block, w_recv.at[frm], w_recv.at[frm], sib).wait_recv()
        for relay in relays:
            dom_copy(block, block, w_send, w_recv.at[frm], relay).start()
        dom_copy(block, block, f_send, f_recv, sib).start()

    pass_on(6, (device_at(2, core), device_at(1, core)))
    pass_on(2, (device_at(6, 1 - core), device_at(7, core)))
    each(3, 5, lambda i: pass_on(step_of(i)))
    pass_on(5)
    pass_on(3)

    def gather_slices(n):
        def gather(frm, total):
            @pl.when(frm != g)
            def _():
                gz_copy(spb.at[n], sp_in.at[n, frm], rs_recv.at[n, frm], rs_recv.at[n, frm],
                        lax.rem(g + 1, G)).wait_recv()
            return total + sp_in[n, frm].astype(F32)

        total = lax.fori_loop(low[n], top[n] + 1, gather, jnp.zeros((16, BL), F32))
        j = lax.div(n, PAIRS)
        k = lax.rem(n, PAIRS)
        for m in range(8):
            for i in range(2):
                s_all[j, pl.ds(8 * m + 2 * k + i, 1), :] = total[2 * m + i:2 * m + i + 1]

    each(0, NU, gather_slices)

    def rows_of(kind, r):
        at = 32 * kind + 8 * r
        rounded = jnp.concatenate([s_all[j, at:at + 8, :] for j in range(BLOCKS)], 1)
        return rounded.astype(BF16).astype(F32)

    lead = [rows_of(0, r) for r in range(R)]
    slope = [rows_of(1, r) for r in range(R)]
    curve = jnp.concatenate([slope[y] * slope[y] + slope[y + 2] * slope[y + 2] for y in range(2)], 1)
    cross = jnp.concatenate([lead[y] * slope[y] + lead[y + 2] * slope[y + 2] for y in range(2)], 1)
    quad = jnp.concatenate([curve, cross], 0)
    quad_high = quad.astype(BF16)
    quad_low = (quad - quad_high.astype(F32)).astype(BF16)
    first = lax.dot_general(jnp.concatenate([quad_high, quad_low], 0), c2h[...], NT,
                            preferred_element_type=F32)
    tables = first[:16] + first[16:] + lax.dot_general(quad_high, c2l[...], NT,
                                                       preferred_element_type=F32)
    tables_high = tables.astype(BF16)
    tables_low = (tables - tables_high.astype(F32)).astype(BF16)
    lookup = jnp.concatenate([tables_high, tables_low], 0)[:, :NCTF]
    slope_rows = jnp.concatenate(slope, 1).astype(BF16)

    ids_in[d] = ids[...]
    others = ids_in.at[0:D - 1]
    dom_copy(others, others, i_recv, i_recv, sib).wait_recv()
    id_row = jnp.sum(ids_in[...], axis=0).astype(jnp.int32)
    bin_row = lax.div(id_row, NCTF)
    cls_rows = (iota((NCTF, ALLP), 0) == lax.rem(id_row, NCTF)).astype(F32).astype(BF16)
    looked = jnp.dot(lookup, cls_rows, preferred_element_type=F32)
    held = looked[0:8] + looked[16:24]
    crossed = looked[8:16] + looked[24:32]
    mask = (bin_of(iota((8, ALLP), 0)) == bin_row).astype(F32)
    power = jnp.sum(mask * held, axis=0, keepdims=True)
    cross_row = jnp.sum(mask * crossed, axis=0, keepdims=True)
    curvature = power + EPS
    slot = iota((16, ALLP), 0)
    sloped_row = lax.rem(lax.div(slot, 2), 2) == 1
    mask_rows = (2 * d + 2 * D * lax.div(slot, 4) + lax.rem(slot, 2) == bin_row).astype(F32)

    for on in (core, 1 - core):
        frm = device_at(D // 4, on)
        block = w_all.at[frm]
        dom_copy(block, block, w_recv.at[frm], w_recv.at[frm], sib).wait_recv()
    passed = w_all.at[0:D // 2 - 1]
    dom_copy(passed, passed, f_recv, f_recv, sib).wait_recv()

    images = w_all[...].reshape(ALLP, WC)
    along = lax.dot_general(slope_rows, images, NT, preferred_element_type=F32)
    match = jnp.sum(mask * along, axis=0, keepdims=True) - cross_row
    shift = jnp.zeros_like(power)
    for _ in range(ITERS):
        shift = shift + 0.5 * (match - shift * power) / curvature
    pose_s[...] = shift * jnp.sqrt(curvature)
    spread = mask_rows * jnp.where(sloped_row, shift, 1.0)
    spread_high = spread.astype(BF16)
    spread_low = (spread - spread_high.astype(F32)).astype(BF16)
    sums = jnp.dot(jnp.concatenate([spread_high, spread_low], 0), images, preferred_element_type=F32)
    sums = sums[:16] + sums[16:]
    for n, (k, j) in enumerate(UNITS):
        for r in range(R):
            at = r * U + BL * j
            sf[n, 4 * r:4 * r + 4, :] = sums[4 * k:4 * k + 4, at:at + BL]
    ss[...] = sf[...].astype(BF16)

    def each_slab(n, act):
        def one(to):
            @pl.when(to != g)
            def _():
                act(gz_copy(ss.at[n], ss_in.at[n, g], rs2_send.at[n, to], rs2_recv.at[n], to))

        each(low[n], top[n] + 1, one)

    each(0, NU, lambda n: each_slab(NU - 1 - n, lambda copy: copy.start()))
    each(1, D, lambda i: dom_copy(pose_s, pose_in.at[d], p_send, p_recv, lax.rem(d + i, D)).start())

    acc[...] = jnp.zeros_like(acc)
    row = iota((256, R * SLAB), 0)
    within = lax.rem(row, 16)
    source = lax.rem(row, 4) * SLAB + 3 * lax.div(row, 16) + lax.div(within, 4)
    order = ((iota((256, R * SLAB), 1) == source) & (within < 12)).astype(F32).astype(BF16)

    for j in reversed(range(BLOCKS)):
        wide = BL * (j + 1)

        def spread_back(n, k, j=j, wide=wide):
            ss_in[n, g] = ss[n]
            others = ss_in.at[n, 0:G - 1]
            gz_copy(others, others, rs2_recv.at[n], rs2_recv.at[n], lax.rem(g + 1, G)).wait_recv()
            rows_t[...] = jnp.sum(ss_in[n].astype(F32), axis=0)
            for i in range(2):
                b = 2 * k + i
                wz = kz[b, :, BL * j:BL * (j + 1)]
                wd = kzd[b, :, BL * j:BL * (j + 1)]
                parts = []
                for r in range(R):
                    plain = rows_t[4 * r + i:4 * r + i + 1, :]
                    sloped = rows_t[4 * r + 2 + i:4 * r + 3 + i, :]
                    parts.append(jnp.concatenate([wz * plain + wd * sloped, wz * sloped], 1))
                left = jnp.concatenate(parts, 0)
                left_high = left.astype(BF16)
                left_low = (left - left_high.astype(F32)).astype(BF16)
                both = lax.dot_general(
                    jnp.concatenate([left_high, left_low], 0),
                    kt[b, :wide, 2 * BL * j:2 * BL * (j + 1)], NT, preferred_element_type=F32)
                acc[:, :wide] += both[:R * SLAB] + both[R * SLAB:]

        def unit(k, j=j, spread_back=spread_back):
            @pl.when(active(PAIRS * j + k, g))
            def _():
                spread_back(PAIRS * j + k, k)

        each(0, PAIRS, unit)

        ordered = jnp.dot(order, acc[:, BL * j:BL * (j + 1)].astype(BF16), preferred_element_type=F32)
        bk[j] = ordered.astype(BF16).reshape(D, 16, BL)
        def send_block(i, j=j):
            to = lax.rem(d + far_first(i, D), D)
            dom_copy(bk.at[j, to, 0:12], bk_in.at[j, d, 0:12], b_send.at[j], b_recv.at[j], to).start()

        each(1, D, send_block, 15)

    pose_in[d] = pose_s[...]
    others = pose_in.at[0:D - 1]
    dom_copy(others, others, p_recv, p_recv, sib).wait_recv()
    pose = jnp.sum(pose_in[...], axis=0)
    lane = iota((8, ALLP), 1)
    kept = jnp.where(lax.div(lane, PART) == d, pose, 0.0)
    choose = (lax.rem(iota((ALLP, 128), 0), PART) == iota((ALLP, 128), 1)).astype(F32)
    picked = jnp.dot(kept, choose, precision=lax.Precision.HIGHEST, preferred_element_type=F32)
    pose_out[...] = picked[0:1, :PART]

    def finish(n):
        @pl.when(active(n, g))
        def _():
            sent = sp_in.at[n, 0:G - 1]
            gz_copy(sent, sent, rs_send.at[n], rs_send.at[n], lax.rem(g + 1, G)).wait_send()

        each_slab(n, lambda copy: copy.wait_send())

    each(0, NU, finish)
    sent = w_all.at[0:D // 2]
    dom_copy(sent, sent, w_send, w_send, sib).wait_send()
    dom_copy(passed, passed, f_send, f_send, sib).wait_send()
    sent = pose_in.at[0:D - 1]
    dom_copy(sent, sent, p_send, p_send, sib).wait_send()
    sent = ids_in.at[0:D - 1]
    dom_copy(sent, sent, i_send, i_send, sib).wait_send()

    for j in reversed(range(BLOCKS)):
        bk_in[j, d] = bk[j, d]
        others = bk_in.at[j, 0:D - 1, 0:12]
        dom_copy(others, others, b_recv.at[j], b_recv.at[j], sib).wait_recv()
        total = jnp.sum(bk_in[j].astype(F32), axis=0)
        for k in range(3):
            back_out[k, :, BL * j:BL * (j + 1)] = total[4 * k:4 * k + 4]

    for j in range(BLOCKS):
        sent = bk_in.at[j, 0:D - 1, 0:12]
        dom_copy(sent, sent, b_send.at[j], b_send.at[j], sib).wait_send()


def local(volume, observed, ctf_table, ctf_class, bin_ids):
    vmem = pl.BlockSpec(memory_space=pltpu.VMEM)
    hbm = pl.BlockSpec(memory_space=pltpu.HBM)
    dma = pltpu.SemaphoreType.DMA
    pose, back = pl.pallas_call(
        body,
        out_shape=(jax.ShapeDtypeStruct((1, PART), F32), jax.ShapeDtypeStruct((3, R, X), F32)),
        in_specs=[hbm] * 4,
        out_specs=(vmem, vmem),
        scratch_shapes=[
            pltpu.VMEM((SLAB, R, X), F32),
            pltpu.VMEM((PART, R, U), BF16),
            pltpu.VMEM((NCTF, 2, U), F32),
            pltpu.SMEM((PART,), jnp.int32),
            pltpu.SMEM((NU,), jnp.int32),
            pltpu.SMEM((NU,), jnp.int32),
            dma((4,)),
            pltpu.VMEM((2 * R * SLAB, X), BF16),
            pltpu.VMEM((NB_DEV, X, 2 * U), BF16),
            pltpu.VMEM((NB_DEV, SLAB, U), F32),
            pltpu.VMEM((NB_DEV, SLAB, U), F32),
            pltpu.VMEM((2 * NB_DEV, 128), F32),
            pltpu.VMEM((NU, 16, BL), F32),
            pltpu.VMEM((NU, 16, BL), BF16),
            pltpu.VMEM((NU, G, 16, BL), BF16),
            pltpu.VMEM((BLOCKS, 64, BL), F32),
            pltpu.VMEM((NU, 16, BL), F32),
            pltpu.VMEM((NU, 16, BL), BF16),
            pltpu.VMEM((NU, G, 16, BL), BF16),
            pltpu.VMEM((16, BL), F32),
            pltpu.VMEM((D, PART, WC), BF16),
            pltpu.VMEM((EXT, 2 * U), BF16),
            pltpu.VMEM((EXT, 2 * U), BF16),
            pltpu.VMEM((R * SLAB, X), F32),
            pltpu.VMEM((BLOCKS, D, 16, BL), BF16),
            pltpu.VMEM((BLOCKS, D, 16, BL), BF16),
            pltpu.VMEM((1, ALLP), F32),
            pltpu.VMEM((D, 1, ALLP), F32),
        ] + [
            pltpu.VMEM((1, ALLP), F32),
            pltpu.VMEM((D, 1, ALLP), F32),
            dma, dma((D,)), dma, dma, dma, dma,
            dma((NU,)), dma((NU, G)), dma((NU, G)), dma((NU,)),
            dma((BLOCKS,)), dma((BLOCKS,)), dma, dma,
        ],
        compiler_params=pltpu.CompilerParams(
            collective_id=0, has_side_effects=True, vmem_limit_bytes=55200 << 10),
        name="tilt_refine",
    )(volume, observed, ctf_table, NCTF * bin_ids + ctf_class)
    return (pose.reshape(PART), back)


def solution(mesh):
    return jax.shard_map(
        local,
        mesh=mesh,
        in_specs=(
            P("gz", None, None),
            P(("gz", "dom"), None, None),
            P(),
            P(("gz", "dom")),
            P(("gz", "dom")),
        ),
        out_specs=(P(("gz", "dom")), P(("gz", "dom"), None, None)),
        check_vma=False,
    )
```

```python
import math

import jax
import jax.numpy as jnp
from jax import lax
from jax.experimental import pallas as pl
from jax.experimental.pallas import tpu as pltpu
from jax.sharding import PartitionSpec as P

NZ = 768
NB = 128
NB_DEV = 8
NCTF = 32
ITERS = 3
EPS = 1e-05
G = 16
D = 16
SLAB = 48
R = 4
X = 384
U = 384
PART = 16
ALLP = PART * D
WC = R * U
EXT = 128
BLOCKS = 3
BL = 128
PAIRS = 4
UNITS = [(k, j) for j in range(BLOCKS) for k in range(PAIRS)]
F32 = jnp.float32
BF16 = jnp.bfloat16
NU = len(UNITS)
NT = (((1,), (1,)), ((), ()))


def slab_spans():
    spans = []
    for k, j in UNITS:
        row = []
        for dom in range(D):
            sines = [math.sin(-0.5 * math.pi + math.pi * (2 * (dom + D * k) + i + 0.5) / NB)
                     for i in range(2)]
            centres = [0.5 * NZ + u * sine for sine in sines for u in (j * BL, j * BL + BL - 1)]
            first = math.floor(min(centres) - 1e-3)
            last = math.floor(max(centres) + 1e-3) + 1
            row.append((max(first, 0) // SLAB, min(last, NZ - 1) // SLAB))
        spans.append(row)
    return spans


def iota(shape, dim):
    return lax.broadcasted_iota(jnp.int32, shape, dim)


def gz_copy(src, dst, send, recv, to):
    return pltpu.make_async_remote_copy(
        src_ref=src, dst_ref=dst, send_sem=send, recv_sem=recv,
        device_id={"gz": to}, device_id_type=pl.DeviceIdType.MESH)


def dom_copy(src, dst, send, recv, to):
    return pltpu.make_async_remote_copy(
        src_ref=src, dst_ref=dst, send_sem=send, recv_sem=recv,
        device_id={"dom": to}, device_id_type=pl.DeviceIdType.MESH)


def each(first, last, act, unroll=1):
    def one(i, carry):
        act(i)
        return carry

    lax.fori_loop(first, last, one, 0, unroll=unroll)


def far_first(i, n):
    return n // 2 + lax.div(i, 2) * (2 * lax.rem(i, 2) - 1)


def body(vol_hbm, obs_hbm, ctf_hbm, mark_hbm, pose_out, back_out,
         vol, obs, ctf, mark, low, top, in_sem, vb, kt, kl, kz, kzd, sc, sp, spb, sp_in, s_all, sf, ss, ss_in, rows_t,
         w_all, c2h, c2l, acc, bk, bk_in, pose_s, pose_in,
         ids, ids_in, w_send, w_recv, f_send, f_recv, i_send, i_recv,
         rs_send, rs_recv, rs2_send, rs2_recv, b_send, b_recv, p_send, p_recv):
    g = lax.axis_index("gz")
    d = lax.axis_index("dom")
    core = lax.rem(d, 2)
    zpos = lax.div(d, 2)
    sib = d + 1 - 2 * core

    def bin_of(slot):
        return 2 * d + 2 * D * lax.div(slot, 2) + lax.rem(slot, 2)


    barrier = pltpu.get_barrier_semaphore()
    each(1, D, lambda i: pl.semaphore_signal(
        barrier, inc=1, device_id={"dom": lax.rem(d + far_first(i, D), D)}, device_id_type=pl.DeviceIdType.MESH))
    each(1, G, lambda i: pl.semaphore_signal(
        barrier, inc=1, device_id={"gz": lax.rem(g + i, G)}, device_id_type=pl.DeviceIdType.MESH))

    for n, row in enumerate(slab_spans()):
        least, most = jnp.int32(row[0][0]), jnp.int32(row[0][1])
        for k in range(1, D):
            least = jnp.where(d == k, row[k][0], least)
            most = jnp.where(d == k, row[k][1], most)
        low[n] = least
        top[n] = most

    def active(n, slab):
        return (low[n] <= slab) & (slab <= top[n])

    fetches = [pltpu.make_async_copy(src, dst, in_sem.at[k]) for k, (src, dst) in enumerate(
        ((mark_hbm, mark), (obs_hbm, obs), (ctf_hbm, ctf), (vol_hbm, vol)))]
    for fetch in fetches:
        fetch.start()
    for fetch in fetches[:3]:
        fetch.wait()

    rows = iota((PART, NCTF), 0)
    along_row = iota((1, ALLP), 1) - PART * d
    cls_col = jnp.zeros((PART, NCTF), jnp.int32)
    id_row = jnp.zeros((1, ALLP), jnp.int32)
    for i in range(PART):
        cls_col = jnp.where(rows == i, lax.rem(mark[i], NCTF), cls_col)
        id_row = jnp.where(along_row == i, mark[i], id_row)
    cls_hot = (cls_col == iota((PART, NCTF), 1)).astype(F32)
    ids[...] = id_row.astype(F32)
    table = jnp.concatenate([ctf[:, 0, :], ctf[:, 1, :]], 1)
    contrast = jnp.dot(cls_hot, table, precision=lax.Precision.HIGHEST,
                       preferred_element_type=F32)
    for r in range(R):
        y = r % 2
        image = obs[:, r, :].astype(F32)
        w_all[d, :, r * U:(r + 1) * U] = (image * contrast[:, y * U:(y + 1) * U]).astype(BF16)

    pl.semaphore_wait(barrier, (G - 1) + (D - 1))

    def device_at(step, on):
        return lax.rem(zpos + step, D // 2) * 2 + on

    def step_of(i):
        return D // 4 + (1 + lax.div(i + 1, 2)) * (2 * lax.rem(i, 2) - 1)

    each(1, 5, lambda i: dom_copy(
        w_all.at[d], w_all.at[d], w_send, w_recv.at[d], device_at(step_of(i), core)).start())
    dom_copy(w_all.at[d], w_all.at[d], f_send, f_recv, sib).start()
    each(1, D, lambda i: dom_copy(ids, ids_in.at[d], i_send, i_recv, lax.rem(d + i, D)).start())

    square = table * table
    high = square.astype(BF16)
    c2h[...] = jnp.zeros_like(c2h)
    c2l[...] = jnp.zeros_like(c2l)
    c2h[:NCTF, :] = high
    c2l[:NCTF, :] = (square - high.astype(F32)).astype(BF16)

    fetches[3].wait()
    def split_planes(part):
        for r in range(R):
            plane_rows = vol[pl.ds(16 * part, 16), r, :]
            coarse = plane_rows.astype(BF16)
            at = pl.multiple_of(r * SLAB + 16 * part, 16)
            vb[pl.ds(at, 16), :] = coarse
            vb[pl.ds(R * SLAB + at, 16), :] = (plane_rows - coarse.astype(F32)).astype(BF16)

    each(0, SLAB // 16, split_planes)
    bin_index = bin_of(iota((NB_DEV, 128), 0)).astype(F32)
    theta = -0.5 * math.pi + math.pi * (bin_index + 0.5) / NB
    sc[:NB_DEV, :] = jnp.sin(theta)
    sc[NB_DEV:, :] = jnp.cos(theta)

    for j in reversed(range(BLOCKS)):
        wide = BL * (j + 1)
        radius = (BL * j + iota((1, BL), 1)).astype(F32)
        plane = (g * SLAB + iota((SLAB, BL), 0)).astype(F32)
        column = iota((wide, BL), 0).astype(F32)

        def extract(n, k, j=j, wide=wide, radius=radius, plane=plane, column=column):
            for i in range(2):
                b = 2 * k + i
                sine = sc[pl.ds(b, 1), :]
                cosine = sc[pl.ds(NB_DEV + b, 1), :]
                tx = column - radius * cosine
                fx = jnp.maximum(1.0 - tx * tx, 0.0)
                kx = jnp.concatenate([fx * fx, (tx * fx) * (radius * sine * (-4.0 / U))], 1)
                kx_high = kx.astype(BF16)
                kt[b, :wide, 2 * BL * j:2 * BL * (j + 1)] = kx_high
                kx_low = (kx - kx_high.astype(F32)).astype(BF16)
                kl[b, :wide, 2 * BL * j:2 * BL * (j + 1)] = kx_low
                tz = plane - (0.5 * NZ + radius * sine)
                fz = jnp.maximum(1.0 - tz * tz, 0.0)
                wz = fz * fz
                wd = (tz * fz) * (radius * cosine * (4.0 / U))
                kz[b, :, BL * j:BL * (j + 1)] = wz
                kzd[b, :, BL * j:BL * (j + 1)] = wd
                stacked = jnp.dot(vb[:, :wide], kx_high, preferred_element_type=F32)
                both = stacked[:R * SLAB] + stacked[R * SLAB:] + jnp.dot(
                    vb[:R * SLAB, :wide], kx_low, preferred_element_type=F32)
                for r in range(R):
                    direct = both[r * SLAB:(r + 1) * SLAB, :BL]
                    tilted = both[r * SLAB:(r + 1) * SLAB, BL:]
                    at = 2 * r + i
                    sp[n, at:at + 1, :] = jnp.sum(direct * wz, axis=0, keepdims=True)
                    sp[n, 8 + at:8 + at + 1, :] = jnp.sum(
                        direct * wd + tilted * wz, axis=0, keepdims=True)
            spb[n] = sp[n].astype(BF16)

        def unit(k, j=j, extract=extract):
            n = PAIRS * j + k

            @pl.when(active(n, g))
            def _():
                extract(n, k)
                each(1, G, lambda i: gz_copy(
                    spb.at[n], sp_in.at[n, g], rs_send.at[n], rs_recv.at[n, g], lax.rem(g + i, G)).start())
                sp_in[n, g] = spb[n]

        each(0, PAIRS, unit)

    def pass_on(step, relays=()):
        frm = device_at(step, core)
        block = w_all.at[frm]
        dom_copy(block, block, w_recv.at[frm], w_recv.at[frm], sib).wait_recv()
        for relay in relays:
            dom_copy(block, block, w_send, w_recv.at[frm], relay).start()
        dom_copy(block, block, f_send, f_recv, sib).start()

    pass_on(6, (device_at(2, core), device_at(1, core)))
    pass_on(2, (device_at(6, 1 - core), device_at(7, core)))
    each(3, 5, lambda i: pass_on(step_of(i)))
    pass_on(5)
    pass_on(3)

    def gather_slices(n):
        def gather(frm, total):
            @pl.when(frm != g)
            def _():
                gz_copy(spb.at[n], sp_in.at[n, frm], rs_recv.at[n, frm], rs_recv.at[n, frm],
                        lax.rem(g + 1, G)).wait_recv()
            return total + sp_in[n, frm].astype(F32)

        total = lax.fori_loop(low[n], top[n] + 1, gather, jnp.zeros((16, BL), F32))
        j = lax.div(n, PAIRS)
        k = lax.rem(n, PAIRS)
        for m in range(8):
            for i in range(2):
                s_all[j, pl.ds(8 * m + 2 * k + i, 1), :] = total[2 * m + i:2 * m + i + 1]

    each(0, NU, gather_slices)

    def rows_of(kind, r):
        at = 32 * kind + 8 * r
        rounded = jnp.concatenate([s_all[j, at:at + 8, :] for j in range(BLOCKS)], 1)
        return rounded.astype(BF16).astype(F32)

    lead = [rows_of(0, r) for r in range(R)]
    slope = [rows_of(1, r) for r in range(R)]
    curve = jnp.concatenate([slope[y] * slope[y] + slope[y + 2] * slope[y + 2] for y in range(2)], 1)
    cross = jnp.concatenate([lead[y] * slope[y] + lead[y + 2] * slope[y + 2] for y in range(2)], 1)
    quad = jnp.concatenate([curve, cross], 0)
    quad_high = quad.astype(BF16)
    quad_low = (quad - quad_high.astype(F32)).astype(BF16)
    first = lax.dot_general(jnp.concatenate([quad_high, quad_low], 0), c2h[...], NT,
                            preferred_element_type=F32)
    tables = first[:16] + first[16:] + lax.dot_general(quad_high, c2l[...], NT,
                                                       preferred_element_type=F32)
    tables_high = tables.astype(BF16)
    tables_low = (tables - tables_high.astype(F32)).astype(BF16)
    lookup = jnp.concatenate([tables_high, tables_low], 0)[:, :NCTF]
    slope_rows = jnp.concatenate(slope, 1).astype(BF16)

    ids_in[d] = ids[...]
    others = ids_in.at[0:D - 1]
    dom_copy(others, others, i_recv, i_recv, sib).wait_recv()
    id_row = jnp.sum(ids_in[...], axis=0).astype(jnp.int32)
    bin_row = lax.div(id_row, NCTF)
    cls_rows = (iota((NCTF, ALLP), 0) == lax.rem(id_row, NCTF)).astype(F32).astype(BF16)
    looked = jnp.dot(lookup, cls_rows, preferred_element_type=F32)
    held = looked[0:8] + looked[16:24]
    crossed = looked[8:16] + looked[24:32]
    mask = (bin_of(iota((8, ALLP), 0)) == bin_row).astype(F32)
    power = jnp.sum(mask * held, axis=0, keepdims=True)
    cross_row = jnp.sum(mask * crossed, axis=0, keepdims=True)
    curvature = power + EPS
    slot = iota((16, ALLP), 0)
    sloped_row = lax.rem(lax.div(slot, 2), 2) == 1
    mask_rows = (2 * d + 2 * D * lax.div(slot, 4) + lax.rem(slot, 2) == bin_row).astype(F32)

    for on in (core, 1 - core):
        frm = device_at(D // 4, on)
        block = w_all.at[frm]
        dom_copy(block, block, w_recv.at[frm], w_recv.at[frm], sib).wait_recv()
    passed = w_all.at[0:D // 2 - 1]
    dom_copy(passed, passed, f_recv, f_recv, sib).wait_recv()

    images = w_all[...].reshape(ALLP, WC)
    along = lax.dot_general(slope_rows, images, NT, preferred_element_type=F32)
    match = jnp.sum(mask * along, axis=0, keepdims=True) - cross_row
    shift = jnp.zeros_like(power)
    for _ in range(ITERS):
        shift = shift + 0.5 * (match - shift * power) / curvature
    pose_s[...] = shift * jnp.sqrt(curvature)
    spread = mask_rows * jnp.where(sloped_row, shift, 1.0)
    spread_high = spread.astype(BF16)
    spread_low = (spread - spread_high.astype(F32)).astype(BF16)
    sums = jnp.dot(jnp.concatenate([spread_high, spread_low], 0), images, preferred_element_type=F32)
    sums = sums[:16] + sums[16:]
    for n, (k, j) in enumerate(UNITS):
        for r in range(R):
            at = r * U + BL * j
            sf[n, 4 * r:4 * r + 4, :] = sums[4 * k:4 * k + 4, at:at + BL]
    ss[...] = sf[...].astype(BF16)

    def each_slab(n, act):
        def one(to):
            @pl.when(to != g)
            def _():
                act(gz_copy(ss.at[n], ss_in.at[n, g], rs2_send.at[n, to], rs2_recv.at[n], to))

        each(low[n], top[n] + 1, one)

    each(0, NU, lambda n: each_slab(NU - 1 - n, lambda copy: copy.start()))
    each(1, D, lambda i: dom_copy(pose_s, pose_in.at[d], p_send, p_recv, lax.rem(d + i, D)).start())

    acc[...] = jnp.zeros_like(acc)
    row = iota((256, R * SLAB), 0)
    within = lax.rem(row, 16)
    source = lax.rem(row, 4) * SLAB + 3 * lax.div(row, 16) + lax.div(within, 4)
    order = ((iota((256, R * SLAB), 1) == source) & (within < 12)).astype(F32).astype(BF16)

    for j in reversed(range(BLOCKS)):
        wide = BL * (j + 1)

        def spread_back(n, k, j=j, wide=wide):
            ss_in[n, g] = ss[n]
            others = ss_in.at[n, 0:G - 1]
            gz_copy(others, others, rs2_recv.at[n], rs2_recv.at[n], lax.rem(g + 1, G)).wait_recv()
            rows_t[...] = jnp.sum(ss_in[n].astype(F32), axis=0)
            for i in range(2):
                b = 2 * k + i
                wz = kz[b, :, BL * j:BL * (j + 1)]
                wd = kzd[b, :, BL * j:BL * (j + 1)]
                parts = []
                for r in range(R):
                    plain = rows_t[4 * r + i:4 * r + i + 1, :]
                    sloped = rows_t[4 * r + 2 + i:4 * r + 3 + i, :]
                    parts.append(jnp.concatenate([wz * plain + wd * sloped, wz * sloped], 1))
                left = jnp.concatenate(parts, 0)
                left_high = left.astype(BF16)
                left_low = (left - left_high.astype(F32)).astype(BF16)
                both = lax.dot_general(
                    jnp.concatenate([left_high, left_low], 0),
                    kt[b, :wide, 2 * BL * j:2 * BL * (j + 1)], NT, preferred_element_type=F32)
                acc[:, :wide] += both[:R * SLAB] + both[R * SLAB:] + lax.dot_general(
                    left_high, kl[b, :wide, 2 * BL * j:2 * BL * (j + 1)], NT, preferred_element_type=F32)

        def unit(k, j=j, spread_back=spread_back):
            @pl.when(active(PAIRS * j + k, g))
            def _():
                spread_back(PAIRS * j + k, k)

        each(0, PAIRS, unit)

        ordered = jnp.dot(order, acc[:, BL * j:BL * (j + 1)].astype(BF16), preferred_element_type=F32)
        bk[j] = ordered.astype(BF16).reshape(D, 16, BL)
        def send_block(i, j=j):
            to = lax.rem(d + far_first(i, D), D)
            dom_copy(bk.at[j, to, 0:12], bk_in.at[j, d, 0:12], b_send.at[j], b_recv.at[j], to).start()

        each(1, D, send_block, 15)

    pose_in[d] = pose_s[...]
    others = pose_in.at[0:D - 1]
    dom_copy(others, others, p_recv, p_recv, sib).wait_recv()
    pose = jnp.sum(pose_in[...], axis=0)
    lane = iota((8, ALLP), 1)
    kept = jnp.where(lax.div(lane, PART) == d, pose, 0.0)
    choose = (lax.rem(iota((ALLP, 128), 0), PART) == iota((ALLP, 128), 1)).astype(F32)
    picked = jnp.dot(kept, choose, precision=lax.Precision.HIGHEST, preferred_element_type=F32)
    pose_out[...] = picked[0:1, :PART]

    def finish(n):
        @pl.when(active(n, g))
        def _():
            sent = sp_in.at[n, 0:G - 1]
            gz_copy(sent, sent, rs_send.at[n], rs_send.at[n], lax.rem(g + 1, G)).wait_send()

        each_slab(n, lambda copy: copy.wait_send())

    each(0, NU, finish)
    sent = w_all.at[0:D // 2]
    dom_copy(sent, sent, w_send, w_send, sib).wait_send()
    dom_copy(passed, passed, f_send, f_send, sib).wait_send()
    sent = pose_in.at[0:D - 1]
    dom_copy(sent, sent, p_send, p_send, sib).wait_send()
    sent = ids_in.at[0:D - 1]
    dom_copy(sent, sent, i_send, i_send, sib).wait_send()

    for j in reversed(range(BLOCKS)):
        bk_in[j, d] = bk[j, d]
        others = bk_in.at[j, 0:D - 1, 0:12]
        dom_copy(others, others, b_recv.at[j], b_recv.at[j], sib).wait_recv()
        total = jnp.sum(bk_in[j].astype(F32), axis=0)
        for k in range(3):
            back_out[k, :, BL * j:BL * (j + 1)] = total[4 * k:4 * k + 4]

    for j in range(BLOCKS):
        sent = bk_in.at[j, 0:D - 1, 0:12]
        dom_copy(sent, sent, b_send.at[j], b_send.at[j], sib).wait_send()


def local(volume, observed, ctf_table, ctf_class, bin_ids):
    vmem = pl.BlockSpec(memory_space=pltpu.VMEM)
    hbm = pl.BlockSpec(memory_space=pltpu.HBM)
    dma = pltpu.SemaphoreType.DMA
    pose, back = pl.pallas_call(
        body,
        out_shape=(jax.ShapeDtypeStruct((1, PART), F32), jax.ShapeDtypeStruct((3, R, X), F32)),
        in_specs=[hbm] * 4,
        out_specs=(vmem, vmem),
        scratch_shapes=[
            pltpu.VMEM((SLAB, R, X), F32),
            pltpu.VMEM((PART, R, U), BF16),
            pltpu.VMEM((NCTF, 2, U), F32),
            pltpu.SMEM((PART,), jnp.int32),
            pltpu.SMEM((NU,), jnp.int32),
            pltpu.SMEM((NU,), jnp.int32),
            dma((4,)),
            pltpu.VMEM((2 * R * SLAB, X), BF16),
            pltpu.VMEM((NB_DEV, X, 2 * U), BF16),
            pltpu.VMEM((NB_DEV, X, 2 * U), BF16),
            pltpu.VMEM((NB_DEV, SLAB, U), F32),
            pltpu.VMEM((NB_DEV, SLAB, U), F32),
            pltpu.VMEM((2 * NB_DEV, 128), F32),
            pltpu.VMEM((NU, 16, BL), F32),
            pltpu.VMEM((NU, 16, BL), BF16),
            pltpu.VMEM((NU, G, 16, BL), BF16),
            pltpu.VMEM((BLOCKS, 64, BL), F32),
            pltpu.VMEM((NU, 16, BL), F32),
            pltpu.VMEM((NU, 16, BL), BF16),
            pltpu.VMEM((NU, G, 16, BL), BF16),
            pltpu.VMEM((16, BL), F32),
            pltpu.VMEM((D, PART, WC), BF16),
            pltpu.VMEM((EXT, 2 * U), BF16),
            pltpu.VMEM((EXT, 2 * U), BF16),
            pltpu.VMEM((R * SLAB, X), F32),
            pltpu.VMEM((BLOCKS, D, 16, BL), BF16),
            pltpu.VMEM((BLOCKS, D, 16, BL), BF16),
            pltpu.VMEM((1, ALLP), F32),
            pltpu.VMEM((D, 1, ALLP), F32),
        ] + [
            pltpu.VMEM((1, ALLP), F32),
            pltpu.VMEM((D, 1, ALLP), F32),
            dma, dma((D,)), dma, dma, dma, dma,
            dma((NU,)), dma((NU, G)), dma((NU, G)), dma((NU,)),
            dma((BLOCKS,)), dma((BLOCKS,)), dma, dma,
        ],
        compiler_params=pltpu.CompilerParams(
            collective_id=0, has_side_effects=True, vmem_limit_bytes=55200 << 10),
        name="tilt_refine",
    )(volume, observed, ctf_table, NCTF * bin_ids + ctf_class)
    return (pose.reshape(PART), back)


def solution(mesh):
    return jax.shard_map(
        local,
        mesh=mesh,
        in_specs=(
            P("gz", None, None),
            P(("gz", "dom"), None, None),
            P(),
            P(("gz", "dom")),
            P(("gz", "dom")),
        ),
        out_specs=(P(("gz", "dom")), P(("gz", "dom"), None, None)),
        check_vma=False,
    )
```

```python
import math

import jax
import jax.numpy as jnp
from jax import lax
from jax.experimental import pallas as pl
from jax.experimental.pallas import tpu as pltpu
from jax.sharding import PartitionSpec as P

NZ = 768
NB = 128
NB_DEV = 8
NCTF = 32
ITERS = 3
EPS = 1e-05
G = 16
D = 16
SLAB = 48
R = 4
X = 384
U = 384
PART = 16
ALLP = PART * D
WC = R * U
EXT = 128
BLOCKS = 3
BL = 128
PAIRS = 4
UNITS = [(k, j) for j in range(BLOCKS) for k in range(PAIRS)]
F32 = jnp.float32
BF16 = jnp.bfloat16
NU = len(UNITS)
NT = (((1,), (1,)), ((), ()))


def slab_spans():
    spans = []
    for k, j in UNITS:
        row = []
        for dom in range(D):
            sines = [math.sin(-0.5 * math.pi + math.pi * (2 * (dom + D * k) + i + 0.5) / NB)
                     for i in range(2)]
            centres = [0.5 * NZ + u * sine for sine in sines for u in (j * BL, j * BL + BL - 1)]
            first = math.floor(min(centres) - 1e-3)
            last = math.floor(max(centres) + 1e-3) + 1
            row.append((max(first, 0) // SLAB, min(last, NZ - 1) // SLAB))
        spans.append(row)
    return spans


def iota(shape, dim):
    return lax.broadcasted_iota(jnp.int32, shape, dim)


def gz_copy(src, dst, send, recv, to):
    return pltpu.make_async_remote_copy(
        src_ref=src, dst_ref=dst, send_sem=send, recv_sem=recv,
        device_id={"gz": to}, device_id_type=pl.DeviceIdType.MESH)


def dom_copy(src, dst, send, recv, to):
    return pltpu.make_async_remote_copy(
        src_ref=src, dst_ref=dst, send_sem=send, recv_sem=recv,
        device_id={"dom": to}, device_id_type=pl.DeviceIdType.MESH)


def each(first, last, act, unroll=1):
    def one(i, carry):
        act(i)
        return carry

    lax.fori_loop(first, last, one, 0, unroll=unroll)


def far_first(i, n):
    return n // 2 + lax.div(i, 2) * (2 * lax.rem(i, 2) - 1)


def body(vol_hbm, obs_hbm, ctf_hbm, mark_hbm, pose_out, back_out,
         vol, obs, ctf, mark, low, top, in_sem, vb, kt, kl, kz, kzd, sc, sp, spb, sp_in, s_all, sf, ss, ss_in, rows_t,
         w_all, c2h, c2l, acc, bk, bk_in, pose_s, pose_in,
         ids, ids_in, w_send, w_recv, f_send, f_recv, i_send, i_recv,
         rs_send, rs_recv, rs2_send, rs2_recv, b_send, b_recv, p_send, p_recv):
    g = lax.axis_index("gz")
    d = lax.axis_index("dom")
    core = lax.rem(d, 2)
    zpos = lax.div(d, 2)
    sib = d + 1 - 2 * core

    def bin_of(slot):
        return 2 * d + 2 * D * lax.div(slot, 2) + lax.rem(slot, 2)


    barrier = pltpu.get_barrier_semaphore()
    each(1, D, lambda i: pl.semaphore_signal(
        barrier, inc=1, device_id={"dom": lax.rem(d + far_first(i, D), D)}, device_id_type=pl.DeviceIdType.MESH))
    each(1, G, lambda i: pl.semaphore_signal(
        barrier, inc=1, device_id={"gz": lax.rem(g + i, G)}, device_id_type=pl.DeviceIdType.MESH))

    for n, row in enumerate(slab_spans()):
        least, most = jnp.int32(row[0][0]), jnp.int32(row[0][1])
        for k in range(1, D):
            least = jnp.where(d == k, row[k][0], least)
            most = jnp.where(d == k, row[k][1], most)
        low[n] = least
        top[n] = most

    def active(n, slab):
        return (low[n] <= slab) & (slab <= top[n])

    fetches = [pltpu.make_async_copy(src, dst, in_sem.at[k]) for k, (src, dst) in enumerate(
        ((mark_hbm, mark), (obs_hbm, obs), (ctf_hbm, ctf), (vol_hbm, vol)))]
    for fetch in fetches:
        fetch.start()
    for fetch in fetches[:3]:
        fetch.wait()

    rows = iota((PART, NCTF), 0)
    along_row = iota((1, ALLP), 1) - PART * d
    cls_col = jnp.zeros((PART, NCTF), jnp.int32)
    id_row = jnp.zeros((1, ALLP), jnp.int32)
    for i in range(PART):
        cls_col = jnp.where(rows == i, lax.rem(mark[i], NCTF), cls_col)
        id_row = jnp.where(along_row == i, mark[i], id_row)
    cls_hot = (cls_col == iota((PART, NCTF), 1)).astype(F32)
    ids[...] = id_row.astype(F32)
    table = jnp.concatenate([ctf[:, 0, :], ctf[:, 1, :]], 1)
    contrast = jnp.dot(cls_hot, table, precision=lax.Precision.HIGHEST,
                       preferred_element_type=F32)
    for r in range(R):
        y = r % 2
        image = obs[:, r, :].astype(F32)
        w_all[d, :, r * U:(r + 1) * U] = (image * contrast[:, y * U:(y + 1) * U]).astype(BF16)

    pl.semaphore_wait(barrier, (G - 1) + (D - 1))

    def device_at(step, on):
        return lax.rem(zpos + step, D // 2) * 2 + on

    def step_of(i):
        return D // 4 + (1 + lax.div(i + 1, 2)) * (2 * lax.rem(i, 2) - 1)

    each(1, 5, lambda i: dom_copy(
        w_all.at[d], w_all.at[d], w_send, w_recv.at[d], device_at(step_of(i), core)).start())
    dom_copy(w_all.at[d], w_all.at[d], f_send, f_recv, sib).start()
    each(1, D, lambda i: dom_copy(ids, ids_in.at[d], i_send, i_recv, lax.rem(d + i, D)).start())

    square = table * table
    high = square.astype(BF16)
    c2h[...] = jnp.zeros_like(c2h)
    c2l[...] = jnp.zeros_like(c2l)
    c2h[:NCTF, :] = high
    c2l[:NCTF, :] = (square - high.astype(F32)).astype(BF16)

    fetches[3].wait()
    def split_planes(part):
        for r in range(R):
            plane_rows = vol[pl.ds(16 * part, 16), r, :]
            coarse = plane_rows.astype(BF16)
            at = pl.multiple_of(r * SLAB + 16 * part, 16)
            vb[pl.ds(at, 16), :] = coarse
            vb[pl.ds(R * SLAB + at, 16), :] = (plane_rows - coarse.astype(F32)).astype(BF16)

    each(0, SLAB // 16, split_planes)
    bin_index = bin_of(iota((NB_DEV, 128), 0)).astype(F32)
    theta = -0.5 * math.pi + math.pi * (bin_index + 0.5) / NB
    sc[:NB_DEV, :] = jnp.sin(theta)
    sc[NB_DEV:, :] = jnp.cos(theta)

    for j in reversed(range(BLOCKS)):
        wide = BL * (j + 1)
        radius = (BL * j + iota((1, BL), 1)).astype(F32)
        plane = (g * SLAB + iota((SLAB, BL), 0)).astype(F32)
        column = iota((wide, BL), 0).astype(F32)

        def extract(n, k, j=j, wide=wide, radius=radius, plane=plane, column=column):
            for i in range(2):
                b = 2 * k + i
                sine = sc[pl.ds(b, 1), :]
                cosine = sc[pl.ds(NB_DEV + b, 1), :]
                tx = column - radius * cosine
                fx = jnp.maximum(1.0 - tx * tx, 0.0)
                kx = jnp.concatenate([fx * fx, (tx * fx) * (radius * sine * (-4.0 / U))], 1)
                kx_high = kx.astype(BF16)
                kt[b, :wide, 2 * BL * j:2 * BL * (j + 1)] = kx_high
                kx_low = (kx - kx_high.astype(F32)).astype(BF16)
                kl[b, :wide, 2 * BL * j:2 * BL * (j + 1)] = kx_low
                tz = plane - (0.5 * NZ + radius * sine)
                fz = jnp.maximum(1.0 - tz * tz, 0.0)
                wz = fz * fz
                wd = (tz * fz) * (radius * cosine * (4.0 / U))
                kz[b, :, BL * j:BL * (j + 1)] = wz
                kzd[b, :, BL * j:BL * (j + 1)] = wd
                stacked = jnp.dot(vb[:, :wide], kx_high, preferred_element_type=F32)
                both = stacked[:R * SLAB] + stacked[R * SLAB:] + jnp.dot(
                    vb[:R * SLAB, :wide], kx_low, preferred_element_type=F32)
                for r in range(R):
                    direct = both[r * SLAB:(r + 1) * SLAB, :BL]
                    tilted = both[r * SLAB:(r + 1) * SLAB, BL:]
                    at = 2 * r + i
                    sp[n, at:at + 1, :] = jnp.sum(direct * wz, axis=0, keepdims=True)
                    sp[n, 8 + at:8 + at + 1, :] = jnp.sum(
                        direct * wd + tilted * wz, axis=0, keepdims=True)
            spb[n] = sp[n].astype(BF16)

        def unit(k, j=j, extract=extract):
            n = PAIRS * j + k

            @pl.when(active(n, g))
            def _():
                extract(n, k)
                each(1, G, lambda i: gz_copy(
                    spb.at[n], sp_in.at[n, g], rs_send.at[n], rs_recv.at[n, g], lax.rem(g + i, G)).start())
                sp_in[n, g] = spb[n]

        each(0, PAIRS, unit)

    def pass_on(step, relays=()):
        frm = device_at(step, core)
        block = w_all.at[frm]
        dom_copy(block, block, w_recv.at[frm], w_recv.at[frm], sib).wait_recv()
        for relay in relays:
            dom_copy(block, block, w_send, w_recv.at[frm], relay).start()
        dom_copy(block, block, f_send, f_recv, sib).start()

    pass_on(6, (device_at(2, core), device_at(1, core)))
    pass_on(2, (device_at(6, 1 - core), device_at(7, core)))
    each(3, 5, lambda i: pass_on(step_of(i)))
    def gather_slices(n):
        def gather(frm, total):
            @pl.when(frm != g)
            def _():
                gz_copy(spb.at[n], sp_in.at[n, frm], rs_recv.at[n, frm], rs_recv.at[n, frm],
                        lax.rem(g + 1, G)).wait_recv()
            return total + sp_in[n, frm].astype(F32)

        total = lax.fori_loop(low[n], top[n] + 1, gather, jnp.zeros((16, BL), F32))
        j = lax.div(n, PAIRS)
        k = lax.rem(n, PAIRS)
        for m in range(8):
            for i in range(2):
                s_all[j, pl.ds(8 * m + 2 * k + i, 1), :] = total[2 * m + i:2 * m + i + 1]

    each(0, NU, gather_slices)

    def rows_of(kind, r):
        at = 32 * kind + 8 * r
        rounded = jnp.concatenate([s_all[j, at:at + 8, :] for j in range(BLOCKS)], 1)
        return rounded.astype(BF16).astype(F32)

    lead = [rows_of(0, r) for r in range(R)]
    slope = [rows_of(1, r) for r in range(R)]
    curve = jnp.concatenate([slope[y] * slope[y] + slope[y + 2] * slope[y + 2] for y in range(2)], 1)
    cross = jnp.concatenate([lead[y] * slope[y] + lead[y + 2] * slope[y + 2] for y in range(2)], 1)
    quad = jnp.concatenate([curve, cross], 0)
    quad_high = quad.astype(BF16)
    quad_low = (quad - quad_high.astype(F32)).astype(BF16)
    first = lax.dot_general(jnp.concatenate([quad_high, quad_low], 0), c2h[...], NT,
                            preferred_element_type=F32)
    tables = first[:16] + first[16:] + lax.dot_general(quad_high, c2l[...], NT,
                                                       preferred_element_type=F32)
    tables_high = tables.astype(BF16)
    tables_low = (tables - tables_high.astype(F32)).astype(BF16)
    lookup = jnp.concatenate([tables_high, tables_low], 0)[:, :NCTF]
    slope_rows = jnp.concatenate(slope, 1).astype(BF16)

    ids_in[d] = ids[...]
    others = ids_in.at[0:D - 1]
    dom_copy(others, others, i_recv, i_recv, sib).wait_recv()
    id_row = jnp.sum(ids_in[...], axis=0).astype(jnp.int32)
    bin_row = lax.div(id_row, NCTF)
    cls_rows = (iota((NCTF, ALLP), 0) == lax.rem(id_row, NCTF)).astype(F32).astype(BF16)
    looked = jnp.dot(lookup, cls_rows, preferred_element_type=F32)
    held = looked[0:8] + looked[16:24]
    crossed = looked[8:16] + looked[24:32]
    mask = (bin_of(iota((8, ALLP), 0)) == bin_row).astype(F32)
    power = jnp.sum(mask * held, axis=0, keepdims=True)
    cross_row = jnp.sum(mask * crossed, axis=0, keepdims=True)
    curvature = power + EPS
    slot = iota((16, ALLP), 0)
    sloped_row = lax.rem(lax.div(slot, 2), 2) == 1
    mask_rows = (2 * d + 2 * D * lax.div(slot, 4) + lax.rem(slot, 2) == bin_row).astype(F32)

    pass_on(5)
    pass_on(3)
    for on in (core, 1 - core):
        frm = device_at(D // 4, on)
        block = w_all.at[frm]
        dom_copy(block, block, w_recv.at[frm], w_recv.at[frm], sib).wait_recv()
    passed = w_all.at[0:D // 2 - 1]
    dom_copy(passed, passed, f_recv, f_recv, sib).wait_recv()

    images = w_all[...].reshape(ALLP, WC)
    along = lax.dot_general(slope_rows, images, NT, preferred_element_type=F32)
    match = jnp.sum(mask * along, axis=0, keepdims=True) - cross_row
    shift = jnp.zeros_like(power)
    for _ in range(ITERS):
        shift = shift + 0.5 * (match - shift * power) / curvature
    pose_s[...] = shift * jnp.sqrt(curvature)
    spread = mask_rows * jnp.where(sloped_row, shift, 1.0)
    spread_high = spread.astype(BF16)
    spread_low = (spread - spread_high.astype(F32)).astype(BF16)
    sums = jnp.dot(jnp.concatenate([spread_high, spread_low], 0), images, preferred_element_type=F32)
    sums = sums[:16] + sums[16:]
    for n, (k, j) in enumerate(UNITS):
        for r in range(R):
            at = r * U + BL * j
            sf[n, 4 * r:4 * r + 4, :] = sums[4 * k:4 * k + 4, at:at + BL]
    ss[...] = sf[...].astype(BF16)

    def each_slab(n, act):
        def one(to):
            @pl.when(to != g)
            def _():
                act(gz_copy(ss.at[n], ss_in.at[n, g], rs2_send.at[n, to], rs2_recv.at[n], to))

        each(low[n], top[n] + 1, one)

    each(0, NU, lambda n: each_slab(NU - 1 - n, lambda copy: copy.start()))
    each(1, D, lambda i: dom_copy(pose_s, pose_in.at[d], p_send, p_recv, lax.rem(d + i, D)).start())

    acc[...] = jnp.zeros_like(acc)
    row = iota((256, R * SLAB), 0)
    within = lax.rem(row, 16)
    source = lax.rem(row, 4) * SLAB + 3 * lax.div(row, 16) + lax.div(within, 4)
    order = ((iota((256, R * SLAB), 1) == source) & (within < 12)).astype(F32).astype(BF16)

    for j in reversed(range(BLOCKS)):
        wide = BL * (j + 1)

        def spread_back(n, k, j=j, wide=wide):
            ss_in[n, g] = ss[n]
            others = ss_in.at[n, 0:G - 1]
            gz_copy(others, others, rs2_recv.at[n], rs2_recv.at[n], lax.rem(g + 1, G)).wait_recv()
            rows_t[...] = jnp.sum(ss_in[n].astype(F32), axis=0)
            for i in range(2):
                b = 2 * k + i
                wz = kz[b, :, BL * j:BL * (j + 1)]
                wd = kzd[b, :, BL * j:BL * (j + 1)]
                parts = []
                for r in range(R):
                    plain = rows_t[4 * r + i:4 * r + i + 1, :]
                    sloped = rows_t[4 * r + 2 + i:4 * r + 3 + i, :]
                    parts.append(jnp.concatenate([wz * plain + wd * sloped, wz * sloped], 1))
                left = jnp.concatenate(parts, 0)
                left_high = left.astype(BF16)
                left_low = (left - left_high.astype(F32)).astype(BF16)
                both = lax.dot_general(
                    jnp.concatenate([left_high, left_low], 0),
                    kt[b, :wide, 2 * BL * j:2 * BL * (j + 1)], NT, preferred_element_type=F32)
                acc[:, :wide] += both[:R * SLAB] + both[R * SLAB:] + lax.dot_general(
                    left_high, kl[b, :wide, 2 * BL * j:2 * BL * (j + 1)], NT, preferred_element_type=F32)

        def unit(k, j=j, spread_back=spread_back):
            @pl.when(active(PAIRS * j + k, g))
            def _():
                spread_back(PAIRS * j + k, k)

        each(0, PAIRS, unit)

        ordered = jnp.dot(order, acc[:, BL * j:BL * (j + 1)].astype(BF16), preferred_element_type=F32)
        bk[j] = ordered.astype(BF16).reshape(D, 16, BL)
        def send_block(i, j=j):
            to = lax.rem(d + far_first(i, D), D)
            dom_copy(bk.at[j, to, 0:12], bk_in.at[j, d, 0:12], b_send.at[j], b_recv.at[j], to).start()

        each(1, D, send_block, 15)

    pose_in[d] = pose_s[...]
    others = pose_in.at[0:D - 1]
    dom_copy(others, others, p_recv, p_recv, sib).wait_recv()
    pose = jnp.sum(pose_in[...], axis=0)
    lane = iota((8, ALLP), 1)
    kept = jnp.where(lax.div(lane, PART) == d, pose, 0.0)
    choose = (lax.rem(iota((ALLP, 128), 0), PART) == iota((ALLP, 128), 1)).astype(F32)
    picked = jnp.dot(kept, choose, precision=lax.Precision.HIGHEST, preferred_element_type=F32)
    pose_out[...] = picked[0:1, :PART]

    def finish(n):
        @pl.when(active(n, g))
        def _():
            sent = sp_in.at[n, 0:G - 1]
            gz_copy(sent, sent, rs_send.at[n], rs_send.at[n], lax.rem(g + 1, G)).wait_send()

        each_slab(n, lambda copy: copy.wait_send())

    each(0, NU, finish)
    sent = w_all.at[0:D // 2]
    dom_copy(sent, sent, w_send, w_send, sib).wait_send()
    dom_copy(passed, passed, f_send, f_send, sib).wait_send()
    sent = pose_in.at[0:D - 1]
    dom_copy(sent, sent, p_send, p_send, sib).wait_send()
    sent = ids_in.at[0:D - 1]
    dom_copy(sent, sent, i_send, i_send, sib).wait_send()

    for j in reversed(range(BLOCKS)):
        bk_in[j, d] = bk[j, d]
        others = bk_in.at[j, 0:D - 1, 0:12]
        dom_copy(others, others, b_recv.at[j], b_recv.at[j], sib).wait_recv()
        total = jnp.sum(bk_in[j].astype(F32), axis=0)
        for k in range(3):
            back_out[k, :, BL * j:BL * (j + 1)] = total[4 * k:4 * k + 4]

    for j in range(BLOCKS):
        sent = bk_in.at[j, 0:D - 1, 0:12]
        dom_copy(sent, sent, b_send.at[j], b_send.at[j], sib).wait_send()


def local(volume, observed, ctf_table, ctf_class, bin_ids):
    vmem = pl.BlockSpec(memory_space=pltpu.VMEM)
    hbm = pl.BlockSpec(memory_space=pltpu.HBM)
    dma = pltpu.SemaphoreType.DMA
    pose, back = pl.pallas_call(
        body,
        out_shape=(jax.ShapeDtypeStruct((1, PART), F32), jax.ShapeDtypeStruct((3, R, X), F32)),
        in_specs=[hbm] * 4,
        out_specs=(vmem, vmem),
        scratch_shapes=[
            pltpu.VMEM((SLAB, R, X), F32),
            pltpu.VMEM((PART, R, U), BF16),
            pltpu.VMEM((NCTF, 2, U), F32),
            pltpu.SMEM((PART,), jnp.int32),
            pltpu.SMEM((NU,), jnp.int32),
            pltpu.SMEM((NU,), jnp.int32),
            dma((4,)),
            pltpu.VMEM((2 * R * SLAB, X), BF16),
            pltpu.VMEM((NB_DEV, X, 2 * U), BF16),
            pltpu.VMEM((NB_DEV, X, 2 * U), BF16),
            pltpu.VMEM((NB_DEV, SLAB, U), F32),
            pltpu.VMEM((NB_DEV, SLAB, U), F32),
            pltpu.VMEM((2 * NB_DEV, 128), F32),
            pltpu.VMEM((NU, 16, BL), F32),
            pltpu.VMEM((NU, 16, BL), BF16),
            pltpu.VMEM((NU, G, 16, BL), BF16),
            pltpu.VMEM((BLOCKS, 64, BL), F32),
            pltpu.VMEM((NU, 16, BL), F32),
            pltpu.VMEM((NU, 16, BL), BF16),
            pltpu.VMEM((NU, G, 16, BL), BF16),
            pltpu.VMEM((16, BL), F32),
            pltpu.VMEM((D, PART, WC), BF16),
            pltpu.VMEM((EXT, 2 * U), BF16),
            pltpu.VMEM((EXT, 2 * U), BF16),
            pltpu.VMEM((R * SLAB, X), F32),
            pltpu.VMEM((BLOCKS, D, 16, BL), BF16),
            pltpu.VMEM((BLOCKS, D, 16, BL), BF16),
            pltpu.VMEM((1, ALLP), F32),
            pltpu.VMEM((D, 1, ALLP), F32),
        ] + [
            pltpu.VMEM((1, ALLP), F32),
            pltpu.VMEM((D, 1, ALLP), F32),
            dma, dma((D,)), dma, dma, dma, dma,
            dma((NU,)), dma((NU, G)), dma((NU, G)), dma((NU,)),
            dma((BLOCKS,)), dma((BLOCKS,)), dma, dma,
        ],
        compiler_params=pltpu.CompilerParams(
            collective_id=0, has_side_effects=True, vmem_limit_bytes=55200 << 10),
        name="tilt_refine",
    )(volume, observed, ctf_table, NCTF * bin_ids + ctf_class)
    return (pose.reshape(PART), back)


def solution(mesh):
    return jax.shard_map(
        local,
        mesh=mesh,
        in_specs=(
            P("gz", None, None),
            P(("gz", "dom"), None, None),
            P(),
            P(("gz", "dom")),
            P(("gz", "dom")),
        ),
        out_specs=(P(("gz", "dom")), P(("gz", "dom"), None, None)),
        check_vma=False,
    )
```
